32 devices in a mesh: ctx: 8 (over y, x, core), fsdp: 4 (over z).
Axes of the slice: x: 2, y: 2, z: 4, core: 2. Of those that a mesh axis runs over, the one named last changes fastest.
Arguments:
- tokens_in: bfloat16 [4, 1024, 1024], P('fsdp', 'ctx'), may hold values from -6 to 6
- doc_lengths: int32 [4, 8], P('fsdp'), may hold values from 1 to 512, 1024 in all within a row
- norm1_gain: bfloat16 [1024], P('fsdp'), may hold values from 0.5 to 1.5
- norm1_bias: bfloat16 [1024], P('fsdp'), may hold values from -1.5 to 1.5
- qkv_weight: bfloat16 [1024, 3072], P('fsdp'), may hold values from -0.1875 to 0.1875
- qv_bias: bfloat16 [2048], P('fsdp'), may hold values from -1.5 to 1.5
- out_weight: bfloat16 [1024, 1024], P('fsdp'), may hold values from -1.5 to 1.5
- out_bias: bfloat16 [1024], P('fsdp'), may hold values from -1.5 to 1.5
- norm2_gain: bfloat16 [1024], P('fsdp'), may hold values from 0.5 to 1.5
- norm2_bias: bfloat16 [1024], P('fsdp'), may hold values from -1.5 to 1.5
- up_weight: bfloat16 [1024, 4096], P('fsdp'), may hold values from -0.1875 to 0.1875
- up_bias: bfloat16 [4096], P('fsdp'), may hold values from -1.5 to 1.5
- down_weight: bfloat16 [4096, 1024], P('fsdp'), may hold values from -0.09375 to 0.09375
- down_bias: bfloat16 [1024], P('fsdp'), may hold values from -1.5 to 1.5
- out_cotangent: bfloat16 [4, 1024, 1024], P('fsdp', 'ctx'), may hold values from -6 to 6
Outputs:
- layer_out: bfloat16 [4, 1024, 1024], P('fsdp', 'ctx')
- input_grad: bfloat16 [4, 1024, 1024], P('fsdp', 'ctx')
- norm1_gain_grad: float32 [1024], P(('ctx', 'fsdp'))
- norm1_bias_grad: float32 [1024], P(('ctx', 'fsdp'))
- qkv_weight_grad: float32 [1024, 3072], P(('ctx', 'fsdp'))
- qv_bias_grad: float32 [2048], P(('ctx', 'fsdp'))
- out_weight_grad: float32 [1024, 1024], P(('ctx', 'fsdp'))
- out_bias_grad: float32 [1024], P(('ctx', 'fsdp'))
- norm2_gain_grad: float32 [1024], P(('ctx', 'fsdp'))
- norm2_bias_grad: float32 [1024], P(('ctx', 'fsdp'))
- up_weight_grad: float32 [1024, 4096], P(('ctx', 'fsdp'))
- up_bias_grad: float32 [4096], P(('ctx', 'fsdp'))
- down_weight_grad: float32 [4096, 1024], P(('ctx', 'fsdp'))
- down_bias_grad: float32 [1024], P(('ctx', 'fsdp'))
The draws below stay inside these ranges and needn't reach their ends.
Inputs may be any that keep to these rules, and one draw needn't show every extreme that they name: `doc_lengths`: each row lists one stream's documents in order; they sum to 1024; the longest is 512.
All inputs are finite; a program needn't handle non-finite values.
Results may differ from the reference program's by a relative error of at most 0.018.
Values may be sent and summed in bfloat16 or wider, within the bound.
A program may use at most 128 MiB of HBM per device.

```python
import math
import jax
import jax.numpy as jnp
import numpy as np
from jax import lax

D = 1024
HEADS = 16
HEAD_DIM = 64
FF = 4096
DOCS = 8
STREAMS = 4
SEQ = 1024
MOST = 512


def steps_of(own_key, dims, split, low, high):
    loudness, own = 1.0, jax.random.fold_in(own_key, 6)
    for dim, parts in split:
        heights = jnp.exp(jax.random.uniform(jax.random.fold_in(own, dim), (parts,), jnp.float32, low / len(split), high / len(split)))
        loudness = loudness * jnp.repeat(heights, dims[dim] // parts).reshape([-1 if axis == dim else 1 for axis in range(len(dims))])
    return loudness


def profile(amount, total, limit, slope):
    portions = [(1 << 20) // math.isqrt(rank ** slope) + 1 for rank in range(2, amount + 1)]
    surplus, given = total - limit - (amount - 1), [1] * (amount - 1)
    while surplus > 0:
        candidates = [i for i in range(amount - 1) if given[i] < limit]
        pool, left = sum([portions[i] for i in candidates]), surplus
        for i in candidates:
            extra = min(limit - given[i], max(1, left * portions[i] // pool), surplus)
            given[i] = given[i] + extra
            surplus = surplus - extra
    return np.array([limit] + given)


def uneven_parts(rng, count, total, reach, slope):
    if count == 2:
        one = jax.random.randint(rng, (), max(1, total - reach), min(reach, total - 1) + 1)
        return jnp.stack([one, total - one])
    lengths = jnp.asarray(profile(count, total, reach, slope), jnp.int32)
    couples = (count - 1) // 2
    donor, sink = lengths[1:1 + 2 * couples:2], lengths[2:2 + 2 * couples:2]
    slack = jnp.minimum(donor - 1, reach - sink)
    passed = jax.random.randint(jax.random.fold_in(rng, 1), (couples,), 0, 1 << 20) % (slack + 1)
    lengths = lengths.at[1:1 + 2 * couples:2].set(donor - passed).at[2:2 + 2 * couples:2].set(sink + passed)
    return lengths[jax.random.permutation(jax.random.fold_in(rng, 2), count)]


def centred(rng, dims, scale, bound, shards=(), kind=jnp.bfloat16):
    drawn = scale * jax.random.normal(rng, dims, jnp.float32)
    if shards:
        drawn = drawn * steps_of(rng, dims, shards, -0.22, 0.18)
    return jnp.clip(drawn, -bound, bound).astype(kind)


def setup_inputs(seed: int = 0) -> dict:
    streams_of = jax.random.split(jax.random.key(seed), 16)
    return {
        "tokens_in": centred(streams_of[0], (STREAMS, SEQ, D), 1.0, 6.0, ((0, 4), (1, 8))),
        "doc_lengths": jax.vmap(lambda own: uneven_parts(own, DOCS, SEQ, MOST, 2))(jax.random.split(streams_of[1], STREAMS)).reshape((STREAMS, DOCS)).astype(jnp.int32),
        "norm1_gain": jnp.clip(1.0 + 0.1 * jax.random.normal(streams_of[2], (D,), jnp.float32), 0.5, 1.5).astype(jnp.bfloat16),
        "norm1_bias": centred(streams_of[3], (D,), 0.3, 1.5, ((0, 4),)),
        "qkv_weight": centred(streams_of[4], (D, 3 * D), D ** -0.5, 0.1875, ((0, 4),)),
        "qv_bias": centred(streams_of[5], (2 * D,), 0.3, 1.5, ((0, 4),)),
        "out_weight": centred(streams_of[6], (D, D), (D // 64) ** -0.5, 1.5, ((0, 4),)),
        "out_bias": centred(streams_of[7], (D,), 0.3, 1.5, ((0, 4),)),
        "norm2_gain": jnp.clip(1.0 + 0.1 * jax.random.normal(streams_of[8], (D,), jnp.float32), 0.5, 1.5).astype(jnp.bfloat16),
        "norm2_bias": centred(streams_of[9], (D,), 0.3, 1.5, ((0, 4),)),
        "up_weight": centred(streams_of[10], (D, FF), D ** -0.5, 0.1875, ((0, 4),)),
        "up_bias": centred(streams_of[11], (FF,), 0.3, 1.5, ((0, 4),)),
        "down_weight": centred(streams_of[12], (FF, D), FF ** -0.5, 0.09375, ((0, 4),)),
        "down_bias": centred(streams_of[13], (D,), 0.3, 1.5, ((0, 4),)),
        "out_cotangent": centred(streams_of[14], (STREAMS, SEQ, D), 1.0, 6.0, ((0, 4), (1, 8))),
    }


@jax.custom_vjp
def low(v):
    return lax.optimization_barrier(v.astype(jnp.bfloat16)).astype(jnp.float32)

@jax.custom_vjp
def low_back(v):
    return v

def low_keep(v):
    return (low(v), None)

def low_pass(kept, grad):
    return (grad,)

def back_keep(v):
    return (v, None)

def back_low(kept, grad):
    return (low(grad),)
low.defvjp(low_keep, low_pass)
low_back.defvjp(back_keep, back_low)
epsilon = 1e-05
highest = lax.Precision.HIGHEST

def matmul(left, right):
    return jnp.dot(left, right, precision=highest, preferred_element_type=jnp.float32)

def norm_rows(values, gain, offset):
    centre = values - lax.optimization_barrier(jnp.mean(values, axis=-1, keepdims=True))
    spread = lax.optimization_barrier(jnp.mean(centre * centre, axis=-1, keepdims=True))
    return centre * lax.rsqrt(spread + epsilon) * gain + offset

def head_attention(query, keys, values, allowed):
    scores = low_back(matmul(query, keys.T) * HEAD_DIM ** (-0.5))
    scores = jnp.where(allowed, scores, -1e+30)
    probs = jax.nn.softmax(scores, axis=-1)
    return matmul(low(probs), values)

def stream_attention(qkv_stream, stream_doc):
    positions = jnp.arange(SEQ, dtype=jnp.int32)
    allowed = (positions[None, :] <= positions[:, None]) & (stream_doc[None, :] == stream_doc[:, None])
    queries = qkv_stream[:, :D].reshape(SEQ, HEADS, HEAD_DIM).transpose(1, 0, 2)
    keys = qkv_stream[:, D:2 * D].reshape(SEQ, HEADS, HEAD_DIM).transpose(1, 0, 2)
    values = qkv_stream[:, 2 * D:].reshape(SEQ, HEADS, HEAD_DIM).transpose(1, 0, 2)
    attend_head = jax.checkpoint(lambda trio: head_attention(trio[0], trio[1], trio[2], allowed))
    heads_out = lax.map(attend_head, (queries, keys, values))
    return heads_out.transpose(1, 0, 2).reshape(SEQ, D)

def reference(tokens_in, doc_lengths, norm1_gain, norm1_bias, qkv_weight, qv_bias, out_weight, out_bias, norm2_gain, norm2_bias, up_weight, up_bias, down_weight, down_bias, out_cotangent):
    doc_ends = jnp.cumsum(doc_lengths, axis=1).astype(jnp.int32)
    positions = jnp.arange(SEQ, dtype=jnp.int32)
    doc_ids = lax.optimization_barrier(jnp.sum((doc_ends[:, None, :] <= positions[None, :, None]).astype(jnp.int32), axis=2)).astype(jnp.int32)

    def forward(inputs, gain_one, shift_one, w_qkv, b_qv, w_out, b_out, gain_two, shift_two, w_up, b_up, w_down, b_down):
        flat = inputs.reshape(-1, D)
        normed1 = low(norm_rows(flat, gain_one, shift_one))
        bias_full = jnp.concatenate([b_qv[:D], jnp.zeros((D,), jnp.float32), b_qv[D:]])
        qkv = low(low_back(matmul(normed1, w_qkv) + bias_full))
        mixed = lax.map(lambda pair: stream_attention(pair[0], pair[1]), (qkv.reshape(STREAMS, SEQ, 3 * D), doc_ids))
        mix = low(low_back(mixed.reshape(-1, D)))
        resid = flat + low_back(matmul(mix, w_out) + b_out)
        normed2 = low(norm_rows(resid, gain_two, shift_two))
        pre = low_back(matmul(normed2, w_up) + b_up)
        hidden = low(jax.nn.gelu(pre, approximate=True))
        result = resid + low_back(matmul(hidden, w_down) + b_down)
        return result.reshape(STREAMS, SEQ, D)
    members = tuple((member.astype(jnp.float32) for member in (tokens_in, norm1_gain, norm1_bias, qkv_weight, qv_bias, out_weight, out_bias, norm2_gain, norm2_bias, up_weight, up_bias, down_weight, down_bias)))
    result, pullback = jax.vjp(forward, *members)
    grads = pullback(out_cotangent.astype(jnp.float32))
    return (result.astype(jnp.bfloat16), grads[0].astype(jnp.bfloat16), grads[1], grads[2], grads[3], grads[4], grads[5], grads[6], grads[7], grads[8], grads[9], grads[10], grads[11], grads[12])
```

```python
import jax
import jax.numpy as jnp
from jax import lax
from jax.sharding import PartitionSpec as P

HEADS = 16
HEAD_DIM = 64

epsilon = 1e-05
masked_score = -1e30
f32 = jnp.float32
bf16 = jnp.bfloat16


def row_stats(values):
    mean = jnp.mean(values, axis=-1, keepdims=True)
    centre = values - mean
    spread = jnp.mean(centre * centre, axis=-1, keepdims=True)
    scale = lax.rsqrt(spread + epsilon)
    return centre * scale, scale


def norm_back(grad, xhat, scale, gain):
    gh = grad * gain
    return scale * (
        gh
        - jnp.mean(gh, axis=-1, keepdims=True)
        - xhat * jnp.mean(gh * xhat, axis=-1, keepdims=True)
    )


def gelu_both(v):
    k = 0.7978845608028654
    inner = jnp.tanh(k * (v + 0.044715 * v * v * v))
    value = 0.5 * v * (1.0 + inner)
    slope = 0.5 * (1.0 + inner) + 0.5 * v * (1.0 - inner * inner) * k * (
        1.0 + 3 * 0.044715 * v * v
    )
    return value, slope


def mm(a, b, dims):
    return lax.dot_general(a, b, (dims, ((), ())), preferred_element_type=f32)


NN = ((1,), (0,))
NT = ((1,), (1,))
TN = ((0,), (0,))


def columns(weight, start, width):
    return lax.dynamic_slice_in_dim(weight, start, width, axis=1)


def shards(
    tokens_in,
    doc_lengths,
    norm1_gain,
    norm1_bias,
    qkv_weight,
    qv_bias,
    out_weight,
    out_bias,
    norm2_gain,
    norm2_bias,
    up_weight,
    up_bias,
    down_weight,
    down_bias,
    out_cotangent,
):
    C = lax.axis_size("ctx")
    Z = lax.axis_size("fsdp")
    c = lax.axis_index("ctx")
    rows, width = tokens_in.shape[1:]
    seq = rows * C
    heads = HEADS // C
    hw = heads * HEAD_DIM
    ff = up_weight.shape[1]
    fw = ff // C
    score_scale = HEAD_DIM ** (-0.5)

    def along_z(x):
        return lax.all_gather(x, "fsdp", axis=0, tiled=True)

    def along_ctx(x):
        return lax.all_gather(x, "ctx", axis=0, tiled=True)

    def scatter_ctx(x):
        return lax.psum_scatter(x.astype(bf16), "ctx", scatter_dimension=0, tiled=True).astype(f32)

    vectors = jnp.concatenate(
        [norm1_gain, norm1_bias, qv_bias, out_bias, norm2_gain, norm2_bias, up_bias, down_bias]
    )
    vectors = lax.all_gather(vectors, "fsdp", axis=0)
    sizes = [
        v.shape[0]
        for v in (norm1_gain, norm1_bias, qv_bias, out_bias, norm2_gain, norm2_bias, up_bias, down_bias)
    ]
    pieces, at = [], 0
    for size in sizes:
        pieces.append(vectors[:, at : at + size].reshape(-1).astype(f32))
        at += size
    gain_one, shift_one, b_qv, b_out, gain_two, shift_two, b_up, b_down = pieces

    w_qkv_part = jnp.concatenate(
        [columns(qkv_weight, part * width + c * hw, hw) for part in range(3)], axis=1
    )
    w_qkv = along_z(w_qkv_part)
    out_rows = width // C
    w_out_full = along_z(out_weight)
    w_out = lax.dynamic_slice_in_dim(w_out_full, c * out_rows, out_rows, axis=0)
    w_up = along_z(columns(up_weight, c * fw, fw))
    w_down_full = along_z(down_weight)
    w_down = lax.dynamic_slice_in_dim(w_down_full, c * fw, fw, axis=0)

    x = tokens_in[0].astype(f32)
    xhat1, scale1 = row_stats(x)
    n1 = along_ctx((xhat1 * gain_one + shift_one).astype(bf16))
    bias_q = lax.dynamic_slice_in_dim(b_qv, c * hw, hw)
    bias_v = lax.dynamic_slice_in_dim(b_qv, width + c * hw, hw)
    qkv = mm(n1, w_qkv, NN) + jnp.concatenate([bias_q, jnp.zeros((hw,), f32), bias_v])
    qkv = qkv.astype(bf16)

    ends = jnp.cumsum(doc_lengths[0])
    pos = jnp.arange(seq, dtype=jnp.int32)
    doc = jnp.sum((ends[None, :] <= pos[:, None]).astype(jnp.int32), axis=1)
    allowed = (pos[None, :] <= pos[:, None]) & (doc[None, :] == doc[:, None])

    def head(part, h):
        at = part * hw + h * HEAD_DIM
        return qkv[:, at : at + HEAD_DIM]

    mixes, lses = [], []
    for h in range(heads):
        s = mm(head(0, h), head(1, h), NT) * score_scale
        s = jnp.where(allowed, s, masked_score)
        top = jnp.max(s, axis=1, keepdims=True)
        e = jnp.exp(s - top)
        total = jnp.sum(e, axis=1, keepdims=True)
        mixes.append((mm(e.astype(bf16), head(2, h), NN) / total).astype(bf16))
        lses.append(top + jnp.log(total))
    mix = jnp.concatenate(mixes, axis=1)

    resid = x + scatter_ctx(mm(mix, w_out, NN)) + b_out
    xhat2, scale2 = row_stats(resid)
    n2 = along_ctx((xhat2 * gain_two + shift_two).astype(bf16))
    pre = mm(n2, w_up, NN) + lax.dynamic_slice_in_dim(b_up, c * fw, fw)
    value, slope = gelu_both(pre)
    hidden = value.astype(bf16)
    layer_out = (resid + scatter_ctx(mm(hidden, w_down, NN)) + b_down).astype(bf16)[None]

    cot = along_ctx(out_cotangent[0])
    hidden_grad = mm(cot, w_down, NT)
    pre_grad = (hidden_grad * slope).astype(bf16)
    down_w_grad = mm(hidden, cot, TN)
    up_w_grad = mm(n2, pre_grad, TN)
    up_b_grad = jnp.sum(pre_grad.astype(f32), axis=0)
    n2_grad = scatter_ctx(mm(pre_grad, w_up, NT))
    cot_own = out_cotangent[0].astype(f32)
    resid_grad = cot_own + norm_back(n2_grad, xhat2, scale2, gain_two)
    branch_own = resid_grad.astype(bf16)
    branch = along_ctx(branch_own)
    out_w_grad = mm(mix, branch, TN)
    mix_grad = mm(branch, w_out, NT).astype(bf16)

    grads = [[], [], []]
    for h in range(heads):
        at = h * HEAD_DIM
        q, k, v = (head(part, h) for part in range(3))
        g = mix_grad[:, at : at + HEAD_DIM]
        p = jnp.where(allowed, jnp.exp(mm(q, k, NT) * score_scale - lses[h]), 0.0)
        delta = jnp.sum(g.astype(f32) * mixes[h].astype(f32), axis=1, keepdims=True)
        ds = (p * (mm(g, v, NT) - delta)).astype(bf16)
        grads[0].append(score_scale * mm(ds, k, NN))
        grads[1].append(score_scale * mm(ds, q, TN))
        grads[2].append(mm(p.astype(bf16), g, TN))
    qkv_grad = jnp.concatenate(grads[0] + grads[1] + grads[2], axis=1).astype(bf16)

    qkv_w_grad = mm(n1, qkv_grad, TN)
    qkv_sums = jnp.sum(qkv_grad.astype(f32), axis=0)
    n1_grad = scatter_ctx(mm(qkv_grad, w_qkv, NT))
    input_grad = (resid_grad + norm_back(n1_grad, xhat1, scale1, gain_one)).astype(bf16)[None]

    def rows_home(grad):
        return lax.psum_scatter(grad.astype(bf16), "fsdp", scatter_dimension=0, tiled=True).astype(f32)

    def columns_home(grad):
        r = grad.shape[0] // (C * Z)
        grad = grad.astype(bf16).reshape(C, Z, r, grad.shape[1])
        mine = lax.psum_scatter(grad, "fsdp", scatter_dimension=1, tiled=True)[:, 0]
        return lax.all_to_all(mine, "ctx", 0, 0, tiled=False).astype(f32)

    d_down = rows_home(down_w_grad)
    d_out = rows_home(out_w_grad)
    up_parts = columns_home(up_w_grad)
    d_up = up_parts.transpose(1, 0, 2).reshape(-1, ff)
    qkv_parts = columns_home(qkv_w_grad)
    r = qkv_parts.shape[1]
    d_qkv = qkv_parts.reshape(C, r, 3, hw).transpose(1, 2, 0, 3).reshape(r, 3 * width)

    def spread(v, size):
        return lax.dynamic_update_slice(jnp.zeros((size,), f32), v, (c * v.shape[0],))

    parts = [
        jnp.sum(n1_grad * xhat1, axis=0),
        jnp.sum(n1_grad, axis=0),
        jnp.concatenate([spread(qkv_sums[:hw], width), spread(qkv_sums[2 * hw :], width)]),
        jnp.sum(branch_own.astype(f32), axis=0),
        jnp.sum(n2_grad * xhat2, axis=0),
        jnp.sum(n2_grad, axis=0),
        spread(up_b_grad, ff),
        jnp.sum(cot_own, axis=0),
    ]
    packed = jnp.concatenate([p.reshape(C * Z, -1) for p in parts], axis=1)
    packed = lax.psum_scatter(packed, ("ctx", "fsdp"), scatter_dimension=0, tiled=True)[0]
    small, at = [], 0
    for p in parts:
        n = p.shape[0] // (C * Z)
        small.append(packed[at : at + n])
        at += n
    return (
        layer_out,
        input_grad,
        small[0],
        small[1],
        d_qkv,
        small[2],
        d_out,
        small[3],
        small[4],
        small[5],
        d_up,
        small[6],
        d_down,
        small[7],
    )


def solution(mesh):
    token = P("fsdp", "ctx", None)
    flat, table = P("fsdp"), P("fsdp", None)
    home, home2 = P(("ctx", "fsdp")), P(("ctx", "fsdp"), None)
    return jax.shard_map(
        shards,
        mesh=mesh,
        in_specs=(
            token, table, flat, flat, table, flat, table, flat,
            flat, flat, table, flat, table, flat, token,
        ),
        out_specs=(
            token, token, home, home, home2, home, home2, home,
            home, home, home2, home, home2, home,
        ),
        check_vma=False,
    )
```

```python
import functools
import jax
import jax.numpy as jnp
from jax import lax
from jax.experimental import pallas as pl
from jax.experimental.pallas import tpu as pltpu
from jax.sharding import PartitionSpec as P

HEADS = 16
HEAD_DIM = 64
MESH = pl.DeviceIdType.MESH

epsilon = 1e-05
masked_score = -1e30
score_scale = HEAD_DIM ** (-0.5)
f32 = jnp.float32
bf16 = jnp.bfloat16


def row_stats(values):
    mean = jnp.mean(values, axis=-1, keepdims=True)
    centre = values - mean
    spread = jnp.mean(centre * centre, axis=-1, keepdims=True)
    scale = lax.rsqrt(spread + epsilon)
    return centre * scale, scale


def norm_back(grad, xhat, scale, gain):
    gh = grad * gain
    return scale * (
        gh
        - jnp.mean(gh, axis=-1, keepdims=True)
        - xhat * jnp.mean(gh * xhat, axis=-1, keepdims=True)
    )


def gelu_both(v):
    k = 0.7978845608028654
    inner = jnp.tanh(k * (v + 0.044715 * v * v * v))
    value = 0.5 * v * (1.0 + inner)
    slope = 0.5 * (1.0 + inner) + 0.5 * v * (1.0 - inner * inner) * k * (
        1.0 + 3 * 0.044715 * v * v
    )
    return value, slope


def mm(a, b, dims):
    return lax.dot_general(a, b, (dims, ((), ())), preferred_element_type=f32)


NN = ((1,), (0,))
NT = ((1,), (1,))
TN = ((0,), (0,))


class Net:
    def __init__(self, chips, Z):
        self.chips, self.Z = chips, Z
        self.c = lax.axis_index("ctx")
        self.z = lax.axis_index("fsdp")

    def barrier(self):
        sem = pltpu.get_barrier_semaphore()
        peers = [(self.c ^ d, self.z) for d in range(1, 2 * self.chips)]
        peers += [(self.c, self.z ^ d) for d in range(1, self.Z)]
        for peer in peers:
            pl.semaphore_signal(sem, inc=1, device_id=peer, device_id_type=MESH)
        pl.semaphore_wait(sem, len(peers))

    def to_ctx(self, d, src, dst, sems, i):
        return pltpu.make_async_remote_copy(
            src, dst, sems.at[0, i], sems.at[1, i],
            device_id=(self.c ^ d, self.z), device_id_type=MESH,
        )

    def to_z(self, d, src, dst, sems, i):
        return pltpu.make_async_remote_copy(
            src, dst, sems.at[0, i], sems.at[1, i],
            device_id=(self.c, self.z ^ d), device_id_type=MESH,
        )


class ZExchange:
    def __init__(self, net, src, dst, sems, local):
        self.copies = [
            net.to_z(d, src, dst.at[net.z], sems, d) for d in range(net.Z - 1, 0, -1)
        ]
        self.own = pltpu.make_async_copy(src, dst.at[net.z], local)

    def start(self):
        for copy in self.copies:
            copy.start()
        self.own.start()

    def wait(self):
        self.own.wait()
        for copy in self.copies:
            copy.wait_recv()

    def finish(self):
        for copy in self.copies:
            copy.wait_send()


class Gather:
    def __init__(self, net, src, dst, sems):
        self.net, self.src, self.dst, self.sems = net, src, dst, sems
        self.sent = []

    def copy(self, d, src, dst, i):
        copy = self.net.to_ctx(d, src, dst, self.sems, i)
        copy.start()
        self.sent.append(copy)
        return copy

    def block(self, d, rows=None):
        index = self.net.c ^ d
        return self.dst.at[index] if rows is None else self.dst.at[index, rows]

    def begin(self):
        c = self.net.c
        if self.net.chips == 4:
            half = self.src.shape[0] // 2
            self.lo, self.hi = pl.ds(0, half), pl.ds(half, half)
            lo, hi, src, own = self.lo, self.hi, self.src, self.dst.at[c]
            self.x_lo = self.copy(2, src.at[lo], self.dst.at[c, lo], 0)
            self.y_hi = self.copy(4, src.at[hi], self.dst.at[c, hi], 1)
            self.x_hi = self.copy(2, src.at[hi], self.dst.at[c, hi], 2)
            self.y_lo = self.copy(4, src.at[lo], self.dst.at[c, lo], 3)
            self.beside = self.copy(1, src, own, 4)
        else:
            self.far = {
                d: self.copy(2 * d, self.src, self.dst.at[c], 2 * d)
                for d in range(self.net.chips - 1, 0, -1)
            }
            self.beside = self.copy(1, self.src, self.dst.at[c], 1)

    def relay(self, d, rows, target, i):
        part = self.block(d, rows)
        return self.copy(target, part, part, i)

    def middle(self):
        if self.net.chips == 4:
            self.x_lo.wait_recv()
            self.r_lo = self.relay(2, self.lo, 4, 5)
            self.s0 = self.relay(2, self.lo, 1, 6)
            self.y_hi.wait_recv()
            self.r_hi = self.relay(4, self.hi, 2, 7)
            self.s1 = self.relay(4, self.hi, 1, 8)

    def finish(self, ready=None):
        ready = ready or (lambda d: None)
        self.beside.wait_recv()
        ready(1)
        if self.net.chips == 4:
            self.x_hi.wait_recv()
            s2 = self.relay(2, self.hi, 1, 9)
            ready(2)
            self.y_lo.wait_recv()
            s3 = self.relay(4, self.lo, 1, 10)
            ready(4)
            self.r_lo.wait_recv()
            s4 = self.relay(6, self.lo, 1, 11)
            self.r_hi.wait_recv()
            s5 = self.relay(6, self.hi, 1, 12)
            ready(6)
            self.s0.wait_recv()
            s2.wait_recv()
            ready(3)
            self.s1.wait_recv()
            s3.wait_recv()
            ready(5)
            s4.wait_recv()
            s5.wait_recv()
            ready(7)
        else:
            on = {}
            for d, copy in self.far.items():
                copy.wait_recv()
                on[d] = self.relay(2 * d, None, 1, 2 * d + 1)
                ready(2 * d)
            for d, copy in on.items():
                copy.wait_recv()
                ready(2 * d + 1)
        for copy in self.sent:
            copy.wait_send()


class Reduce:
    def __init__(self, net, rows, width, sems, sib_send, sib_recv, far_send, far_recv, keep):
        self.net, self.sems = net, sems
        self.sib_send, self.sib_recv = sib_send, sib_recv
        self.far_send, self.far_recv, self.keep = far_send, far_recv, keep

    def run(self, partial):
        net = self.net
        c, chips = net.c, net.chips
        order = list(range(chips - 1, -1, -1))
        sib, far = {}, {}

        def pass_on(d):
            sib[d].wait_recv()
            total = self.keep[d] + self.sib_recv[d].astype(f32)
            self.far_send[d] = total.astype(bf16)
            far[d] = net.to_ctx(2 * d, self.far_send.at[d], self.far_recv.at[d], self.sems, chips + d)
            far[d].start()

        last = None
        for d in order:
            self.sib_send[d] = partial((c ^ (2 * d)) ^ 1).astype(bf16)
            sib[d] = net.to_ctx(1, self.sib_send.at[d], self.sib_recv.at[d], self.sems, d)
            sib[d].start()
            self.keep[d] = partial(c ^ (2 * d))
            if last is not None:
                pass_on(last)
            last = d
        sib[0].wait_recv()
        total = self.keep[0] + self.sib_recv[0].astype(f32)
        for d in order[:-1]:
            far[d].wait_recv()
            total = total + self.far_recv[d].astype(f32)
        for copy in list(sib.values()) + list(far.values()):
            copy.wait_send()
        return total


class Route:
    def __init__(self, net, parts, dst, sems, local):
        self.net, self.parts, self.dst, self.sems, self.local = net, parts, dst, sems, local
        self.per = 2 * net.chips // net.Z

    def each(self, remote, own):
        net = self.net
        c, Z = net.c, net.Z
        slot = c % Z
        for z in range(Z):
            target = z * self.per + c // Z
            copy = pltpu.make_async_remote_copy(
                self.parts.at[z], self.dst.at[slot], self.sems.at[0, z], self.sems.at[1, slot],
                device_id=(target, net.z), device_id_type=MESH,
            )
            here = pltpu.make_async_copy(self.parts.at[z], self.dst.at[slot], self.local)

            @pl.when(target != c)
            def _():
                remote(copy)

            @pl.when(target == c)
            def _():
                own(here)

    def start(self):
        self.each(lambda copy: copy.start(), lambda here: here.start())

    def wait(self):
        net = self.net
        for s in range(net.Z):
            source = (net.c % self.per) * net.Z + s

            @pl.when(source != net.c)
            def _():
                pltpu.make_async_remote_copy(
                    self.dst.at[s], self.dst.at[s], self.sems.at[0, s], self.sems.at[1, s],
                    device_id=(net.c ^ 1, net.z), device_id_type=MESH,
                ).wait_recv()

        self.each(lambda copy: copy.wait_send(), lambda here: here.wait())


class Vectors:
    names = ("gain1", "shift1", "qv", "out", "gain2", "shift2", "up", "down")

    def __init__(self, ref, Z, sizes):
        self.ref, self.Z, self.at = ref, Z, {}
        start = 0
        for name, size in zip(self.names, sizes):
            self.at[name] = (start, size)
            start += size

    def get(self, name):
        start, size = self.at[name]
        return jnp.concatenate(
            [self.ref[z, :, start : start + size] for z in range(self.Z)], axis=1
        )


def forward_kernel(
    chips, Z, sizes,
    x_in, cot_in, vec_in, bias_in, first_in, wqkv_in, wout_in, wup_in, wdown_in,
    n1, qkv, mix, lse, resid, n2, cot, wqkv, wout, wup, wdown, vec,
    xs, wout_parts, sib_send, sib_recv, far_send, far_recv, keep, sems, local,
):
    net = Net(chips, Z)
    c = net.c
    C = 2 * chips
    R, D = x_in.shape
    S = R * C
    hw = mix.shape[1]
    heads = hw // HEAD_DIM
    net.barrier()
    zv = ZExchange(net, vec_in, vec, sems.at[0], local.at[0])
    zq = ZExchange(net, wqkv_in, wqkv, sems.at[1], local.at[1])
    zo = ZExchange(net, wout_in, wout_parts, sems.at[2], local.at[2])
    zu = ZExchange(net, wup_in, wup, sems.at[3], local.at[3])
    zd = ZExchange(net, wdown_in, wdown, sems.at[4], local.at[4])
    zv.start()
    gx = Gather(net, x_in, xs, sems.at[5])
    gx.begin()
    zq.start()
    own = pltpu.make_async_copy(x_in, xs.at[c], local.at[5])
    own.start()
    own_cot = pltpu.make_async_copy(cot_in, cot.at[c], local.at[6])
    own_cot.start()
    own.wait()
    zv.wait()
    vectors = Vectors(vec, Z, sizes)
    gain1, shift1 = vectors.get("gain1"), vectors.get("shift1")

    def norm_one(d):
        block = c ^ d
        xhat, _ = row_stats(xs[block].astype(f32))
        n1[block] = (xhat * gain1 + shift1).astype(bf16)

    norm_one(0)
    gx.middle()
    gx.finish(norm_one)
    gc = Gather(net, cot_in, cot, sems.at[6])
    gc.begin()
    zq.wait()
    zo.start()
    zu.start()
    w = wqkv[...].reshape(D, 3 * hw)
    bias = bias_in[...]
    step = 2 * R

    def project(i, carry):
        rows = pl.ds(pl.multiple_of(i * step, step), step)
        a = n1[pl.ds(2 * i, 2)].reshape(step, D)
        qkv[rows, :] = (mm(a, w, NN) + bias).astype(bf16)
        return carry

    lax.fori_loop(0, S // step, project, 0)
    gc.middle()

    route = Route(net, wout_parts, wout, sems.at[9], local.at[7])
    for i in range(S // step):
        if i == S // step - 2:
            zo.wait()
            route.start()
        rows = pl.ds(i * step, step)
        n = (i + 1) * step
        row = lax.broadcasted_iota(jnp.int32, (step, n), 0) + i * step
        col = lax.broadcasted_iota(jnp.int32, (step, n), 1)
        allowed = (col <= row) & (col >= first_in[rows, :])
        parts = []
        for h in range(heads):
            lane = h * HEAD_DIM
            q = qkv[rows, lane : lane + HEAD_DIM]
            k = qkv[0:n, hw + lane : hw + lane + HEAD_DIM]
            v = qkv[0:n, 2 * hw + lane : 2 * hw + lane + HEAD_DIM]
            s = jnp.where(allowed, mm(q, k, NT) * score_scale, masked_score)
            top = jnp.max(s, axis=1, keepdims=True)
            e = jnp.exp(s - top)
            total = jnp.sum(e, axis=1, keepdims=True)
            parts.append((mm(e.astype(bf16), v, NN) / total).astype(bf16))
            lse[h, rows, :] = top + jnp.log(total)
        mix[rows, :] = jnp.concatenate(parts, axis=1) if heads > 1 else parts[0]
    gc.finish()
    route.wait()
    zu.wait()
    zd.start()
    w_o = wout[...].reshape(hw, D)

    def out_part(block):
        return mm(mix[pl.ds(pl.multiple_of(block * R, R), R), :], w_o, NN)

    red = Reduce(net, R, D, sems.at[7], sib_send, sib_recv, far_send, far_recv, keep)
    total = red.run(out_part)
    r = xs[c].astype(f32) + total + vectors.get("out")
    resid[...] = r
    xhat2, _ = row_stats(r)
    n2[c] = (xhat2 * vectors.get("gain2") + vectors.get("shift2")).astype(bf16)
    gn = Gather(net, n2.at[c], n2, sems.at[8])
    gn.begin()
    gn.middle()
    gn.finish()
    zd.wait()
    own_cot.wait()
    for exchange in (zv, zq, zo, zu, zd):
        exchange.finish()


def columns(weight, start, width):
    return lax.dynamic_slice_in_dim(weight, start, width, axis=1)


def shards(
    tokens_in,
    doc_lengths,
    norm1_gain,
    norm1_bias,
    qkv_weight,
    qv_bias,
    out_weight,
    out_bias,
    norm2_gain,
    norm2_bias,
    up_weight,
    up_bias,
    down_weight,
    down_bias,
    out_cotangent,
):
    C = lax.axis_size("ctx")
    Z = lax.axis_size("fsdp")
    c = lax.axis_index("ctx")
    rows, width = tokens_in.shape[1:]
    seq = rows * C
    heads = HEADS // C
    hw = heads * HEAD_DIM
    ff = up_weight.shape[1]
    fw = ff // C

    chips = C // 2
    fz, fzc = ff // Z, ff // Z // C
    orows = width // (C * Z)

    def scatter_ctx(x):
        return lax.psum_scatter(x.astype(bf16), "ctx", scatter_dimension=0, tiled=True).astype(f32)

    def along_ctx(x):
        return lax.all_gather(x, "ctx", axis=0, tiled=True)

    all_vectors = (
        norm1_gain, norm1_bias, qv_bias, out_bias, norm2_gain, norm2_bias, up_bias, down_bias
    )
    sizes = tuple(v.shape[0] for v in all_vectors)
    vec_in = jnp.concatenate(all_vectors).astype(f32)[None]
    wqkv_in = jnp.concatenate(
        [columns(qkv_weight, part * width + c * hw, hw) for part in range(3)], axis=1
    )
    wup_in = lax.dynamic_index_in_dim(
        up_weight.reshape(width // Z, Z, C, fzc), c, axis=2, keepdims=False
    ).reshape(width // Z, fw)
    wdown_in = lax.dynamic_slice_in_dim(down_weight, c * fzc, fzc, axis=0)
    wout_in = lax.dynamic_slice_in_dim(out_weight, c * orows, orows, axis=0)

    ends = jnp.cumsum(doc_lengths[0])
    pos = jnp.arange(seq, dtype=jnp.int32)
    first = jnp.max(jnp.where(ends[None, :] <= pos[:, None], ends[None, :], 0), axis=1)[:, None]

    vec_q = lax.all_gather(qv_bias, "fsdp", axis=0, tiled=True).astype(f32)
    bias = jnp.concatenate(
        [
            lax.dynamic_slice_in_dim(vec_q, c * hw, hw),
            jnp.zeros((hw,), f32),
            lax.dynamic_slice_in_dim(vec_q, width + c * hw, hw),
        ]
    )[None]

    sds = jax.ShapeDtypeStruct
    V = sum(sizes)
    outs = (
        sds((C, rows, width), bf16),
        sds((seq, 3 * hw), bf16),
        sds((seq, hw), bf16),
        sds((heads, seq, 1), f32),
        sds((rows, width), f32),
        sds((C, rows, width), bf16),
        sds((C, rows, width), bf16),
        sds((Z, width // Z, 3 * hw), bf16),
        sds((Z, orows, width), bf16),
        sds((Z, width // Z, fw), bf16),
        sds((Z, fzc, width), bf16),
        sds((Z, 1, V), f32),
    )
    nsem = max(13, 2 * C)
    vmem = pltpu.VMEM
    any_in = pl.BlockSpec(memory_space=pl.ANY)
    vmem_in = pl.BlockSpec(memory_space=vmem)
    n1, qkv, mix, lse, resid, n2, cot, w_qkv, w_out, w_up, w_down, vec = pl.pallas_call(
        functools.partial(forward_kernel, chips, Z, sizes),
        out_shape=outs,
        in_specs=[any_in] * 3 + [vmem_in] * 2 + [any_in] * 4,
        out_specs=[vmem_in] * len(outs),
        scratch_shapes=[
            vmem((C, rows, width), bf16),
            vmem((Z, orows, width), bf16),
            vmem((chips, rows, width), bf16),
            vmem((chips, rows, width), bf16),
            vmem((chips, rows, width), bf16),
            vmem((chips, rows, width), bf16),
            vmem((chips, rows, width), f32),
            pltpu.SemaphoreType.DMA((10, 2, nsem)),
            pltpu.SemaphoreType.DMA((8,)),
        ],
        compiler_params=pltpu.CompilerParams(
            collective_id=1, has_side_effects=True, vmem_limit_bytes=56 << 20
        ),
        name="forward",
    )(tokens_in[0], out_cotangent[0], vec_in, bias, first, wqkv_in, wout_in, wup_in, wdown_in)

    n1, n2, cot = (v.reshape(seq, width) for v in (n1, n2, cot))
    w_qkv, w_up = w_qkv.reshape(width, 3 * hw), w_up.reshape(width, fw)
    w_out, w_down = w_out.reshape(hw, width), w_down.reshape(fw, width)
    pieces, at = [], 0
    for size in sizes:
        pieces.append(vec[:, 0, at : at + size].reshape(-1))
        at += size
    gain_one, shift_one, b_qv, b_out, gain_two, shift_two, b_up, b_down = pieces
    x = tokens_in[0].astype(f32)
    xhat1, scale1 = row_stats(x)
    xhat2, scale2 = row_stats(resid)
    allowed = (pos[None, :] <= pos[:, None]) & (pos[None, :] >= first)

    def head(part, h):
        at = part * hw + h * HEAD_DIM
        return qkv[:, at : at + HEAD_DIM]

    b_up_part = lax.dynamic_index_in_dim(b_up.reshape(Z, C, fzc), c, axis=1, keepdims=False)
    pre = mm(n2, w_up, NN) + b_up_part.reshape(fw)
    value, slope = gelu_both(pre)
    hidden = value.astype(bf16)
    layer_out = (resid + scatter_ctx(mm(hidden, w_down, NN)) + b_down).astype(bf16)[None]

    hidden_grad = mm(cot, w_down, NT)
    pre_grad = (hidden_grad * slope).astype(bf16)
    down_w_grad = mm(hidden, cot, TN)
    up_w_grad = mm(n2, pre_grad, TN)
    up_b_grad = jnp.sum(pre_grad.astype(f32), axis=0)
    n2_grad = scatter_ctx(mm(pre_grad, w_up, NT))
    cot_own = out_cotangent[0].astype(f32)
    resid_grad = cot_own + norm_back(n2_grad, xhat2, scale2, gain_two)
    branch_own = resid_grad.astype(bf16)
    branch = along_ctx(branch_own)
    out_w_grad = mm(mix, branch, TN)
    mix_grad = mm(branch, w_out, NT).astype(bf16)

    grads = [[], [], []]
    for h in range(heads):
        at = h * HEAD_DIM
        q, k, v = (head(part, h) for part in range(3))
        g = mix_grad[:, at : at + HEAD_DIM]
        p = jnp.where(allowed, jnp.exp(mm(q, k, NT) * score_scale - lse[h]), 0.0)
        delta = jnp.sum(g.astype(f32) * mix[:, at : at + HEAD_DIM].astype(f32), axis=1, keepdims=True)
        ds = (p * (mm(g, v, NT) - delta)).astype(bf16)
        grads[0].append(score_scale * mm(ds, k, NN))
        grads[1].append(score_scale * mm(ds, q, TN))
        grads[2].append(mm(p.astype(bf16), g, TN))
    qkv_grad = jnp.concatenate(grads[0] + grads[1] + grads[2], axis=1).astype(bf16)

    qkv_w_grad = mm(n1, qkv_grad, TN)
    qkv_sums = jnp.sum(qkv_grad.astype(f32), axis=0)
    n1_grad = scatter_ctx(mm(qkv_grad, w_qkv, NT))
    input_grad = (resid_grad + norm_back(n1_grad, xhat1, scale1, gain_one)).astype(bf16)[None]

    def rows_home(grad):
        return lax.psum_scatter(grad.astype(bf16), "fsdp", scatter_dimension=0, tiled=True).astype(f32)

    def columns_home(grad):
        r = grad.shape[0] // (C * Z)
        grad = grad.astype(bf16).reshape(C, Z, r, grad.shape[1])
        mine = lax.psum_scatter(grad, "fsdp", scatter_dimension=1, tiled=True)[:, 0]
        return lax.all_to_all(mine, "ctx", 0, 0, tiled=False).astype(f32)

    order = [(i * Z + j, j * C + i) for i in range(C) for j in range(Z)]
    d_down = lax.ppermute(rows_home(down_w_grad).astype(bf16), ("ctx", "fsdp"), order).astype(f32)
    d_out = rows_home(out_w_grad)
    up_parts = columns_home(up_w_grad)
    d_up = up_parts.reshape(C, -1, Z, fzc).transpose(1, 2, 0, 3).reshape(-1, ff)
    qkv_parts = columns_home(qkv_w_grad)
    r = qkv_parts.shape[1]
    d_qkv = qkv_parts.reshape(C, r, 3, hw).transpose(1, 2, 0, 3).reshape(r, 3 * width)

    def spread(v, size):
        return lax.dynamic_update_slice(jnp.zeros((size,), f32), v, (c * v.shape[0],))

    parts = [
        jnp.sum(n1_grad * xhat1, axis=0),
        jnp.sum(n1_grad, axis=0),
        jnp.concatenate([spread(qkv_sums[:hw], width), spread(qkv_sums[2 * hw :], width)]),
        jnp.sum(branch_own.astype(f32), axis=0),
        jnp.sum(n2_grad * xhat2, axis=0),
        jnp.sum(n2_grad, axis=0),
        lax.dynamic_update_slice(
            jnp.zeros((Z, C, fzc), f32), up_b_grad.reshape(Z, 1, fzc), (0, c, 0)
        ).reshape(ff),
        jnp.sum(cot_own, axis=0),
    ]
    packed = jnp.concatenate([p.reshape(C * Z, -1) for p in parts], axis=1)
    packed = lax.psum_scatter(packed, ("ctx", "fsdp"), scatter_dimension=0, tiled=True)[0]
    small, at = [], 0
    for p in parts:
        n = p.shape[0] // (C * Z)
        small.append(packed[at : at + n])
        at += n
    return (
        layer_out,
        input_grad,
        small[0],
        small[1],
        d_qkv,
        small[2],
        d_out,
        small[3],
        small[4],
        small[5],
        d_up,
        small[6],
        d_down,
        small[7],
    )


def solution(mesh):
    token = P("fsdp", "ctx", None)
    flat, table = P("fsdp"), P("fsdp", None)
    home, home2 = P(("ctx", "fsdp")), P(("ctx", "fsdp"), None)
    return jax.shard_map(
        shards,
        mesh=mesh,
        in_specs=(
            token, table, flat, flat, table, flat, table, flat,
            flat, flat, table, flat, table, flat, token,
        ),
        out_specs=(
            token, token, home, home, home2, home, home2, home,
            home, home, home2, home, home2, home,
        ),
        check_vma=False,
    )
```

```python
import functools
import jax
import jax.numpy as jnp
from jax import lax
from jax.experimental import pallas as pl
from jax.experimental.pallas import tpu as pltpu
from jax.sharding import PartitionSpec as P

HEADS = 16
HEAD_DIM = 64
MESH = pl.DeviceIdType.MESH

epsilon = 1e-05
masked_score = -1e30
score_scale = HEAD_DIM ** (-0.5)
f32 = jnp.float32
bf16 = jnp.bfloat16


def row_stats(values):
    mean = jnp.mean(values, axis=-1, keepdims=True)
    centre = values - mean
    spread = jnp.mean(centre * centre, axis=-1, keepdims=True)
    scale = lax.rsqrt(spread + epsilon)
    return centre * scale, scale


def norm_back(grad, xhat, scale, gain):
    gh = grad * gain
    return scale * (
        gh
        - jnp.mean(gh, axis=-1, keepdims=True)
        - xhat * jnp.mean(gh * xhat, axis=-1, keepdims=True)
    )


def gelu_both(v):
    k = 0.7978845608028654
    square = v * v
    inner = jnp.tanh(k * v * (1.0 + 0.044715 * square))
    half = 0.5 * (1.0 + inner)
    slope = half + 0.5 * v * (1.0 - inner * inner) * (k * (1.0 + 3 * 0.044715 * square))
    return v * half, slope


def mm(a, b, dims):
    return lax.dot_general(a, b, (dims, ((), ())), preferred_element_type=f32)


NN = ((1,), (0,))
NT = ((1,), (1,))
TN = ((0,), (0,))


def column_sum(v):
    return jnp.sum(v, axis=0, keepdims=True)


def bits(n):
    out = []
    while n > 1:
        n //= 2
        out.append(n)
    return out


class Net:
    def __init__(self, chips, Z, sems):
        self.chips, self.Z, self.C = chips, Z, 2 * chips
        self.c = lax.axis_index("ctx")
        self.z = lax.axis_index("fsdp")
        self.sems, self.used = sems, 0
        block = self.z * self.C + self.c
        self.home = (block // Z, block % Z)
        mine = self.c * Z + self.z
        self.origin = (mine % self.C, mine // self.C)
        self.at_home = block == mine

    def take(self, count):
        self.used += count
        return self.used - count

    def barrier(self):
        sem = pltpu.get_barrier_semaphore()
        peers = [(self.c ^ d, self.z) for d in range(1, self.C)]
        peers += [(self.c, self.z ^ d) for d in range(1, self.Z)]
        for peer in peers:
            pl.semaphore_signal(sem, inc=1, device_id=peer, device_id_type=MESH)

        @pl.when(jnp.logical_not(self.at_home))
        def _():
            for peer in (self.home, self.origin):
                pl.semaphore_signal(sem, inc=1, device_id=peer, device_id_type=MESH)

        pl.semaphore_wait(sem, len(peers) + jnp.where(self.at_home, 0, 2))

    def to(self, device, src, dst, out, into):
        return pltpu.make_async_remote_copy(
            src, dst, self.sems.at[0, out], self.sems.at[1, into],
            device_id=device, device_id_type=MESH,
        )

    def to_ctx(self, d, src, dst, i):
        return self.to((self.c ^ d, self.z), src, dst, i, i)

    def to_z(self, d, src, dst, i):
        return self.to((self.c, self.z ^ d), src, dst, i, i)


class ZGather:
    def __init__(self, net, dst):
        self.net, self.dst = net, dst
        self.base = net.take(net.Z)
        self.copies, self.got = {}, {0}

    def send(self, e, d):
        part = self.dst.at[self.net.z ^ e]
        copy = self.net.to_z(d, part, part, self.base + (e ^ d))
        copy.start()
        self.copies[e ^ d] = copy

    def begin(self):
        for d in bits(self.net.Z):
            self.send(0, d)

    def receive(self, e):
        if e not in self.got:
            self.copies[e].wait_recv()
            self.got.add(e)

    def relay(self):
        held = [0]
        for d in bits(self.net.Z):
            for e in held[1:]:
                self.receive(e)
                self.send(e, d)
            held = held + [e ^ d for e in held]

    def wait(self):
        for e in range(self.net.Z):
            self.receive(e)

    def finish(self):
        for copy in self.copies.values():
            copy.wait_send()


class ZReduce:
    def __init__(self, net, shard, recv, sums):
        self.net, self.shard, self.recv, self.sums = net, shard, recv, sums
        self.base = net.take(net.Z)
        self.terms = {e: [shard(net.z ^ e)] for e in range(net.Z)}
        self.copies, self.slot, self.full = [], 0, 0
        self.stages = bits(net.Z)[::-1]
        self.pending = {}

    def load(self, e):
        if e in self.pending:
            for copy in self.pending.pop(e):
                copy.wait_recv()
        total = None
        for ref in self.terms[e]:
            v = ref[...].astype(f32)
            total = v if total is None else total + v
        return total

    def stage(self, d):
        go = [e for e in sorted(self.terms) if e & d]
        for e in go:
            ref = self.terms[e][0]
            if len(self.terms[e]) > 1:
                total = self.load(e)
                ref = self.sums.at[self.full]
                self.full += 1
                ref[...] = total.astype(bf16)
            del self.terms[e]
            keep = e ^ d
            into = self.recv.at[self.slot]
            copy = self.net.to_z(d, ref, into, self.base + self.slot)
            copy.start()
            self.slot += 1
            self.copies.append(copy)
            self.pending.setdefault(keep, []).append(copy)
            self.terms[keep].append(into)

    def begin(self):
        self.stage(self.stages[0])

    def relay(self):
        for d in self.stages[1:]:
            self.stage(d)

    def total(self):
        return self.load(0)

    def finish(self):
        for copy in self.copies:
            copy.wait_send()


class Gather:
    def __init__(self, net, src, dst):
        self.net, self.src, self.dst = net, src, dst
        self.base = net.take(13 if net.chips == 4 else net.C)
        self.sent = []

    def copy(self, d, src, dst, i):
        copy = self.net.to_ctx(d, src, dst, self.base + i)
        copy.start()
        self.sent.append(copy)
        return copy

    def block(self, d, rows=None):
        index = self.net.c ^ d
        return self.dst.at[index] if rows is None else self.dst.at[index, rows]

    def begin(self):
        c = self.net.c
        if self.net.chips == 4:
            half = self.src.shape[0] // 2
            self.lo, self.hi = pl.ds(0, half), pl.ds(half, half)
            lo, hi, src, own = self.lo, self.hi, self.src, self.dst.at[c]
            self.x_lo = self.copy(2, src.at[lo], self.dst.at[c, lo], 0)
            self.y_hi = self.copy(4, src.at[hi], self.dst.at[c, hi], 1)
            self.x_hi = self.copy(2, src.at[hi], self.dst.at[c, hi], 2)
            self.y_lo = self.copy(4, src.at[lo], self.dst.at[c, lo], 3)
            self.beside = self.copy(1, src, own, 4)
        else:
            self.far = {
                d: self.copy(2 * d, self.src, self.dst.at[c], 2 * d)
                for d in range(self.net.chips - 1, 0, -1)
            }
            self.beside = self.copy(1, self.src, self.dst.at[c], 1)

    def relay(self, d, rows, target, i):
        part = self.block(d, rows)
        return self.copy(target, part, part, i)

    def middle(self):
        if self.net.chips == 4:
            self.x_lo.wait_recv()
            self.r_lo = self.relay(2, self.lo, 4, 5)
            self.s0 = self.relay(2, self.lo, 1, 6)
            self.y_hi.wait_recv()
            self.r_hi = self.relay(4, self.hi, 2, 7)
            self.s1 = self.relay(4, self.hi, 1, 8)

    def finish(self, ready=None):
        ready = ready or (lambda d: None)
        self.beside.wait_recv()
        ready(1)
        if self.net.chips == 4:
            self.x_hi.wait_recv()
            s2 = self.relay(2, self.hi, 1, 9)
            ready(2)
            self.y_lo.wait_recv()
            s3 = self.relay(4, self.lo, 1, 10)
            ready(4)
            self.r_lo.wait_recv()
            s4 = self.relay(6, self.lo, 1, 11)
            self.r_hi.wait_recv()
            s5 = self.relay(6, self.hi, 1, 12)
            ready(6)
            self.s0.wait_recv()
            s2.wait_recv()
            ready(3)
            self.s1.wait_recv()
            s3.wait_recv()
            ready(5)
            s4.wait_recv()
            s5.wait_recv()
            ready(7)
        else:
            on = {}
            for d, copy in self.far.items():
                copy.wait_recv()
                on[d] = self.relay(2 * d, None, 1, 2 * d + 1)
                ready(2 * d)
            for d, copy in on.items():
                copy.wait_recv()
                ready(2 * d + 1)
        for copy in self.sent:
            copy.wait_send()


class Reduce:
    def __init__(self, net, sib_send, sib_recv, far_send, far_recv, keep):
        self.net = net
        self.base = net.take(2 * net.chips)
        self.sib_send, self.sib_recv = sib_send, sib_recv
        self.far_send, self.far_recv, self.keep = far_send, far_recv, keep
        self.sib, self.far = {}, {}

    def pass_on(self, d):
        self.sib[d].wait_recv()
        total = self.keep[d] + self.sib_recv[d].astype(f32)
        self.far_send[d] = total.astype(bf16)
        self.far[d] = self.net.to_ctx(
            2 * d, self.far_send.at[d], self.far_recv.at[d], self.base + self.net.chips + d
        )
        self.far[d].start()

    def begin(self, partial):
        net = self.net
        core, chip = net.c % 2, net.c // 2
        last = None
        for d in range(net.chips - 1, -1, -1):
            terms = partial(chip ^ d)
            rows = terms.shape[0] // 2
            low, high = terms[:rows], terms[rows:]
            self.sib_send[d] = jnp.where(core == 0, high, low).astype(bf16)
            self.sib[d] = net.to_ctx(1, self.sib_send.at[d], self.sib_recv.at[d], self.base + d)
            self.sib[d].start()
            self.keep[d] = jnp.where(core == 0, low, high)
            if last is not None:
                self.pass_on(last)
            last = d

    def finish(self):
        self.sib[0].wait_recv()
        total = self.keep[0] + self.sib_recv[0].astype(f32)
        for d in range(self.net.chips - 1, 0, -1):
            self.far[d].wait_recv()
            total = total + self.far_recv[d].astype(f32)
        for copy in list(self.sib.values()) + list(self.far.values()):
            copy.wait_send()
        return total


class Swap:
    def __init__(self, net, parts, dst):
        self.net, self.parts, self.dst = net, parts, dst
        self.base = net.take(net.C)

    def start(self):
        net = self.net
        self.copies = [
            net.to_ctx(d, self.parts.at[net.c ^ d], self.dst.at[net.c], self.base + d)
            for d in range(net.C - 1, 0, -1)
        ]
        for copy in self.copies:
            copy.start()
        self.dst[net.c] = self.parts[net.c]

    def wait(self):
        for copy in self.copies:
            copy.wait()


class Spread:
    def __init__(self, net, dst, plane):
        self.net, self.dst, self.plane = net, dst, plane
        self.base = net.take(net.C if plane else net.Z)

    def start(self):
        net = self.net
        part = self.dst.at[net.c if self.plane else net.z]
        send = net.to_ctx if self.plane else net.to_z
        count = net.C if self.plane else net.Z
        self.copies = [send(d, part, part, self.base + d) for d in range(count - 1, 0, -1)]
        for copy in self.copies:
            copy.start()

    def wait(self):
        for copy in self.copies:
            copy.wait()


class Route:
    def __init__(self, net, parts, dst, local):
        self.net, self.parts, self.dst, self.local = net, parts, dst, local
        self.base = net.take(net.Z)
        self.per = net.C // net.Z

    def each(self, remote, own):
        net = self.net
        slot = net.c % net.Z
        for z in range(net.Z):
            target = z * self.per + net.c // net.Z
            copy = net.to(
                (target, net.z), self.parts.at[z], self.dst.at[slot], self.base + z, self.base + slot
            )
            here = pltpu.make_async_copy(self.parts.at[z], self.dst.at[slot], self.local)

            @pl.when(target != net.c)
            def _():
                remote(copy)

            @pl.when(target == net.c)
            def _():
                own(here)

    def start(self):
        self.each(lambda copy: copy.start(), lambda here: here.start())

    def wait(self):
        net = self.net
        for s in range(net.Z):
            source = (net.c % self.per) * net.Z + s

            @pl.when(source != net.c)
            def _():
                part = self.dst.at[s]
                net.to((net.c ^ 1, net.z), part, part, self.base + s, self.base + s).wait_recv()

        self.each(lambda copy: copy.wait_send(), lambda here: here.wait())


class Vectors:
    names = ("gain1", "shift1", "qv", "out", "gain2", "shift2", "up", "down")

    def __init__(self, ref, Z, sizes):
        self.ref, self.Z, self.at = ref, Z, {}
        start = 0
        for name, size in zip(self.names, sizes):
            self.at[name] = (start, size)
            start += size

    def get(self, name):
        start, size = self.at[name]
        return jnp.concatenate(
            [self.ref[z, :, start : start + size] for z in range(self.Z)], axis=1
        )


def chosen(pieces, index):
    out = jnp.zeros_like(pieces[0])
    for i, piece in enumerate(pieces):
        out = jnp.where(index == i, piece, out)
    return out


def layer_kernel(names, chips, Z, sizes, aligned, *refs):
    ref = dict(zip(names, refs))
    net = Net(chips, Z, ref["sems"])
    local = ref["local"]
    c, z, C = net.c, net.z, net.C
    x_in, cot_in = ref["x_in"], ref["cot_in"]
    R, D = x_in.shape
    S = R * C
    hw = ref["mix"].shape[1]
    heads = hw // HEAD_DIM
    fw = ref["hid"].shape[1]
    fzc = fw // Z
    r = D // (C * Z)
    step = 2 * R
    xs, n1, n2, cot, bg = (ref[k] for k in ("xs", "n1", "n2", "cot", "bg"))
    qkv, mix, lse = ref["qkv"], ref["mix"], ref["lse"]

    started = []

    def bring(src, dst, i):
        copy = pltpu.make_async_copy(src, dst, local.at[i])
        copy.start()
        return copy

    load_vec = [bring(ref["vec_in"], ref["vec"].at[z], 0)]
    load_x = bring(x_in, xs.at[c], 1)
    if aligned:
        load_q = [
            bring(
                ref["wqkv_in"].at[:, pl.ds(pl.multiple_of(p * D + c * hw, hw), hw)],
                ref["wqkv"].at[z, :, p * hw : (p + 1) * hw], 2 + p,
            )
            for p in range(3)
        ]
        FZ = fzc * C
        load_u = [
            bring(
                ref["wup_in"].at[:, pl.ds(pl.multiple_of(p * FZ + c * fzc, fzc), fzc)],
                ref["wup"].at[z, :, p * fzc : (p + 1) * fzc], 8 + p,
            )
            for p in range(Z)
        ]
    else:
        load_q = [bring(ref["wqkv_in"], ref["wqkv"].at[z], 2)]
        load_u = [bring(ref["wup_in"], ref["wup"].at[z], 8)]
    load_o = bring(ref["wout_in"].at[pl.ds(pl.multiple_of(c * r, r), r)], ref["wout_parts"].at[z], 5)
    load_d = bring(ref["wdown_in"].at[pl.ds(pl.multiple_of(c * fzc, fzc), fzc)], ref["wdown"].at[z], 6)
    load_c = bring(cot_in, cot.at[c], 7)

    zv, zq = ZGather(net, ref["vec"]), ZGather(net, ref["wqkv"])
    zo, zu = ZGather(net, ref["wout_parts"]), ZGather(net, ref["wup"])
    zd = ZGather(net, ref["wdown"])
    net.barrier()
    load_vec[0].wait()
    zv.begin()
    gx = Gather(net, x_in, xs)
    gx.begin()
    for copy in load_q:
        copy.wait()
    zq.begin()

    pos = lax.broadcasted_iota(jnp.int32, (S, 1), 0)
    first = jnp.zeros((S, 1), jnp.int32)
    end = jnp.int32(0)
    for i in range(ref["docs"].shape[1]):
        end = end + ref["docs"][0, i]
        first = jnp.where(pos >= end, end, first)
    ref["first"][...] = first

    zv.relay()
    zv.wait()
    vectors = Vectors(ref["vec"], Z, sizes)
    gain1, shift1 = vectors.get("gain1"), vectors.get("shift1")
    load_x.wait()

    def norm_one(d):
        block = c ^ d
        xhat, _ = row_stats(xs[block].astype(f32))
        n1[block] = (xhat * gain1 + shift1).astype(bf16)

    norm_one(0)
    gx.middle()
    zq.relay()
    gx.finish(norm_one)
    load_o.wait()
    zo.begin()
    for copy in load_u:
        copy.wait()
    zu.begin()
    load_c.wait()
    gc = Gather(net, cot_in, cot)
    gc.begin()

    qv = vectors.get("qv")
    bias = jnp.concatenate(
        [
            chosen([qv[:, i * hw : (i + 1) * hw] for i in range(C)], c),
            jnp.zeros((1, hw), f32),
            chosen([qv[:, D + i * hw : D + (i + 1) * hw] for i in range(C)], c),
        ],
        axis=1,
    )
    zq.wait()
    w_qkv = ref["wqkv"][...].reshape(D, 3 * hw)

    def blocks(array, i):
        return array[pl.ds(2 * i, 2)].reshape(step, D)

    def tile(i):
        return pl.ds(pl.multiple_of(i * step, step), step)

    def project(i, carry):
        qkv[tile(i), :] = (mm(blocks(n1, i), w_qkv, NN) + bias).astype(bf16)
        return carry

    lax.fori_loop(0, S // step, project, 0)
    gc.middle()
    zo.relay()

    route = Route(net, ref["wout_parts"], ref["wout"], local.at[5])
    tiles = S // step

    def masked(i):
        n = (i + 1) * step
        row = lax.broadcasted_iota(jnp.int32, (step, n), 0) + i * step
        col = lax.broadcasted_iota(jnp.int32, (step, n), 1)
        return (col <= row) & (col >= ref["first"][i * step : n, :])

    def head(part, h, rows):
        at = part * hw + h * HEAD_DIM
        return qkv[rows, at : at + HEAD_DIM]

    def beside(parts):
        return jnp.concatenate(parts, axis=1) if len(parts) > 1 else parts[0]

    for i in range(tiles):
        if i == tiles - 2:
            zo.wait()
            route.start()
            zu.relay()
            load_d.wait()
            zd.begin()
        n = (i + 1) * step
        rows, keys = slice(i * step, n), slice(0, n)
        allowed = masked(i)
        parts = []
        for h in range(heads):
            s = mm(head(0, h, rows), head(1, h, keys), NT) * score_scale
            s = jnp.where(allowed, s, masked_score)
            top = jnp.max(s, axis=1, keepdims=True)
            e = jnp.exp(s - top)
            total = jnp.sum(e, axis=1, keepdims=True)
            parts.append((mm(e.astype(bf16), head(2, h, keys), NN) / total).astype(bf16))
            lse[h, rows, :] = top + jnp.log(total)
        mix[rows, :] = beside(parts)
    gc.finish()
    route.wait()
    w_out = ref["wout"][...].reshape(hw, D)

    def reducer(k):
        return Reduce(
            net, ref["sib_send"], ref["sib_recv"].at[k % 2], ref["far_send"], ref["far_recv"].at[k % 2],
            ref["keep"],
        )

    red = reducer(0)
    red.begin(lambda chip: mm(mix[tile(chip), :], w_out, NN))
    zd.relay()
    total = red.finish()
    resid = xs[c].astype(f32) + total + vectors.get("out")
    xhat2, scale2 = row_stats(resid)
    gain2 = vectors.get("gain2")
    n2[c] = (xhat2 * gain2 + vectors.get("shift2")).astype(bf16)
    ref["resid"][...] = resid
    gn = Gather(net, n2.at[c], n2)
    gn.begin()
    gn.middle()
    zu.wait()
    w_up = ref["wup"][...].reshape(D, fw)
    up = vectors.get("up")
    b_up = jnp.concatenate(
        [
            chosen([up[:, (q * C + i) * fzc : (q * C + i + 1) * fzc] for i in range(C)], c)
            for q in range(Z)
        ],
        axis=1,
    )
    gn.finish()
    zd.wait()
    w_down = ref["wdown"][...].reshape(fw, D)
    hid, pg = ref["hid"], ref["pg"]

    def feed(i, sums):
        rows = tile(i)
        value, slope = gelu_both(mm(blocks(n2, i), w_up, NN) + b_up)
        hid[rows, :] = value.astype(bf16)
        grad = (mm(blocks(cot, i), w_down, NT) * slope).astype(bf16)
        pg[rows, :] = grad
        return sums + column_sum(grad.astype(f32))

    up_sums = lax.fori_loop(0, tiles, feed, jnp.zeros((1, fw), f32))

    red = reducer(1)
    red.begin(lambda chip: mm(pg[tile(chip), :], w_up, NT))

    lanes = 128

    def whole(array):
        return array[...].reshape(S, D)

    def chunk(i):
        return pl.ds(pl.multiple_of(i * lanes, lanes), lanes)

    dbuf, ubuf, obuf, qbuf = (ref[k] for k in ("dbuf", "ubuf", "obuf", "qbuf"))

    def down_part(i, carry):
        dbuf[chunk(i), :] = mm(hid[:, chunk(i)], whole(cot), TN).astype(bf16)
        return carry

    lax.fori_loop(0, fw // lanes, down_part, 0)
    rd = ZReduce(
        net, lambda zs: dbuf.at[pl.ds(pl.multiple_of(zs * fzc, fzc), fzc)], ref["drecv"], ref["dsum"]
    )
    rd.begin()
    per = lanes // (Z * r)

    def up_part(i, carry):
        grad = mm(n2[:, :, chunk(i)].reshape(S, lanes), pg[...], TN).astype(bf16)
        ubuf[pl.ds(i * per, per)] = grad.reshape(per, Z, r, fw)
        return carry

    lax.fori_loop(0, D // lanes, up_part, 0)
    ru = ZReduce(net, lambda zs: ubuf.at[:, zs], ref["urecv"], ref["usum"])
    ru.begin()

    n2_grad = red.finish()
    cot_own = cot[c].astype(f32)
    xhat2, scale2 = row_stats(ref["resid"][...])
    resid_grad = cot_own + norm_back(n2_grad, xhat2, scale2, gain2)
    branch = resid_grad.astype(bf16)
    bg[c] = branch
    ref["rgrad"][...] = resid_grad
    gb = Gather(net, bg.at[c], bg)
    gb.begin()
    sums = {
        "out": column_sum(branch.astype(f32)),
        "gain2": column_sum(n2_grad * xhat2),
        "shift2": column_sum(n2_grad),
        "down": column_sum(cot_own),
    }
    mg = ref["mg"]

    def back_out(d):
        block = c ^ d
        rows = pl.ds(pl.multiple_of(block * R, R), R)
        mg[rows, :] = mm(bg[block], w_out, NT).astype(bf16)

    back_out(0)
    gb.middle()
    rd.relay()
    gb.finish(back_out)
    obuf[...] = mm(mix[...], whole(bg), TN).astype(bf16)
    ro = ZReduce(
        net, lambda zs: obuf.at[pl.ds(pl.multiple_of(zs * r, r), r)], ref["orecv"], ref["osum"]
    )
    ro.begin()
    red = reducer(2)
    red.begin(lambda chip: mm(hid[tile(chip), :], w_down, NN))

    qg, dk, dv = ref["qg"], ref["dk"], ref["dv"]
    dk[...] = jnp.zeros((S, hw), f32)
    dv[...] = jnp.zeros((S, hw), f32)
    swap_up = Swap(net, ref["uparts"], ref["ufrom"])
    for i in range(tiles):
        n = (i + 1) * step
        rows, keys = slice(i * step, n), slice(0, n)
        allowed = masked(i)
        dqs, dks, dvs = [], [], []
        for h in range(heads):
            at = h * HEAD_DIM
            q, k, v = head(0, h, rows), head(1, h, keys), head(2, h, keys)
            g = mg[rows, at : at + HEAD_DIM]
            m = mix[rows, at : at + HEAD_DIM]
            s = mm(q, k, NT) * score_scale - lse[h, rows, :]
            p = jnp.where(allowed, jnp.exp(s), 0.0)
            delta = jnp.sum(g.astype(f32) * m.astype(f32), axis=1, keepdims=True)
            ds = (p * (mm(g, v, NT) - delta)).astype(bf16)
            dqs.append(score_scale * mm(ds, k, NN))
            dks.append(mm(ds, q, TN))
            dvs.append(mm(p.astype(bf16), g, TN))
        qg[rows, 0:hw] = beside(dqs).astype(bf16)
        dk[keys, :] += beside(dks)
        dv[keys, :] += beside(dvs)
        if i == tiles - 3:
            ref["hbuf"][...] = rd.total().astype(bf16)
            there = net.to(net.home, ref["hbuf"], ref["hrecv"], net.take(1), net.used - 1)
            here = pltpu.make_async_copy(ref["hbuf"], ref["hrecv"], local.at[0])

            @pl.when(net.at_home)
            def _():
                here.start()

            @pl.when(jnp.logical_not(net.at_home))
            def _():
                there.start()

            ru.relay()
        if i == tiles - 2:
            total = red.finish()
            ref["layer_out"][...] = (ref["resid"][...] + total + vectors.get("down")).astype(bf16)
            ro.relay()
    qg[:, hw : 2 * hw] = (score_scale * dk[...]).astype(bf16)
    qg[:, 2 * hw : 3 * hw] = dv[...].astype(bf16)

    def qkv_part(i, carry):
        grad = mm(n1[:, :, chunk(i)].reshape(S, lanes), qg[...], TN).astype(bf16)
        qbuf[pl.ds(i * per, per)] = grad.reshape(per, Z, r, 3 * hw)
        return carry

    lax.fori_loop(0, D // lanes, qkv_part, 0)
    rq = ZReduce(net, lambda zs: qbuf.at[:, zs], ref["qrecv"], ref["qsum"])
    rq.begin()
    red = reducer(3)
    red.begin(lambda chip: mm(qg[tile(chip), :], w_qkv, NT))
    qkv_sums = column_sum(qg[...].astype(f32))
    ref["uparts"][...] = ru.total().astype(bf16)
    swap_up.start()
    ref["d_out"][...] = ro.total()
    colz, colp = ref["colz"], ref["colp"]
    colz[z] = jnp.concatenate([qkv_sums[:, 0:hw], qkv_sums[:, 2 * hw : 3 * hw], up_sums], axis=1)
    line = Spread(net, colz, False)
    line.start()

    @pl.when(net.at_home)
    def _():
        here.wait()

    @pl.when(jnp.logical_not(net.at_home))
    def _():
        there.wait()

    ref["d_down"][...] = ref["hrecv"][...].astype(f32)
    swap_up.wait()
    for i in range(C):
        for q in range(Z):
            ref["d_up"][:, (q * C + i) * fzc : (q * C + i + 1) * fzc] = ref["ufrom"][
                i, :, q * fzc : (q + 1) * fzc
            ].astype(f32)
    line.wait()
    total = colz[0]
    for i in range(1, Z):
        total = total + colz[i]
    colp[c] = total
    plane = Spread(net, colp, True)
    plane.start()
    rq.relay()
    n1_grad = red.finish()
    xhat1, scale1 = row_stats(xs[c].astype(f32))
    ref["input_grad"][...] = (
        ref["rgrad"][...] + norm_back(n1_grad, xhat1, scale1, gain1)
    ).astype(bf16)
    stack = jnp.concatenate(
        [
            column_sum(n1_grad * xhat1), column_sum(n1_grad), sums["out"], sums["gain2"],
            sums["shift2"], sums["down"], jnp.zeros((2, D), f32),
        ],
        axis=0,
    )
    w = D // C
    for i in range(C):
        ref["tok_to"][i] = stack[:, i * w : (i + 1) * w]
    swap_tok = Swap(net, ref["tok_to"], ref["tok_from"])
    swap_tok.start()
    ref["qparts"][...] = rq.total().astype(bf16)
    swap_q = Swap(net, ref["qparts"], ref["qfrom"])
    swap_q.start()
    swap_tok.wait()
    tokz = ref["tokz"]
    total = ref["tok_from"][0]
    for i in range(1, C):
        total = total + ref["tok_from"][i]
    tokz[z] = total
    tok_line = Spread(net, tokz, False)
    tok_line.start()
    swap_q.wait()
    for i in range(C):
        for p in range(3):
            ref["d_qkv"][:, p * D + i * hw : p * D + (i + 1) * hw] = ref["qfrom"][
                i, :, p * hw : (p + 1) * hw
            ].astype(f32)
    tok_line.wait()
    total = tokz[0]
    for i in range(1, Z):
        total = total + tokz[i]
    ref["tok"][...] = total
    plane.wait()
    for part in (zv, zq, zo, zu, zd, rd, ru, ro, rq):
        part.finish()


def shards(
    tokens_in,
    doc_lengths,
    norm1_gain,
    norm1_bias,
    qkv_weight,
    qv_bias,
    out_weight,
    out_bias,
    norm2_gain,
    norm2_bias,
    up_weight,
    up_bias,
    down_weight,
    down_bias,
    out_cotangent,
):
    C, Z = lax.axis_size("ctx"), lax.axis_size("fsdp")
    c, z = lax.axis_index("ctx"), lax.axis_index("fsdp")
    R, D = tokens_in.shape[1:]
    chips, S, hw = C // 2, R * C, D // C
    ff = up_weight.shape[1]
    fw, fzc, r = ff // C, ff // (C * Z), D // (C * Z)
    heads = hw // HEAD_DIM
    all_vectors = (
        norm1_gain, norm1_bias, qv_bias, out_bias, norm2_gain, norm2_bias, up_bias, down_bias
    )
    sizes = tuple(v.shape[0] for v in all_vectors)
    V, W = sum(sizes), 2 * hw + fw
    vec_in = jnp.concatenate(all_vectors).astype(f32)[None]
    aligned = hw % 128 == 0 and fzc % 128 == 0
    wqkv_in, wup_in = qkv_weight, up_weight
    if not aligned:
        wqkv_in = lax.dynamic_index_in_dim(
            qkv_weight.reshape(D // Z, 3, C, hw), c, axis=2, keepdims=False
        ).reshape(D // Z, 3 * hw)
        wup_in = lax.dynamic_index_in_dim(
            up_weight.reshape(D // Z, Z, C, fzc), c, axis=2, keepdims=False
        ).reshape(D // Z, fw)

    vmem, hbm = pltpu.VMEM, pl.BlockSpec(memory_space=pl.ANY)
    ins = {
        "x_in": (tokens_in[0], hbm),
        "cot_in": (out_cotangent[0], hbm),
        "docs": (doc_lengths, pl.BlockSpec(memory_space=pltpu.SMEM)),
        "vec_in": (vec_in, hbm),
        "wqkv_in": (wqkv_in, hbm),
        "wout_in": (out_weight, hbm),
        "wup_in": (wup_in, hbm),
        "wdown_in": (down_weight, hbm),
    }
    outs = {
        "layer_out": ((R, D), bf16),
        "input_grad": ((R, D), bf16),
        "d_qkv": ((r, 3 * D), f32),
        "d_out": ((r, D), f32),
        "d_up": ((r, ff), f32),
        "d_down": ((fzc, D), f32),
        "tok": ((8, D // C), f32),
        "colp": ((C, 1, W), f32),
    }
    token, own = (C, R, D), (R, D)
    exchange = {"far_send": bf16, "sib_send": bf16, "keep": f32}
    scratch = {
        **{k: (token, bf16) for k in ("xs", "n1", "n2", "cot", "bg")},
        "qkv": ((S, 3 * hw), bf16),
        "qg": ((S, 3 * hw), bf16),
        "mix": ((S, hw), bf16),
        "mg": ((S, hw), bf16),
        "lse": ((heads, S, 1), f32),
        "dk": ((S, hw), f32),
        "dv": ((S, hw), f32),
        "hid": ((S, fw), bf16),
        "pg": ((S, fw), bf16),
        "resid": (own, f32),
        "rgrad": (own, f32),
        "vec": ((Z, 1, V), f32),
        "wqkv": ((Z, D // Z, 3 * hw), bf16),
        "wout_parts": ((Z, r, D), bf16),
        "wout": ((Z, r, D), bf16),
        "wup": ((Z, D // Z, fw), bf16),
        "wdown": ((Z, fzc, D), bf16),
        "first": ((S, 1), jnp.int32),
        **{k: ((chips, R, D), t) for k, t in exchange.items()},
        "sib_recv": ((2, chips, R, D), bf16),
        "far_recv": ((2, chips, R, D), bf16),
        "dbuf": ((fw, D), bf16),
        "ubuf": ((C, Z, r, fw), bf16),
        "obuf": ((hw, D), bf16),
        "qbuf": ((C, Z, r, 3 * hw), bf16),
        "hbuf": ((fzc, D), bf16),
        "hrecv": ((fzc, D), bf16),
        "colz": ((Z, 1, W), f32),
        "tok_to": ((C, 8, D // C), f32),
        "tok_from": ((C, 8, D // C), f32),
        "tokz": ((Z, 8, D // C), f32),
    }
    shard = {"d": (fzc, D), "u": (C, r, fw), "o": (r, D), "q": (C, r, 3 * hw)}
    for k, shape in shard.items():
        scratch[k + "recv"] = ((Z - 1, *shape), bf16)
        scratch[k + "sum"] = ((Z // 2, *shape), bf16)
    for k in ("u", "q"):
        scratch[k + "parts"] = (shard[k], bf16)
        scratch[k + "from"] = (shard[k], bf16)
    gathers = 4 * max(13, C)
    count = gathers + 10 * Z + 8 * chips + 5 * C + 8
    names = (*ins, *outs, *scratch, "sems", "local")
    got = pl.pallas_call(
        functools.partial(layer_kernel, names, chips, Z, sizes, aligned),
        out_shape=[jax.ShapeDtypeStruct(*v) for v in outs.values()],
        in_specs=[v[1] for v in ins.values()],
        out_specs=[pl.BlockSpec(memory_space=vmem)] * len(outs),
        scratch_shapes=[vmem(*v) for v in scratch.values()]
        + [pltpu.SemaphoreType.DMA((2, count)), pltpu.SemaphoreType.DMA((8 + Z,))],
        compiler_params=pltpu.CompilerParams(
            collective_id=1, has_side_effects=True, vmem_limit_bytes=63 << 20
        ),
        name="layer",
    )(*[v[0] for v in ins.values()])
    got = dict(zip(outs, got))

    mine = c * Z + z
    tok = lax.dynamic_slice_in_dim(got["tok"], z * r, r, axis=1)
    col = got["colp"][:, 0]
    qv = jnp.concatenate([col[:, :hw].reshape(D), col[:, hw : 2 * hw].reshape(D)])
    up = col[:, 2 * hw :].reshape(C, Z, fzc).transpose(1, 0, 2).reshape(C * Z, fzc)
    return (
        got["layer_out"][None],
        got["input_grad"][None],
        tok[0],
        tok[1],
        got["d_qkv"],
        lax.dynamic_index_in_dim(qv.reshape(C * Z, -1), mine, keepdims=False),
        got["d_out"],
        tok[2],
        tok[3],
        tok[4],
        got["d_up"],
        lax.dynamic_index_in_dim(up, mine, keepdims=False),
        got["d_down"],
        tok[5],
    )


def solution(mesh):
    token = P("fsdp", "ctx", None)
    flat, table = P("fsdp"), P("fsdp", None)
    home, home2 = P(("ctx", "fsdp")), P(("ctx", "fsdp"), None)
    return jax.shard_map(
        shards,
        mesh=mesh,
        in_specs=(
            token, table, flat, flat, table, flat, table, flat,
            flat, flat, table, flat, table, flat, token,
        ),
        out_specs=(
            token, token, home, home, home2, home, home2, home,
            home, home, home2, home, home2, home,
        ),
        check_vma=False,
    )
```

```python
import functools
from types import SimpleNamespace

import jax
import jax.numpy as jnp
from jax import lax
from jax.experimental import pallas as pl
from jax.experimental.pallas import tpu as pltpu
from jax.sharding import PartitionSpec as P

HEADS = 16
HEAD_DIM = 64
MESH = pl.DeviceIdType.MESH

epsilon = 1e-05
masked_score = -1e30
score_scale = HEAD_DIM ** (-0.5)
f32 = jnp.float32
bf16 = jnp.bfloat16


def row_stats(values):
    mean = jnp.mean(values, axis=-1, keepdims=True)
    centre = values - mean
    spread = jnp.mean(centre * centre, axis=-1, keepdims=True)
    scale = lax.rsqrt(spread + epsilon)
    return centre * scale, scale


def norm_back(grad, xhat, scale, gain):
    gh = grad * gain
    return scale * (
        gh
        - jnp.mean(gh, axis=-1, keepdims=True)
        - xhat * jnp.mean(gh * xhat, axis=-1, keepdims=True)
    )


def gelu_both(v):
    k = 0.7978845608028654
    square = v * v
    inner = jnp.tanh(k * v * (1.0 + 0.044715 * square))
    half = 0.5 * (1.0 + inner)
    slope = half + 0.5 * v * (1.0 - inner * inner) * (k * (1.0 + 3 * 0.044715 * square))
    return v * half, slope


def mm(a, b, dims):
    return lax.dot_general(a, b, (dims, ((), ())), preferred_element_type=f32)


NN = ((1,), (0,))
NT = ((1,), (1,))
TN = ((0,), (0,))


def column_sum(v):
    return jnp.sum(v, axis=0, keepdims=True)


def bits(n):
    out = []
    while n > 1:
        n //= 2
        out.append(n)
    return out


class Net:
    def __init__(self, chips, Z, sems):
        self.chips, self.Z, self.C = chips, Z, 2 * chips
        self.c = lax.axis_index("ctx")
        self.z = lax.axis_index("fsdp")
        self.sems, self.used = sems, 0
        block = self.z * self.C + self.c
        self.home = (block // Z, block % Z)
        mine = self.c * Z + self.z
        self.origin = (mine % self.C, mine // self.C)
        self.at_home = block == mine

    def take(self, count):
        self.used += count
        return self.used - count

    def barrier(self):
        sem = pltpu.get_barrier_semaphore()
        peers = [(self.c ^ d, self.z) for d in range(1, self.C)]
        peers += [(self.c, self.z ^ d) for d in range(1, self.Z)]
        for peer in peers:
            pl.semaphore_signal(sem, inc=1, device_id=peer, device_id_type=MESH)

        @pl.when(jnp.logical_not(self.at_home))
        def _():
            for peer in (self.home, self.origin):
                pl.semaphore_signal(sem, inc=1, device_id=peer, device_id_type=MESH)

        pl.semaphore_wait(sem, len(peers) + jnp.where(self.at_home, 0, 2))

    def to(self, device, src, dst, out, into):
        return pltpu.make_async_remote_copy(
            src, dst, self.sems.at[0, out], self.sems.at[1, into],
            device_id=device, device_id_type=MESH,
        )

    def to_ctx(self, d, src, dst, i):
        return self.to((self.c ^ d, self.z), src, dst, i, i)

    def to_z(self, d, src, dst, i):
        return self.to((self.c, self.z ^ d), src, dst, i, i)


class ZGather:
    def __init__(self, net, dst):
        self.net, self.dst = net, dst
        self.base = net.take(net.Z)
        self.copies, self.got = {}, {0}

    def send(self, e, d):
        part = self.dst.at[self.net.z ^ e]
        copy = self.net.to_z(d, part, part, self.base + (e ^ d))
        copy.start()
        self.copies[e ^ d] = copy

    def begin(self):
        for d in bits(self.net.Z):
            self.send(0, d)

    def receive(self, e):
        if e not in self.got:
            self.copies[e].wait_recv()
            self.got.add(e)

    def relay(self):
        held = [0]
        for d in bits(self.net.Z):
            for e in held[1:]:
                self.receive(e)
                self.send(e, d)
            held = held + [e ^ d for e in held]

    def wait(self):
        for e in range(self.net.Z):
            self.receive(e)

    def finish(self):
        for copy in self.copies.values():
            copy.wait_send()


class ZReduce:
    def __init__(self, net, shard, recv, sums):
        self.net, self.shard, self.recv, self.sums = net, shard, recv, sums
        self.base = net.take(net.Z)
        self.terms = {e: [shard(net.z ^ e)] for e in range(net.Z)}
        self.copies, self.slot, self.full = [], 0, 0
        self.stages = bits(net.Z)[::-1]
        self.pending = {}

    def load(self, e):
        if e in self.pending:
            for copy in self.pending.pop(e):
                copy.wait_recv()
        total = None
        for ref in self.terms[e]:
            v = ref[...].astype(f32)
            total = v if total is None else total + v
        return total

    def stage(self, d):
        go = [e for e in sorted(self.terms) if e & d]
        for e in go:
            ref = self.terms[e][0]
            if len(self.terms[e]) > 1:
                total = self.load(e)
                ref = self.sums.at[self.full]
                self.full += 1
                ref[...] = total.astype(bf16)
            del self.terms[e]
            keep = e ^ d
            into = self.recv.at[self.slot]
            copy = self.net.to_z(d, ref, into, self.base + self.slot)
            copy.start()
            self.slot += 1
            self.copies.append(copy)
            self.pending.setdefault(keep, []).append(copy)
            self.terms[keep].append(into)

    def begin(self):
        self.stage(self.stages[0])

    def relay(self):
        for d in self.stages[1:]:
            self.stage(d)

    def total(self):
        return self.load(0)

    def finish(self):
        for copy in self.copies:
            copy.wait_send()


class Gather:
    def __init__(self, net, src, place, rows):
        self.net, self.src, self.place, self.rows = net, src, place, rows
        self.base = net.take(13 if net.chips == 4 else net.C)
        self.sent = []

    def copy(self, d, src, dst, i):
        copy = self.net.to_ctx(d, src, dst, self.base + i)
        copy.start()
        self.sent.append(copy)
        return copy

    def own(self, d, rows, i):
        return self.copy(d, self.src(rows), self.place(self.net.c, rows), i)

    def relay(self, d, rows, target, i):
        part = self.place(self.net.c ^ d, rows)
        return self.copy(target, part, part, i)

    def begin(self):
        every = pl.ds(0, self.rows)
        if self.net.chips == 4:
            half = self.rows // 2
            self.lo, self.hi = pl.ds(0, half), pl.ds(half, half)
            self.x_lo = self.own(2, self.lo, 0)
            self.y_hi = self.own(4, self.hi, 1)
            self.x_hi = self.own(2, self.hi, 2)
            self.y_lo = self.own(4, self.lo, 3)
            self.beside = self.own(1, every, 4)
        else:
            self.far = {d: self.own(2 * d, every, 2 * d) for d in range(self.net.chips - 1, 0, -1)}
            self.beside = self.own(1, every, 1)

    def middle(self):
        if self.net.chips == 4:
            self.x_lo.wait_recv()
            self.r_lo = self.relay(2, self.lo, 4, 5)
            self.s0 = self.relay(2, self.lo, 1, 6)
            self.y_hi.wait_recv()
            self.r_hi = self.relay(4, self.hi, 2, 7)
            self.s1 = self.relay(4, self.hi, 1, 8)

    def finish(self, ready=None):
        ready = ready or (lambda d: None)
        self.beside.wait_recv()
        ready(1)
        if self.net.chips == 4:
            self.x_hi.wait_recv()
            s2 = self.relay(2, self.hi, 1, 9)
            ready(2)
            self.y_lo.wait_recv()
            s3 = self.relay(4, self.lo, 1, 10)
            ready(4)
            self.r_lo.wait_recv()
            s4 = self.relay(6, self.lo, 1, 11)
            self.r_hi.wait_recv()
            s5 = self.relay(6, self.hi, 1, 12)
            ready(6)
            self.s0.wait_recv()
            s2.wait_recv()
            ready(3)
            self.s1.wait_recv()
            s3.wait_recv()
            ready(5)
            s4.wait_recv()
            s5.wait_recv()
            ready(7)
        else:
            on, every = {}, pl.ds(0, self.rows)
            for d, copy in self.far.items():
                copy.wait_recv()
                on[d] = self.relay(2 * d, every, 1, 2 * d + 1)
                ready(2 * d)
            for d, copy in on.items():
                copy.wait_recv()
                ready(2 * d + 1)
        for copy in self.sent:
            copy.wait_send()


class Reduce:
    def __init__(self, net, sib_send, sib_recv, far_send, far_recv, keep):
        self.net = net
        self.base = net.take(2 * net.chips)
        self.sib_send, self.sib_recv = sib_send, sib_recv
        self.far_send, self.far_recv, self.keep = far_send, far_recv, keep
        self.sib, self.far = {}, {}

    def pass_on(self, d):
        self.sib[d].wait_recv()
        total = self.keep[d] + self.sib_recv[d].astype(f32)
        self.far_send[d] = total.astype(bf16)
        self.far[d] = self.net.to_ctx(
            2 * d, self.far_send.at[d], self.far_recv.at[d], self.base + self.net.chips + d
        )
        self.far[d].start()

    def begin(self, partial):
        net = self.net
        core, chip = net.c % 2, net.c // 2
        last = None
        for d in range(net.chips - 1, -1, -1):
            terms = partial(chip ^ d)
            rows = terms.shape[0] // 2
            low, high = terms[:rows], terms[rows:]
            self.sib_send[d] = jnp.where(core == 0, high, low).astype(bf16)
            self.sib[d] = net.to_ctx(1, self.sib_send.at[d], self.sib_recv.at[d], self.base + d)
            self.sib[d].start()
            self.keep[d] = jnp.where(core == 0, low, high)
            if last is not None:
                self.pass_on(last)
            last = d

    def finish(self):
        self.sib[0].wait_recv()
        total = self.keep[0] + self.sib_recv[0].astype(f32)
        for d in range(self.net.chips - 1, 0, -1):
            self.far[d].wait_recv()
            total = total + self.far_recv[d].astype(f32)
        for copy in list(self.sib.values()) + list(self.far.values()):
            copy.wait_send()
        return total


class Swap:
    def __init__(self, net, parts, dst):
        self.net, self.parts, self.dst = net, parts, dst
        self.base = net.take(net.C)

    def start(self):
        net = self.net
        self.copies = [
            net.to_ctx(d, self.parts.at[net.c ^ d], self.dst.at[net.c], self.base + d)
            for d in range(net.C - 1, 0, -1)
        ]
        for copy in self.copies:
            copy.start()
        self.dst[net.c] = self.parts[net.c]

    def wait(self):
        for copy in self.copies:
            copy.wait()


class Spread:
    def __init__(self, net, dst, plane):
        self.net, self.dst, self.plane = net, dst, plane
        self.base = net.take(net.C if plane else net.Z)

    def start(self):
        net = self.net
        part = self.dst.at[net.c if self.plane else net.z]
        send = net.to_ctx if self.plane else net.to_z
        count = net.C if self.plane else net.Z
        self.copies = [send(d, part, part, self.base + d) for d in range(count - 1, 0, -1)]
        for copy in self.copies:
            copy.start()

    def wait(self):
        for copy in self.copies:
            copy.wait()


class Vectors:
    names = ("gain1", "shift1", "qv", "out", "gain2", "shift2", "up", "down")

    def __init__(self, ref, Z, sizes):
        self.ref, self.Z, self.at = ref, Z, {}
        start = 0
        for name, size in zip(self.names, sizes):
            self.at[name] = (start, size)
            start += size

    def get(self, name):
        start, size = self.at[name]
        return jnp.concatenate(
            [self.ref[z, :, start : start + size] for z in range(self.Z)], axis=1
        )


def chosen(pieces, index):
    out = jnp.zeros_like(pieces[0])
    for i, piece in enumerate(pieces):
        out = jnp.where(index == i, piece, out)
    return out


def layer_kernel(names, chips, Z, sizes, aligned, *refs):
    ref = SimpleNamespace(**dict(zip(names, refs)))
    net = Net(chips, Z, ref.sems)
    local = ref.local
    c, z, C = net.c, net.z, net.C
    x_in, cot_in = ref.x_in, ref.cot_in
    R, D = x_in.shape
    S = R * C
    hw = ref.mix.shape[2]
    heads = hw // HEAD_DIM
    fw = ref.hid.shape[1]
    fzc = fw // Z
    r = D // (C * Z)
    step = 2 * R
    xs, n1, n2, cot = (ref.xs, ref.n1, ref.n2, ref.cot)
    bg = xs
    qkv, mix, lse = ref.qkv, ref.mix, ref.lse

    started = []

    def bring(src, dst, i):
        copy = pltpu.make_async_copy(src, dst, local.at[i])
        copy.start()
        return copy

    load_vec = [bring(ref.vec_in, ref.vec.at[z], 0)]
    load_x = bring(x_in, xs.at[c], 1)
    if aligned:
        load_q = [
            bring(
                ref.wqkv_in.at[:, pl.ds(pl.multiple_of(p * D + c * hw, hw), hw)],
                ref.wqkv.at[z, :, p * hw : (p + 1) * hw], 2 + p,
            )
            for p in range(3)
        ]
        FZ = fzc * C
        load_u = [
            bring(
                ref.wup_in.at[:, pl.ds(pl.multiple_of(p * FZ + c * fzc, fzc), fzc)],
                ref.wup.at[z, :, p * fzc : (p + 1) * fzc], 8 + p,
            )
            for p in range(Z)
        ]
    else:
        load_q = [bring(ref.wqkv_in, ref.wqkv.at[z], 2)]
        load_u = [bring(ref.wup_in, ref.wup.at[z], 8)]
    load_o = bring(ref.wout_in.at[pl.ds(pl.multiple_of(c * r, r), r)], ref.wout_parts.at[z], 5)
    load_d = bring(ref.wdown_in.at[pl.ds(pl.multiple_of(c * fzc, fzc), fzc)], ref.wdown.at[z], 6)
    load_c = bring(cot_in, cot.at[c], 7)

    zv, zq = ZGather(net, ref.vec), ZGather(net, ref.wqkv)
    zo, zu = ZGather(net, ref.wout_parts), ZGather(net, ref.wup)
    zd = ZGather(net, ref.wdown)
    net.barrier()
    load_vec[0].wait()
    zv.begin()

    def tokens(src, dst):
        return Gather(net, lambda rows: src.at[rows], lambda i, rows: dst.at[i, rows], R)

    gx = tokens(x_in, xs)
    gx.begin()
    for copy in load_q:
        copy.wait()
    zq.begin()

    pos = lax.broadcasted_iota(jnp.int32, (S, 1), 0)
    first = jnp.zeros((S, 1), jnp.int32)
    end = jnp.int32(0)
    for i in range(ref.docs.shape[1]):
        end = end + ref.docs[0, i]
        first = jnp.where(pos >= end, end, first)
    ref.first[...] = first

    zv.relay()
    zv.wait()
    vectors = Vectors(ref.vec, Z, sizes)
    gain1, shift1 = vectors.get("gain1"), vectors.get("shift1")
    load_x.wait()

    def norm_one(d):
        block = c ^ d
        xhat, _ = row_stats(xs[block].astype(f32))
        n1[block] = (xhat * gain1 + shift1).astype(bf16)

    norm_one(0)
    gx.middle()
    zq.relay()
    load_o.wait()
    zo.begin()
    for copy in load_u:
        copy.wait()
    zu.begin()
    load_c.wait()
    gc = tokens(cot_in, cot)
    gc.begin()
    gx.finish(norm_one)

    qv = vectors.get("qv")
    bias = jnp.concatenate(
        [
            chosen([qv[:, i * hw : (i + 1) * hw] for i in range(C)], c),
            jnp.zeros((1, hw), f32),
            chosen([qv[:, D + i * hw : D + (i + 1) * hw] for i in range(C)], c),
        ],
        axis=1,
    )
    gc.middle()
    zq.wait()
    w_qkv = ref.wqkv[...].reshape(D, 3 * hw)

    def blocks(array, i):
        return array[pl.ds(2 * i, 2)].reshape(step, D)

    def tile(i):
        return pl.ds(pl.multiple_of(i * step, step), step)

    def project(i, carry):
        qkv[tile(i), :] = (mm(blocks(n1, i), w_qkv, NN) + bias).astype(bf16)
        return carry

    lax.fori_loop(0, S // step, project, 0)
    zo.relay()
    gc.finish()
    tiles = S // step

    def masked(i):
        n = (i + 1) * step
        row = lax.broadcasted_iota(jnp.int32, (step, n), 0) + i * step
        col = lax.broadcasted_iota(jnp.int32, (step, n), 1)
        return (col <= row) & (col >= ref.first[i * step : n, :])

    def head(part, h, rows):
        at = part * hw + h * HEAD_DIM
        return qkv[rows, at : at + HEAD_DIM]

    def beside(parts):
        return jnp.concatenate(parts, axis=1) if len(parts) > 1 else parts[0]

    parts_o, wo = ref.wout_parts, ref.wo
    wg = Gather(net, lambda rows: parts_o.at[:, rows], lambda i, rows: wo.at[:, i, rows], r)

    def put(array, i, value):
        array[2 * i], array[2 * i + 1] = value[:R], value[R:]

    for i in range(tiles):
        if i == tiles - 2:
            zo.wait()
            wg.begin()
            load_d.wait()
            zd.begin()
        n = (i + 1) * step
        rows, keys = slice(i * step, n), slice(0, n)
        allowed = masked(i)
        parts = []
        for h in range(heads):
            s = mm(head(0, h, rows), head(1, h, keys), NT) * score_scale
            s = jnp.where(allowed, s, masked_score)
            top = jnp.max(s, axis=1, keepdims=True)
            e = jnp.exp(s - top)
            total = jnp.sum(e, axis=1, keepdims=True)
            parts.append((mm(e.astype(bf16), head(2, h, keys), NN) / total).astype(bf16))
            lse[h, rows, :] = top + jnp.log(total)
        put(mix, i, beside(parts))
    swap_mix = Swap(net, mix, ref.mixf)
    swap_mix.start()
    wg.middle()
    wo[:, c] = parts_o[...]
    zu.relay()
    swap_mix.wait()
    wg.finish()
    w_out = wo[...].reshape(D, D)
    mixed = jnp.concatenate([ref.mixf[i] for i in range(C)], axis=1)
    x_own = xs[c]
    ref.x_own[...] = x_own
    resid = x_own.astype(f32) + mm(mixed, w_out, NN) + vectors.get("out")
    xhat2, scale2 = row_stats(resid)
    gain2 = vectors.get("gain2")
    n2[c] = (xhat2 * gain2 + vectors.get("shift2")).astype(bf16)
    ref.resid[...] = resid
    gn = tokens(n2.at[c], n2)
    gn.begin()
    gn.middle()
    zd.relay()
    zu.wait()
    w_up = ref.wup[...].reshape(D, fw)
    up = vectors.get("up")
    b_up = jnp.concatenate(
        [
            chosen([up[:, (q * C + i) * fzc : (q * C + i + 1) * fzc] for i in range(C)], c)
            for q in range(Z)
        ],
        axis=1,
    )
    gn.finish()
    hid, pg, slopes = ref.hid, ref.pg, ref.slopes

    def feed(i, carry):
        rows = tile(i)
        value, slope = gelu_both(mm(blocks(n2, i), w_up, NN) + b_up)
        hid[rows, :] = value.astype(bf16)
        slopes[rows, :] = slope
        return carry

    lax.fori_loop(0, tiles, feed, 0)

    lanes = 128

    def whole(array):
        return array[...].reshape(S, D)

    def chunk(i):
        return pl.ds(pl.multiple_of(i * lanes, lanes), lanes)

    dbuf, ubuf, obuf, qbuf = (ref.dbuf, ref.ubuf, ref.obuf, ref.qbuf)

    def down_part(i, carry):
        dbuf[chunk(i), :] = mm(hid[:, chunk(i)], whole(cot), TN).astype(bf16)
        return carry

    lax.fori_loop(0, fw // lanes, down_part, 0)
    zd.wait()
    rd = ZReduce(
        net, lambda zs: dbuf.at[pl.ds(pl.multiple_of(zs * fzc, fzc), fzc)], ref.drecv, ref.dsum
    )
    rd.begin()
    w_down = ref.wdown[...].reshape(fw, D)

    up_sums = []

    def feed_back(chip):
        rows = tile(chip)
        grad = (mm(blocks(cot, chip), w_down, NT) * slopes[rows, :]).astype(bf16)
        pg[rows, :] = grad
        up_sums.append(column_sum(grad.astype(f32)))
        return mm(grad, w_up, NT)

    sib_recv, far_recv = ref.sib_recv, ref.far_recv
    red = Reduce(net, ref.sib_send, sib_recv.at[0], ref.far_send, far_recv.at[0], ref.keep)
    red.begin(feed_back)
    up_sums = sum(up_sums)
    per = lanes // (Z * r)

    def up_part(i, carry):
        grad = mm(n2[:, :, chunk(i)].reshape(S, lanes), pg[...], TN).astype(bf16)
        ubuf[pl.ds(i * per, per)] = grad.reshape(per, Z, r, fw)
        return carry

    lax.fori_loop(0, D // lanes, up_part, 0)
    ru = ZReduce(net, lambda zs: ubuf.at[:, zs], ref.urecv, ref.usum)
    ru.begin()

    n2_grad = red.finish()
    cot_own = cot[c].astype(f32)
    xhat2, scale2 = row_stats(ref.resid[...])
    resid_grad = cot_own + norm_back(n2_grad, xhat2, scale2, gain2)
    branch = resid_grad.astype(bf16)
    bg[c] = branch
    ref.rgrad[...] = resid_grad
    back = mm(branch, w_out, NT).astype(bf16)
    mg = ref.mg
    for i in range(C):
        ref.mixf[i] = back[:, i * hw : (i + 1) * hw]
    swap_mg = Swap(net, ref.mixf, mg)
    swap_mg.start()
    gb = tokens(bg.at[c], bg)
    gb.begin()
    sums = {
        "out": column_sum(branch.astype(f32)),
        "gain2": column_sum(n2_grad * xhat2),
        "shift2": column_sum(n2_grad),
        "down": column_sum(cot_own),
    }
    swap_mg.wait()
    qg, dkv = ref.qg, ref.dkv
    dkv[...] = jnp.zeros((S, 2 * hw), f32)
    swap_up = Swap(net, ref.uparts, ref.ufrom)
    for i in range(tiles):
        n = (i + 1) * step
        rows, keys = slice(i * step, n), slice(0, n)
        if i == 1:
            gb.middle()
        if i == tiles - 1:
            rd.relay()
            ru.relay()
        allowed = masked(i)
        g_rows = mg[2 * i : 2 * i + 2].reshape(step, hw)
        m_rows = mix[2 * i : 2 * i + 2].reshape(step, hw)
        dqs, dks, dvs = [], [], []
        for h in range(heads):
            at = h * HEAD_DIM
            q, k, v = head(0, h, rows), head(1, h, keys), head(2, h, keys)
            g, m = g_rows[:, at : at + HEAD_DIM], m_rows[:, at : at + HEAD_DIM]
            s = mm(q, k, NT) * score_scale - lse[h, rows, :]
            p = jnp.where(allowed, jnp.exp(s), 0.0)
            delta = jnp.sum(g.astype(f32) * m.astype(f32), axis=1, keepdims=True)
            ds = (p * (mm(g, v, NT) - delta)).astype(bf16)
            dqs.append(score_scale * mm(ds, k, NN))
            dks.append(score_scale * mm(ds, q, TN))
            dvs.append(mm(p.astype(bf16), g, TN))
        qg[rows, 0:hw] = beside(dqs).astype(bf16)
        dkv[keys, :] += beside(dks + dvs)
    qg[:, hw : 3 * hw] = dkv[...].astype(bf16)

    def qkv_part(i, carry):
        grad = mm(n1[:, :, chunk(i)].reshape(S, lanes), qg[...], TN).astype(bf16)
        qbuf[pl.ds(i * per, per)] = grad.reshape(per, Z, r, 3 * hw)
        return carry

    lax.fori_loop(0, D // lanes, qkv_part, 0)
    rq = ZReduce(net, lambda zs: qbuf.at[:, zs], ref.qrecv, ref.qsum)
    rq.begin()
    red = Reduce(net, ref.sib_send, sib_recv.at[1], ref.far_send, far_recv.at[1], ref.keep)
    red.begin(lambda chip: mm(qg[tile(chip), :], w_qkv, NT))
    gb.finish()
    obuf[...] = mm(mix[...].reshape(S, hw), whole(bg), TN).astype(bf16)
    ro = ZReduce(
        net, lambda zs: obuf.at[pl.ds(pl.multiple_of(zs * r, r), r)], ref.orecv, ref.osum
    )
    ro.begin()
    qkv_sums = column_sum(qg[...].astype(f32))
    colz, colp = ref.colz, ref.colp
    colz[z] = jnp.concatenate([qkv_sums[:, 0:hw], qkv_sums[:, 2 * hw : 3 * hw], up_sums], axis=1)
    line = Spread(net, colz, False)
    line.start()

    n1_grad = red.finish()
    red_out = Reduce(net, ref.sib_send, sib_recv.at[0], ref.far_send, far_recv.at[0], ref.keep)
    red_out.begin(lambda chip: mm(hid[tile(chip), :], w_down, NN))
    xhat1, scale1 = row_stats(ref.x_own[...].astype(f32))
    ref.input_grad[...] = (ref.rgrad[...] + norm_back(n1_grad, xhat1, scale1, gain1)).astype(bf16)
    stack = jnp.concatenate(
        [
            column_sum(n1_grad * xhat1), column_sum(n1_grad), sums["out"], sums["gain2"],
            sums["shift2"], sums["down"], jnp.zeros((2, D), f32),
        ],
        axis=0,
    )
    w = D // C
    for i in range(C):
        ref.tok_to[i] = stack[:, i * w : (i + 1) * w]
    swap_tok = Swap(net, ref.tok_to, ref.tok_from)
    swap_tok.start()
    rq.relay()
    ro.relay()

    ref.dparts[...] = rd.total().astype(bf16)
    home = net.take(1)
    there = net.to(net.home, ref.dparts, ref.dfrom, home, home)
    here = pltpu.make_async_copy(ref.dparts, ref.dfrom, local.at[0])

    @pl.when(net.at_home)
    def _():
        here.start()

    @pl.when(jnp.logical_not(net.at_home))
    def _():
        there.start()

    ref.uparts[...] = ru.total().astype(bf16)
    swap_up.start()
    line.wait()
    total = colz[0]
    for i in range(1, Z):
        total = total + colz[i]
    colp[c] = total
    plane = Spread(net, colp, True)
    plane.start()
    swap_tok.wait()
    tokz = ref.tokz
    total = ref.tok_from[0]
    for i in range(1, C):
        total = total + ref.tok_from[i]
    tokz[z] = total
    tok_line = Spread(net, tokz, False)
    tok_line.start()

    @pl.when(net.at_home)
    def _():
        here.wait()

    @pl.when(jnp.logical_not(net.at_home))
    def _():
        there.wait()

    ref.d_down[...] = ref.dfrom[...].astype(f32)
    swap_up.wait()
    for i in range(C):
        for q in range(Z):
            ref.d_up[:, (q * C + i) * fzc : (q * C + i + 1) * fzc] = ref.ufrom[
                i, :, q * fzc : (q + 1) * fzc
            ].astype(f32)
    ref.qparts[...] = rq.total().astype(bf16)
    swap_q = Swap(net, ref.qparts, ref.qfrom)
    swap_q.start()
    ref.d_out[...] = ro.total()
    tok_line.wait()
    total = tokz[0]
    for i in range(1, Z):
        total = total + tokz[i]
    ref.tok[...] = chosen([total[:, i * r : (i + 1) * r] for i in range(Z)], z)
    total = red_out.finish()
    ref.layer_out[...] = (ref.resid[...] + total + vectors.get("down")).astype(bf16)
    plane.wait()
    mine = c * Z + z
    part = D * 2 // (C * Z)

    def piece(at, size):
        rest, row = at % hw, (at % D) // hw
        start = hw * (at // D) + rest
        return colp[row, :, start : start + size]

    ref.qv[...] = chosen([piece(i * part, part) for i in range(C * Z)], mine)
    ref.up[...] = chosen(
        [
            colp[i, :, 2 * hw + q * fzc : 2 * hw + (q + 1) * fzc]
            for q in range(Z)
            for i in range(C)
        ],
        mine,
    )
    swap_q.wait()
    for i in range(C):
        for p in range(3):
            ref.d_qkv[:, p * D + i * hw : p * D + (i + 1) * hw] = ref.qfrom[
                i, :, p * hw : (p + 1) * hw
            ].astype(f32)
    assert net.used <= ref.sems.shape[1]
    for part in (zv, zq, zo, zu, zd, rd, ru, ro, rq):
        part.finish()


def hand_over(count, *refs):
    big, (tok, qv, up) = refs[:count], refs[count : count + 3]
    rest, sems = refs[count + 3 :], refs[-1]
    outs, held = rest[: count + 8], rest[count + 8 : -1]
    into = [pltpu.make_async_copy(big[i], held[i], sems.at[0, i]) for i in range(count)]
    out = [pltpu.make_async_copy(held[i], outs[i], sems.at[1, i]) for i in range(count)]
    for copy in into:
        copy.start()
    for i in range(6):
        outs[count + i][...] = tok[i : i + 1, :]
    outs[count + 6][...] = qv[...]
    outs[count + 7][...] = up[...]
    for i in range(count):
        into[i].wait()
        out[i].start()
    for copy in out:
        copy.wait()


def shards(
    tokens_in,
    doc_lengths,
    norm1_gain,
    norm1_bias,
    qkv_weight,
    qv_bias,
    out_weight,
    out_bias,
    norm2_gain,
    norm2_bias,
    up_weight,
    up_bias,
    down_weight,
    down_bias,
    out_cotangent,
):
    C, Z = lax.axis_size("ctx"), lax.axis_size("fsdp")
    c, z = lax.axis_index("ctx"), lax.axis_index("fsdp")
    R, D = tokens_in.shape[1:]
    chips, S, hw = C // 2, R * C, D // C
    ff = up_weight.shape[1]
    fw, fzc, r = ff // C, ff // (C * Z), D // (C * Z)
    heads = hw // HEAD_DIM
    all_vectors = (
        norm1_gain, norm1_bias, qv_bias, out_bias, norm2_gain, norm2_bias, up_bias, down_bias
    )
    sizes = tuple(v.shape[0] for v in all_vectors)
    V, W = sum(sizes), 2 * hw + fw
    vec_in, at = jnp.zeros((V,), f32), 0
    for v in all_vectors:
        vec_in = vec_in + jnp.pad(v.astype(f32), (at, V - at - v.shape[0]))
        at += v.shape[0]
    vec_in = vec_in[None]
    aligned = hw % 128 == 0 and fzc % 128 == 0
    wqkv_in, wup_in = qkv_weight, up_weight
    if not aligned:
        wqkv_in = lax.dynamic_index_in_dim(
            qkv_weight.reshape(D // Z, 3, C, hw), c, axis=2, keepdims=False
        ).reshape(D // Z, 3 * hw)
        wup_in = lax.dynamic_index_in_dim(
            up_weight.reshape(D // Z, Z, C, fzc), c, axis=2, keepdims=False
        ).reshape(D // Z, fw)

    vmem, hbm = pltpu.VMEM, pl.BlockSpec(memory_space=pl.ANY)
    ins = dict(
        x_in=(tokens_in[0], hbm),
        cot_in=(out_cotangent[0], hbm),
        docs=(doc_lengths, pl.BlockSpec(memory_space=pltpu.SMEM)),
        vec_in=(vec_in, hbm),
        wqkv_in=(wqkv_in, hbm),
        wout_in=(out_weight, hbm),
        wup_in=(wup_in, hbm),
        wdown_in=(down_weight, hbm),
    )
    outs = dict(
        layer_out=((R, D), bf16),
        input_grad=((R, D), bf16),
        d_qkv=((r, 3 * D), f32),
        d_out=((r, D), f32),
        d_up=((r, ff), f32),
        d_down=((fzc, D), f32),
        tok=((8, r), f32),
        qv=((1, 2 * r), f32),
        up=((1, fzc), f32),
    )
    token, own = (C, R, D), (R, D)
    scratch = dict(
        xs=(token, bf16),
        n1=(token, bf16),
        n2=(token, bf16),
        cot=(token, bf16),
        qkv=((S, 3 * hw), bf16),
        qg=((S, 3 * hw), bf16),
        mix=((C, R, hw), bf16),
        mixf=((C, R, hw), bf16),
        mg=((C, R, hw), bf16),
        slopes=((S, fw), f32),
        wo=((Z, C, r, D), bf16),
        lse=((heads, S, 1), f32),
        dkv=((S, 2 * hw), f32),
        hid=((S, fw), bf16),
        pg=((S, fw), bf16),
        x_own=(own, bf16),
        resid=(own, f32),
        rgrad=(own, f32),
        vec=((Z, 1, V), f32),
        wqkv=((Z, D // Z, 3 * hw), bf16),
        wout_parts=((Z, r, D), bf16),
        wup=((Z, D // Z, fw), bf16),
        wdown=((Z, fzc, D), bf16),
        first=((S, 1), jnp.int32),
        sib_send=((chips, R, D), bf16),
        far_send=((chips, R, D), bf16),
        keep=((chips, R, D), f32),
        sib_recv=((2, chips, R, D), bf16),
        far_recv=((2, chips, R, D), bf16),
        dbuf=((fw, D), bf16),
        ubuf=((C, Z, r, fw), bf16),
        obuf=((hw, D), bf16),
        qbuf=((C, Z, r, 3 * hw), bf16),
        colz=((Z, 1, W), f32),
        tok_to=((C, 8, D // C), f32),
        tok_from=((C, 8, D // C), f32),
        colp=((C, 1, W), f32),
        tokz=((Z, 8, D // C), f32),
    )
    shard = dict(d=(fzc, D), u=(C, r, fw), o=(r, D), q=(C, r, 3 * hw))
    for k, shape in shard.items():
        scratch[k + "recv"] = ((Z - 1, *shape), bf16)
        scratch[k + "sum"] = ((Z // 2, *shape), bf16)
        if k != "o":
            scratch[k + "parts"] = (shape, bf16)
            scratch[k + "from"] = (shape, bf16)
    gathers = 5 * max(13, C)
    count = gathers + 12 * Z + 6 * chips + 6 * C + 2
    names = (*ins, *outs, *scratch, "sems", "local")
    got = pl.pallas_call(
        functools.partial(layer_kernel, names, chips, Z, sizes, aligned),
        out_shape=[jax.ShapeDtypeStruct(*v) for v in outs.values()],
        in_specs=[v[1] for v in ins.values()],
        out_specs=[pl.BlockSpec(memory_space=vmem)] * len(outs),
        scratch_shapes=[vmem(*v) for v in scratch.values()]
        + [pltpu.SemaphoreType.DMA((2, count)), pltpu.SemaphoreType.DMA((8 + Z,))],
        compiler_params=pltpu.CompilerParams(
            collective_id=1, has_side_effects=True, vmem_limit_bytes=63 << 20
        ),
        name="layer",
    )(*[v[0] for v in ins.values()])
    big = 6
    results = list(outs.values())[:big] + [((1, r), f32)] * 6 + [outs[k] for k in list(outs)[-2:]]
    done = pl.pallas_call(
        functools.partial(hand_over, big),
        out_shape=[jax.ShapeDtypeStruct(*v) for v in results],
        in_specs=[hbm] * big + [pl.BlockSpec(memory_space=vmem)] * 3,
        out_specs=[hbm] * big + [pl.BlockSpec(memory_space=vmem)] * 8,
        scratch_shapes=[vmem(*v) for v in results[:big]] + [pltpu.SemaphoreType.DMA((2, big))],
        name="hand_over",
    )(*got)
    layer_out, input_grad, d_qkv, d_out, d_up, d_down = done[:big]
    gain1, shift1, out, gain2, shift2, down, qv, up = (v.reshape(-1) for v in done[big:])
    return (
        layer_out[None], input_grad[None], gain1, shift1, d_qkv, qv, d_out, out,
        gain2, shift2, d_up, up, d_down, down,
    )


def solution(mesh):
    token = P("fsdp", "ctx", None)
    flat, table = P("fsdp"), P("fsdp", None)
    home, home2 = P(("ctx", "fsdp")), P(("ctx", "fsdp"), None)
    return jax.shard_map(
        shards,
        mesh=mesh,
        in_specs=(
            token, table, flat, flat, table, flat, table, flat,
            flat, flat, table, flat, table, flat, token,
        ),
        out_specs=(
            token, token, home, home, home2, home, home2, home,
            home, home, home2, home, home2, home,
        ),
        check_vma=False,
    )
```

```python
import functools
from types import SimpleNamespace

import jax
import jax.numpy as jnp
from jax import lax
from jax.experimental import pallas as pl
from jax.experimental.pallas import tpu as pltpu
from jax.sharding import PartitionSpec as P

HEADS = 16
HEAD_DIM = 64
MESH = pl.DeviceIdType.MESH

epsilon = 1e-05
masked_score = -1e30
score_scale = HEAD_DIM ** (-0.5)
f32 = jnp.float32
bf16 = jnp.bfloat16


def row_stats(values):
    mean = jnp.mean(values, axis=-1, keepdims=True)
    centre = values - mean
    spread = jnp.mean(centre * centre, axis=-1, keepdims=True)
    scale = lax.rsqrt(spread + epsilon)
    return centre * scale, scale


def norm_back(grad, xhat, scale, gain):
    gh = grad * gain
    return scale * (
        gh
        - jnp.mean(gh, axis=-1, keepdims=True)
        - xhat * jnp.mean(gh * xhat, axis=-1, keepdims=True)
    )


def gelu_both(v):
    k = 0.7978845608028654
    square = v * v
    inner = jnp.tanh(k * v * (1.0 + 0.044715 * square))
    half = 0.5 * (1.0 + inner)
    slope = half + 0.5 * v * (1.0 - inner * inner) * (k * (1.0 + 3 * 0.044715 * square))
    return v * half, slope


def mm(a, b, dims):
    return lax.dot_general(a, b, (dims, ((), ())), preferred_element_type=f32)


NN = ((1,), (0,))
NT = ((1,), (1,))
TN = ((0,), (0,))


def column_sum(v):
    return jnp.sum(v, axis=0, keepdims=True)


def bits(n):
    out = []
    while n > 1:
        n //= 2
        out.append(n)
    return out


class Net:
    def __init__(self, chips, Z, sems):
        self.chips, self.Z, self.C = chips, Z, 2 * chips
        self.c = lax.axis_index("ctx")
        self.z = lax.axis_index("fsdp")
        self.sems, self.used = sems, 0
        q = self.z ^ (self.c % Z)
        self.home = q * (self.C // Z) + self.c // Z
        self.at_home = self.home == self.c

    def block(self, q, c):
        return self.Z * (c // self.Z) + (q ^ (c % self.Z))

    def take(self, count):
        self.used += count
        return self.used - count

    def barrier(self):
        sem = pltpu.get_barrier_semaphore()
        peers = [(self.c ^ d, self.z) for d in range(1, self.C)]
        peers += [(self.c, self.z ^ d) for d in range(1, self.Z)]
        for peer in peers:
            pl.semaphore_signal(sem, inc=1, device_id=peer, device_id_type=MESH)

        pl.semaphore_wait(sem, len(peers))

    def to(self, device, src, dst, out, into):
        return pltpu.make_async_remote_copy(
            src, dst, self.sems.at[0, out], self.sems.at[1, into],
            device_id=device, device_id_type=MESH,
        )

    def to_ctx(self, d, src, dst, i):
        return self.to((self.c ^ d, self.z), src, dst, i, i)

    def to_z(self, d, src, dst, i):
        return self.to((self.c, self.z ^ d), src, dst, i, i)


class ZGather:
    def __init__(self, net, dst):
        self.net, self.dst = net, dst
        self.base = net.take(net.Z)
        self.copies, self.got = {}, {0}

    def send(self, e, d):
        part = self.dst.at[self.net.z ^ e]
        copy = self.net.to_z(d, part, part, self.base + (e ^ d))
        copy.start()
        self.copies[e ^ d] = copy

    def begin(self):
        for d in bits(self.net.Z):
            self.send(0, d)

    def receive(self, e):
        if e not in self.got:
            self.copies[e].wait_recv()
            self.got.add(e)

    def relay(self):
        held = [0]
        for d in bits(self.net.Z):
            for e in held[1:]:
                self.receive(e)
                self.send(e, d)
            held = held + [e ^ d for e in held]

    def wait(self):
        for e in range(self.net.Z):
            self.receive(e)

    def finish(self):
        for copy in self.copies.values():
            copy.wait_send()


class ZReduce:
    def __init__(self, net, shard, recv, sums):
        self.net, self.shard, self.recv, self.sums = net, shard, recv, sums
        self.base = net.take(net.Z)
        self.terms = {e: [shard(net.z ^ e)] for e in range(net.Z)}
        self.copies, self.slot, self.full = [], 0, 0
        self.stages = bits(net.Z)[::-1]
        self.pending = {}

    def load(self, e):
        if e in self.pending:
            for copy in self.pending.pop(e):
                copy.wait_recv()
        total = None
        for ref in self.terms[e]:
            v = ref[...].astype(f32)
            total = v if total is None else total + v
        return total

    def stage(self, d):
        go = [e for e in sorted(self.terms) if e & d]
        for e in go:
            ref = self.terms[e][0]
            if len(self.terms[e]) > 1:
                total = self.load(e)
                ref = self.sums.at[self.full]
                self.full += 1
                ref[...] = total.astype(bf16)
            del self.terms[e]
            keep = e ^ d
            into = self.recv.at[self.slot]
            copy = self.net.to_z(d, ref, into, self.base + self.slot)
            copy.start()
            self.slot += 1
            self.copies.append(copy)
            self.pending.setdefault(keep, []).append(copy)
            self.terms[keep].append(into)

    def begin(self):
        self.stage(self.stages[0])

    def relay(self):
        for d in self.stages[1:]:
            self.stage(d)

    def total(self):
        return self.load(0)

    def finish(self):
        for copy in self.copies:
            copy.wait_send()


class Gather:
    def __init__(self, net, src, place, rows):
        self.net, self.src, self.place, self.rows = net, src, place, rows
        self.base = net.take(13 if net.chips == 4 else net.C)
        self.sent = []

    def copy(self, d, src, dst, i):
        copy = self.net.to_ctx(d, src, dst, self.base + i)
        copy.start()
        self.sent.append(copy)
        return copy

    def own(self, d, rows, i):
        return self.copy(d, self.src(rows), self.place(self.net.c, rows), i)

    def relay(self, d, rows, target, i):
        part = self.place(self.net.c ^ d, rows)
        return self.copy(target, part, part, i)

    def begin(self):
        every = pl.ds(0, self.rows)
        if self.net.chips == 4:
            half = self.rows // 2
            self.lo, self.hi = pl.ds(0, half), pl.ds(half, half)
            self.x_lo = self.own(2, self.lo, 0)
            self.y_hi = self.own(4, self.hi, 1)
            self.x_hi = self.own(2, self.hi, 2)
            self.y_lo = self.own(4, self.lo, 3)
            self.beside = self.own(1, every, 4)
        else:
            self.far = {d: self.own(2 * d, every, 2 * d) for d in range(self.net.chips - 1, 0, -1)}
            self.beside = self.own(1, every, 1)

    def middle(self):
        if self.net.chips == 4:
            self.x_lo.wait_recv()
            self.r_lo = self.relay(2, self.lo, 4, 5)
            self.s0 = self.relay(2, self.lo, 1, 6)
            self.y_hi.wait_recv()
            self.r_hi = self.relay(4, self.hi, 2, 7)
            self.s1 = self.relay(4, self.hi, 1, 8)

    def finish(self, ready=None):
        ready = ready or (lambda d: None)
        self.beside.wait_recv()
        ready(1)
        if self.net.chips == 4:
            self.x_hi.wait_recv()
            s2 = self.relay(2, self.hi, 1, 9)
            ready(2)
            self.y_lo.wait_recv()
            s3 = self.relay(4, self.lo, 1, 10)
            ready(4)
            self.r_lo.wait_recv()
            s4 = self.relay(6, self.lo, 1, 11)
            self.r_hi.wait_recv()
            s5 = self.relay(6, self.hi, 1, 12)
            ready(6)
            self.s0.wait_recv()
            s2.wait_recv()
            ready(3)
            self.s1.wait_recv()
            s3.wait_recv()
            ready(5)
            s4.wait_recv()
            s5.wait_recv()
            ready(7)
        else:
            on, every = {}, pl.ds(0, self.rows)
            for d, copy in self.far.items():
                copy.wait_recv()
                on[d] = self.relay(2 * d, every, 1, 2 * d + 1)
                ready(2 * d)
            for d, copy in on.items():
                copy.wait_recv()
                ready(2 * d + 1)
        for copy in self.sent:
            copy.wait_send()


class Reduce:
    def __init__(self, net, sib_send, sib_recv, far_send, far_recv, keep):
        self.net = net
        self.base = net.take(2 * net.chips)
        self.sib_send, self.sib_recv = sib_send, sib_recv
        self.far_send, self.far_recv, self.keep = far_send, far_recv, keep
        self.sib, self.far = {}, {}

    def pass_on(self, d):
        self.sib[d].wait_recv()
        total = self.keep[d] + self.sib_recv[d].astype(f32)
        self.far_send[d] = total.astype(bf16)
        self.far[d] = self.net.to_ctx(
            2 * d, self.far_send.at[d], self.far_recv.at[d], self.base + self.net.chips + d
        )
        self.far[d].start()

    def begin(self, partial):
        net = self.net
        core, chip = net.c % 2, net.c // 2
        last = None
        for d in range(net.chips - 1, -1, -1):
            terms = partial(chip ^ d)
            rows = terms.shape[0] // 2
            low, high = terms[:rows], terms[rows:]
            self.sib_send[d] = jnp.where(core == 0, high, low).astype(bf16)
            self.sib[d] = net.to_ctx(1, self.sib_send.at[d], self.sib_recv.at[d], self.base + d)
            self.sib[d].start()
            self.keep[d] = jnp.where(core == 0, low, high)
            if last is not None:
                self.pass_on(last)
            last = d

    def finish(self):
        self.sib[0].wait_recv()
        total = self.keep[0] + self.sib_recv[0].astype(f32)
        for d in range(self.net.chips - 1, 0, -1):
            self.far[d].wait_recv()
            total = total + self.far_recv[d].astype(f32)
        for copy in list(self.sib.values()) + list(self.far.values()):
            copy.wait_send()
        return total


class Swap:
    def __init__(self, net, parts, dst):
        self.net, self.parts, self.dst = net, parts, dst
        self.base = net.take(net.C)

    def start(self):
        net = self.net
        self.copies = [
            net.to_ctx(d, self.parts.at[net.c ^ d], self.dst.at[net.c], self.base + d)
            for d in range(net.C - 1, 0, -1)
        ]
        for copy in self.copies:
            copy.start()
        self.dst[net.c] = self.parts[net.c]

    def wait(self):
        for copy in self.copies:
            copy.wait()


class Spread:
    def __init__(self, net, dst, plane):
        self.net, self.dst, self.plane = net, dst, plane
        self.base = net.take(net.C if plane else net.Z)

    def start(self):
        net = self.net
        part = self.dst.at[net.c if self.plane else net.z]
        send = net.to_ctx if self.plane else net.to_z
        count = net.C if self.plane else net.Z
        self.copies = [send(d, part, part, self.base + d) for d in range(count - 1, 0, -1)]
        for copy in self.copies:
            copy.start()

    def wait(self):
        for copy in self.copies:
            copy.wait()


class Vectors:
    names = ("gain1", "shift1", "qv", "out", "gain2", "shift2", "up", "down")

    def __init__(self, ref, Z, sizes):
        self.ref, self.Z, self.at = ref, Z, {}
        start = 0
        for name, size in zip(self.names, sizes):
            self.at[name] = (start, size)
            start += size

    def get(self, name):
        start, size = self.at[name]
        return jnp.concatenate(
            [self.ref[z, :, start : start + size] for z in range(self.Z)], axis=1
        )


def chosen(pieces, index):
    out = jnp.zeros_like(pieces[0])
    for i, piece in enumerate(pieces):
        out = jnp.where(index == i, piece, out)
    return out


def layer_kernel(names, chips, Z, sizes, aligned, *refs):
    ref = SimpleNamespace(**dict(zip(names, refs)))
    net = Net(chips, Z, ref.sems)
    local = ref.local
    c, z, C = net.c, net.z, net.C
    x_in, cot_in = ref.x_in, ref.cot_in
    R, D = x_in.shape
    S = R * C
    hw = ref.mix.shape[2]
    heads = hw // HEAD_DIM
    fw = ref.hid.shape[1]
    fzc = fw // Z
    r = D // (C * Z)
    step = 2 * R
    xs, n1, n2, cot = (ref.xs, ref.n1, ref.n2, ref.cot)
    bg = xs
    qkv, mix, lse = ref.qkv, ref.mix, ref.lse

    started = []

    def bring(src, dst, i):
        copy = pltpu.make_async_copy(src, dst, local.at[i])
        copy.start()
        return copy

    load_vec = [bring(ref.vec_in, ref.vec.at[z], 0)]
    load_x = bring(x_in, xs.at[c], 1)
    if aligned:
        load_q = [
            bring(
                ref.wqkv_in.at[:, pl.ds(pl.multiple_of(p * D + c * hw, hw), hw)],
                ref.wqkv.at[z, :, p * hw : (p + 1) * hw], 2 + p,
            )
            for p in range(3)
        ]
        FZ = fzc * C
        load_u = [
            bring(
                ref.wup_in.at[:, pl.ds(pl.multiple_of(p * FZ + net.block(p, c) * fzc, fzc), fzc)],
                ref.wup.at[z, :, p * fzc : (p + 1) * fzc], 8 + p,
            )
            for p in range(Z)
        ]
    else:
        load_q = [bring(ref.wqkv_in, ref.wqkv.at[z], 2)]
        load_u = [bring(ref.wup_in, ref.wup.at[z], 8)]
    load_o = bring(ref.wout_in.at[pl.ds(pl.multiple_of(c * r, r), r)], ref.wout_parts.at[z], 5)
    load_d = bring(ref.wdown_in.at[pl.ds(pl.multiple_of(net.block(z, c) * fzc, fzc), fzc)], ref.wdown.at[z], 6)
    load_c = bring(cot_in, cot.at[c], 7)

    zv, zq = ZGather(net, ref.vec), ZGather(net, ref.wqkv)
    zo, zu = ZGather(net, ref.wout_parts), ZGather(net, ref.wup)
    zd = ZGather(net, ref.wdown)
    net.barrier()
    load_vec[0].wait()
    zv.begin()

    def tokens(src, dst):
        return Gather(net, lambda rows: src.at[rows], lambda i, rows: dst.at[i, rows], R)

    gx = tokens(x_in, xs)
    gx.begin()
    for copy in load_q:
        copy.wait()
    zq.begin()

    pos = lax.broadcasted_iota(jnp.int32, (S, 1), 0)
    first = jnp.zeros((S, 1), jnp.int32)
    end = jnp.int32(0)
    for i in range(ref.docs.shape[1]):
        end = end + ref.docs[0, i]
        first = jnp.where(pos >= end, end, first)
    ref.first[...] = first

    zv.relay()
    zv.wait()
    vectors = Vectors(ref.vec, Z, sizes)
    gain1, shift1 = vectors.get("gain1"), vectors.get("shift1")
    load_x.wait()

    def norm_one(d):
        block = c ^ d
        xhat, _ = row_stats(xs[block].astype(f32))
        n1[block] = (xhat * gain1 + shift1).astype(bf16)

    norm_one(0)
    gx.middle()
    zq.relay()
    load_o.wait()
    zo.begin()
    for copy in load_u:
        copy.wait()
    zu.begin()
    load_c.wait()
    gc = tokens(cot_in, cot)
    gc.begin()
    gx.finish(norm_one)

    qv = vectors.get("qv")
    bias = jnp.concatenate(
        [
            chosen([qv[:, i * hw : (i + 1) * hw] for i in range(C)], c),
            jnp.zeros((1, hw), f32),
            chosen([qv[:, D + i * hw : D + (i + 1) * hw] for i in range(C)], c),
        ],
        axis=1,
    )
    gc.middle()
    zq.wait()
    w_qkv = ref.wqkv[...].reshape(D, 3 * hw)

    def blocks(array, i):
        return array[pl.ds(2 * i, 2)].reshape(step, D)

    def tile(i):
        return pl.ds(pl.multiple_of(i * step, step), step)

    def project(i, carry):
        qkv[tile(i), :] = (mm(blocks(n1, i), w_qkv, NN) + bias).astype(bf16)
        return carry

    lax.fori_loop(0, S // step, project, 0)
    zo.relay()
    gc.finish()
    tiles = S // step

    def masked(i):
        n = (i + 1) * step
        row = lax.broadcasted_iota(jnp.int32, (step, n), 0) + i * step
        col = lax.broadcasted_iota(jnp.int32, (step, n), 1)
        return (col <= row) & (col >= ref.first[i * step : n, :])

    def head(part, h, rows):
        at = part * hw + h * HEAD_DIM
        return qkv[rows, at : at + HEAD_DIM]

    def beside(parts):
        return jnp.concatenate(parts, axis=1) if len(parts) > 1 else parts[0]

    parts_o, wo = ref.wout_parts, ref.wo
    wg = Gather(net, lambda rows: parts_o.at[:, rows], lambda i, rows: wo.at[:, i, rows], r)

    def put(array, i, value):
        array[2 * i], array[2 * i + 1] = value[:R], value[R:]

    for i in range(tiles):
        if i == 1:
            zo.wait()
            wg.begin()
        if i == tiles - 1:
            wg.middle()
            load_d.wait()
            zd.begin()
        n = (i + 1) * step
        rows, keys = slice(i * step, n), slice(0, n)
        allowed = masked(i)
        parts = []
        for h in range(heads):
            s = mm(head(0, h, rows), head(1, h, keys), NT) * score_scale
            s = jnp.where(allowed, s, masked_score)
            top = jnp.max(s, axis=1, keepdims=True)
            e = jnp.exp(s - top)
            total = jnp.sum(e, axis=1, keepdims=True)
            parts.append((mm(e.astype(bf16), head(2, h, keys), NN) / total).astype(bf16))
            lse[h, rows, :] = top + jnp.log(total)
        put(mix, i, beside(parts))
    swap_mix = Swap(net, mix, ref.mixf)
    swap_mix.start()
    wo[:, c] = parts_o[...]
    zu.relay()
    swap_mix.wait()
    wg.finish()
    w_out = wo[...].reshape(D, D)
    mixed = jnp.concatenate([ref.mixf[i] for i in range(C)], axis=1)
    x_own = xs[c]
    ref.x_own[...] = x_own
    resid = x_own.astype(f32) + mm(mixed, w_out, NN) + vectors.get("out")
    xhat2, scale2 = row_stats(resid)
    gain2 = vectors.get("gain2")
    n2[c] = (xhat2 * gain2 + vectors.get("shift2")).astype(bf16)
    ref.resid[...] = resid
    gn = tokens(n2.at[c], n2)
    gn.begin()
    gn.middle()
    zd.relay()
    zu.wait()
    w_up = ref.wup[...].reshape(D, fw)
    up = vectors.get("up")
    b_up = jnp.concatenate(
        [
            chosen(
                [up[:, (q * C + i) * fzc : (q * C + i + 1) * fzc] for i in range(C)],
                net.block(q, c),
            )
            for q in range(Z)
        ],
        axis=1,
    )
    gn.finish()
    hid, pg, slopes = ref.hid, ref.pg, ref.slopes

    def feed(i, carry):
        rows = tile(i)
        value, slope = gelu_both(mm(blocks(n2, i), w_up, NN) + b_up)
        hid[rows, :] = value.astype(bf16)
        slopes[rows, :] = slope
        return carry

    lax.fori_loop(0, tiles, feed, 0)

    lanes = 128

    def whole(array):
        return array[...].reshape(S, D)

    def chunk(i):
        return pl.ds(pl.multiple_of(i * lanes, lanes), lanes)

    dbuf, ubuf, obuf, qbuf = (ref.dbuf, ref.ubuf, ref.obuf, ref.qbuf)

    def down_part(i, carry):
        dbuf[chunk(i), :] = mm(hid[:, chunk(i)], whole(cot), TN).astype(bf16)
        return carry

    lax.fori_loop(0, fw // lanes, down_part, 0)
    zd.wait()
    rd = ZReduce(
        net,
        lambda zs: dbuf.at[pl.ds(pl.multiple_of((zs ^ (c % Z)) * fzc, fzc), fzc)],
        ref.drecv,
        ref.dsum,
    )
    rd.begin()
    w_down = ref.wdown[...].reshape(fw, D)

    up_sums = []

    def feed_back(chip):
        rows = tile(chip)
        grad = (mm(blocks(cot, chip), w_down, NT) * slopes[rows, :]).astype(bf16)
        pg[rows, :] = grad
        up_sums.append(column_sum(grad.astype(f32)))
        return mm(grad, w_up, NT)

    sib_recv, far_recv = ref.sib_recv, ref.far_recv
    red = Reduce(net, ref.sib_send, sib_recv.at[0], ref.far_send, far_recv.at[0], ref.keep)
    red.begin(feed_back)
    up_sums = sum(up_sums)
    per = lanes // (Z * r)

    def up_part(i, carry):
        grad = mm(n2[:, :, chunk(i)].reshape(S, lanes), pg[...], TN).astype(bf16)
        ubuf[pl.ds(i * per, per)] = grad.reshape(per, Z, r, fw)
        return carry

    lax.fori_loop(0, D // lanes, up_part, 0)
    ru = ZReduce(net, lambda zs: ubuf.at[:, zs], ref.urecv, ref.usum)
    ru.begin()

    n2_grad = red.finish()
    cot_own = cot[c].astype(f32)
    xhat2, scale2 = row_stats(ref.resid[...])
    resid_grad = cot_own + norm_back(n2_grad, xhat2, scale2, gain2)
    branch = resid_grad.astype(bf16)
    bg[c] = branch
    ref.rgrad[...] = resid_grad
    back = mm(branch, w_out, NT).astype(bf16)
    mg = ref.mg
    for i in range(C):
        ref.mixf[i] = back[:, i * hw : (i + 1) * hw]
    swap_mg = Swap(net, ref.mixf, mg)
    swap_mg.start()
    gb = tokens(bg.at[c], bg)
    gb.begin()
    sums = {
        "out": column_sum(branch.astype(f32)),
        "gain2": column_sum(n2_grad * xhat2),
        "shift2": column_sum(n2_grad),
        "down": column_sum(cot_own),
    }
    swap_mg.wait()
    rd.relay()
    qg, dkv = ref.qg, ref.dkv
    dkv[...] = jnp.zeros((S, 2 * hw), f32)
    swap_up = Swap(net, ref.uparts, ref.ufrom)
    for i in range(tiles):
        n = (i + 1) * step
        rows, keys = slice(i * step, n), slice(0, n)
        if i == 1:
            gb.middle()
        if i == tiles - 1:
            ru.relay()
        allowed = masked(i)
        g_rows = mg[2 * i : 2 * i + 2].reshape(step, hw)
        m_rows = mix[2 * i : 2 * i + 2].reshape(step, hw)
        dqs, dks, dvs = [], [], []
        for h in range(heads):
            at = h * HEAD_DIM
            q, k, v = head(0, h, rows), head(1, h, keys), head(2, h, keys)
            g, m = g_rows[:, at : at + HEAD_DIM], m_rows[:, at : at + HEAD_DIM]
            s = mm(q, k, NT) * score_scale - lse[h, rows, :]
            p = jnp.where(allowed, jnp.exp(s), 0.0)
            delta = jnp.sum(g.astype(f32) * m.astype(f32), axis=1, keepdims=True)
            ds = (p * (mm(g, v, NT) - delta)).astype(bf16)
            dqs.append(score_scale * mm(ds, k, NN))
            dks.append(score_scale * mm(ds, q, TN))
            dvs.append(mm(p.astype(bf16), g, TN))
        qg[rows, 0:hw] = beside(dqs).astype(bf16)
        dkv[keys, :] += beside(dks + dvs)
    qg[:, hw : 3 * hw] = dkv[...].astype(bf16)

    def qkv_part(i, carry):
        grad = mm(n1[:, :, chunk(i)].reshape(S, lanes), qg[...], TN).astype(bf16)
        qbuf[pl.ds(i * per, per)] = grad.reshape(per, Z, r, 3 * hw)
        return carry

    lax.fori_loop(0, D // lanes, qkv_part, 0)
    rq = ZReduce(net, lambda zs: qbuf.at[:, zs], ref.qrecv, ref.qsum)
    rq.begin()
    red = Reduce(net, ref.sib_send, sib_recv.at[1], ref.far_send, far_recv.at[1], ref.keep)
    red.begin(lambda chip: mm(qg[tile(chip), :], w_qkv, NT))
    gb.finish()
    obuf[...] = mm(mix[...].reshape(S, hw), whole(bg), TN).astype(bf16)
    ro = ZReduce(
        net, lambda zs: obuf.at[pl.ds(pl.multiple_of(zs * r, r), r)], ref.orecv, ref.osum
    )
    ro.begin()
    ref.dparts[...] = rd.total().astype(bf16)
    home = net.take(1)
    there = net.to((net.home, z), ref.dparts, ref.dfrom, home, home)
    here = pltpu.make_async_copy(ref.dparts, ref.dfrom, local.at[0])

    @pl.when(net.at_home)
    def _():
        here.start()

    @pl.when(jnp.logical_not(net.at_home))
    def _():
        there.start()

    qkv_sums = column_sum(qg[...].astype(f32))
    colz, colp = ref.colz, ref.colp
    colz[z] = jnp.concatenate([qkv_sums[:, 0:hw], qkv_sums[:, 2 * hw : 3 * hw], up_sums], axis=1)
    line = Spread(net, colz, False)
    line.start()

    ref.uparts[...] = ru.total().astype(bf16)
    swap_up.start()
    n1_grad = red.finish()
    red_out = Reduce(net, ref.sib_send, sib_recv.at[0], ref.far_send, far_recv.at[0], ref.keep)
    red_out.begin(lambda chip: mm(hid[tile(chip), :], w_down, NN))
    xhat1, scale1 = row_stats(ref.x_own[...].astype(f32))
    ref.input_grad[...] = (ref.rgrad[...] + norm_back(n1_grad, xhat1, scale1, gain1)).astype(bf16)
    stack = jnp.concatenate(
        [
            column_sum(n1_grad * xhat1), column_sum(n1_grad), sums["out"], sums["gain2"],
            sums["shift2"], sums["down"], jnp.zeros((2, D), f32),
        ],
        axis=0,
    )
    w = D // C
    for i in range(C):
        ref.tok_to[i] = stack[:, i * w : (i + 1) * w]
    swap_tok = Swap(net, ref.tok_to, ref.tok_from)
    swap_tok.start()
    rq.relay()
    ro.relay()

    line.wait()
    total = colz[0]
    for i in range(1, Z):
        total = total + colz[i]
    colp[c] = total
    plane = Spread(net, colp, True)
    plane.start()
    swap_tok.wait()
    tokz = ref.tokz
    total = ref.tok_from[0]
    for i in range(1, C):
        total = total + ref.tok_from[i]
    tokz[z] = total
    tok_line = Spread(net, tokz, False)
    tok_line.start()

    @pl.when(net.at_home)
    def _():
        here.wait()

    @pl.when(jnp.logical_not(net.at_home))
    def _():
        there.wait()

    ref.d_down[...] = ref.dfrom[...].astype(f32)
    swap_up.wait()
    for i in range(C):
        for q in range(Z):
            at = (q * C + net.block(q, i)) * fzc
            ref.d_up[:, at : at + fzc] = ref.ufrom[i, :, q * fzc : (q + 1) * fzc].astype(f32)
    ref.qparts[...] = rq.total().astype(bf16)
    swap_q = Swap(net, ref.qparts, ref.qfrom)
    swap_q.start()
    ref.d_out[...] = ro.total()
    tok_line.wait()
    total = tokz[0]
    for i in range(1, Z):
        total = total + tokz[i]
    ref.tok[...] = chosen([total[:, i * r : (i + 1) * r] for i in range(Z)], z)
    total = red_out.finish()
    ref.layer_out[...] = (ref.resid[...] + total + vectors.get("down")).astype(bf16)
    plane.wait()
    mine = c * Z + z
    part = D * 2 // (C * Z)

    def piece(at, size):
        rest, row = at % hw, (at % D) // hw
        start = hw * (at // D) + rest
        return colp[row, :, start : start + size]

    ref.qv[...] = chosen([piece(i * part, part) for i in range(C * Z)], mine)
    ref.up[...] = chosen(
        [
            colp[net.block(q, i), :, 2 * hw + q * fzc : 2 * hw + (q + 1) * fzc]
            for q in range(Z)
            for i in range(C)
        ],
        mine,
    )
    swap_q.wait()
    for i in range(C):
        for p in range(3):
            ref.d_qkv[:, p * D + i * hw : p * D + (i + 1) * hw] = ref.qfrom[
                i, :, p * hw : (p + 1) * hw
            ].astype(f32)
    assert net.used <= ref.sems.shape[1]
    for part in (zv, zq, zo, zu, zd, rd, ru, ro, rq):
        part.finish()


def hand_over(count, *refs):
    big, (tok, qv, up) = refs[:count], refs[count : count + 3]
    rest, sems = refs[count + 3 :], refs[-1]
    outs, held = rest[: count + 8], rest[count + 8 : -1]
    into = [pltpu.make_async_copy(big[i], held[i], sems.at[0, i]) for i in range(count)]
    out = [pltpu.make_async_copy(held[i], outs[i], sems.at[1, i]) for i in range(count)]
    for copy in into:
        copy.start()
    for i in range(6):
        outs[count + i][...] = tok[i : i + 1, :]
    outs[count + 6][...] = qv[...]
    outs[count + 7][...] = up[...]
    for i in range(count):
        into[i].wait()
        out[i].start()
    for copy in out:
        copy.wait()


def shards(
    tokens_in,
    doc_lengths,
    norm1_gain,
    norm1_bias,
    qkv_weight,
    qv_bias,
    out_weight,
    out_bias,
    norm2_gain,
    norm2_bias,
    up_weight,
    up_bias,
    down_weight,
    down_bias,
    out_cotangent,
):
    C, Z = lax.axis_size("ctx"), lax.axis_size("fsdp")
    c, z = lax.axis_index("ctx"), lax.axis_index("fsdp")
    R, D = tokens_in.shape[1:]
    chips, S, hw = C // 2, R * C, D // C
    ff = up_weight.shape[1]
    fw, fzc, r = ff // C, ff // (C * Z), D // (C * Z)
    heads = hw // HEAD_DIM
    all_vectors = (
        norm1_gain, norm1_bias, qv_bias, out_bias, norm2_gain, norm2_bias, up_bias, down_bias
    )
    sizes = tuple(v.shape[0] for v in all_vectors)
    V, W = sum(sizes), 2 * hw + fw
    vec_in, at = jnp.zeros((V,), f32), 0
    for v in all_vectors:
        vec_in = vec_in + jnp.pad(v.astype(f32), (at, V - at - v.shape[0]))
        at += v.shape[0]
    vec_in = vec_in[None]
    aligned = hw % 128 == 0 and fzc % 128 == 0
    wqkv_in, wup_in = qkv_weight, up_weight
    if not aligned:
        wqkv_in = lax.dynamic_index_in_dim(
            qkv_weight.reshape(D // Z, 3, C, hw), c, axis=2, keepdims=False
        ).reshape(D // Z, 3 * hw)
        split = up_weight.reshape(D // Z, Z, C, fzc)
        wup_in = jnp.concatenate(
            [
                lax.dynamic_index_in_dim(
                    split[:, q], Z * (c // Z) + (q ^ (c % Z)), axis=1, keepdims=False
                )
                for q in range(Z)
            ],
            axis=1,
        )

    vmem, hbm = pltpu.VMEM, pl.BlockSpec(memory_space=pl.ANY)
    ins = dict(
        x_in=(tokens_in[0], hbm),
        cot_in=(out_cotangent[0], hbm),
        docs=(doc_lengths, pl.BlockSpec(memory_space=pltpu.SMEM)),
        vec_in=(vec_in, hbm),
        wqkv_in=(wqkv_in, hbm),
        wout_in=(out_weight, hbm),
        wup_in=(wup_in, hbm),
        wdown_in=(down_weight, hbm),
    )
    outs = dict(
        layer_out=((R, D), bf16),
        input_grad=((R, D), bf16),
        d_qkv=((r, 3 * D), f32),
        d_out=((r, D), f32),
        d_up=((r, ff), f32),
        d_down=((fzc, D), f32),
        tok=((8, r), f32),
        qv=((1, 2 * r), f32),
        up=((1, fzc), f32),
    )
    token, own = (C, R, D), (R, D)
    scratch = dict(
        xs=(token, bf16),
        n1=(token, bf16),
        n2=(token, bf16),
        cot=(token, bf16),
        qkv=((S, 3 * hw), bf16),
        qg=((S, 3 * hw), bf16),
        mix=((C, R, hw), bf16),
        mixf=((C, R, hw), bf16),
        mg=((C, R, hw), bf16),
        slopes=((S, fw), f32),
        wo=((Z, C, r, D), bf16),
        lse=((heads, S, 1), f32),
        dkv=((S, 2 * hw), f32),
        hid=((S, fw), bf16),
        pg=((S, fw), bf16),
        x_own=(own, bf16),
        resid=(own, f32),
        rgrad=(own, f32),
        vec=((Z, 1, V), f32),
        wqkv=((Z, D // Z, 3 * hw), bf16),
        wout_parts=((Z, r, D), bf16),
        wup=((Z, D // Z, fw), bf16),
        wdown=((Z, fzc, D), bf16),
        first=((S, 1), jnp.int32),
        sib_send=((chips, R, D), bf16),
        far_send=((chips, R, D), bf16),
        keep=((chips, R, D), f32),
        sib_recv=((2, chips, R, D), bf16),
        far_recv=((2, chips, R, D), bf16),
        dbuf=((fw, D), bf16),
        ubuf=((C, Z, r, fw), bf16),
        obuf=((hw, D), bf16),
        qbuf=((C, Z, r, 3 * hw), bf16),
        colz=((Z, 1, W), f32),
        tok_to=((C, 8, D // C), f32),
        tok_from=((C, 8, D // C), f32),
        colp=((C, 1, W), f32),
        tokz=((Z, 8, D // C), f32),
    )
    shard = dict(d=(fzc, D), u=(C, r, fw), o=(r, D), q=(C, r, 3 * hw))
    for k, shape in shard.items():
        scratch[k + "recv"] = ((Z - 1, *shape), bf16)
        scratch[k + "sum"] = ((Z // 2, *shape), bf16)
        if k != "o":
            scratch[k + "parts"] = (shape, bf16)
            scratch[k + "from"] = (shape, bf16)
    gathers = 5 * max(13, C)
    count = gathers + 12 * Z + 6 * chips + 6 * C + 2
    names = (*ins, *outs, *scratch, "sems", "local")
    got = pl.pallas_call(
        functools.partial(layer_kernel, names, chips, Z, sizes, aligned),
        out_shape=[jax.ShapeDtypeStruct(*v) for v in outs.values()],
        in_specs=[v[1] for v in ins.values()],
        out_specs=[pl.BlockSpec(memory_space=vmem)] * len(outs),
        scratch_shapes=[vmem(*v) for v in scratch.values()]
        + [pltpu.SemaphoreType.DMA((2, count)), pltpu.SemaphoreType.DMA((8 + Z,))],
        compiler_params=pltpu.CompilerParams(
            collective_id=1, has_side_effects=True, vmem_limit_bytes=63 << 20
        ),
        name="layer",
    )(*[v[0] for v in ins.values()])
    big = 6
    results = list(outs.values())[:big] + [((1, r), f32)] * 6 + [outs[k] for k in list(outs)[-2:]]
    done = pl.pallas_call(
        functools.partial(hand_over, big),
        out_shape=[jax.ShapeDtypeStruct(*v) for v in results],
        in_specs=[hbm] * big + [pl.BlockSpec(memory_space=vmem)] * 3,
        out_specs=[hbm] * big + [pl.BlockSpec(memory_space=vmem)] * 8,
        scratch_shapes=[vmem(*v) for v in results[:big]] + [pltpu.SemaphoreType.DMA((2, big))],
        name="hand_over",
    )(*got)
    layer_out, input_grad, d_qkv, d_out, d_up, d_down = done[:big]
    gain1, shift1, out, gain2, shift2, down, qv, up = (v.reshape(-1) for v in done[big:])
    return (
        layer_out[None], input_grad[None], gain1, shift1, d_qkv, qv, d_out, out,
        gain2, shift2, d_up, up, d_down, down,
    )


def solution(mesh):
    token = P("fsdp", "ctx", None)
    flat, table = P("fsdp"), P("fsdp", None)
    home, home2 = P(("ctx", "fsdp")), P(("ctx", "fsdp"), None)
    return jax.shard_map(
        shards,
        mesh=mesh,
        in_specs=(
            token, table, flat, flat, table, flat, table, flat,
            flat, flat, table, flat, table, flat, token,
        ),
        out_specs=(
            token, token, home, home, home2, home, home2, home,
            home, home, home2, home, home2, home,
        ),
        check_vma=False,
    )
```

```python
import functools
from types import SimpleNamespace

import jax
import jax.numpy as jnp
from jax import lax
from jax.experimental import pallas as pl
from jax.experimental.pallas import tpu as pltpu
from jax.sharding import PartitionSpec as P

HEADS = 16
HEAD_DIM = 64
MESH = pl.DeviceIdType.MESH

epsilon = 1e-05
masked_score = -1e30
score_scale = HEAD_DIM ** (-0.5)
f32 = jnp.float32
bf16 = jnp.bfloat16


def row_stats(values):
    mean = jnp.mean(values, axis=-1, keepdims=True)
    centre = values - mean
    spread = jnp.mean(centre * centre, axis=-1, keepdims=True)
    scale = lax.rsqrt(spread + epsilon)
    return centre * scale, scale


def norm_back(grad, xhat, scale, gain):
    gh = grad * gain
    return scale * (
        gh
        - jnp.mean(gh, axis=-1, keepdims=True)
        - xhat * jnp.mean(gh * xhat, axis=-1, keepdims=True)
    )


def gelu_both(v):
    k = 0.7978845608028654
    square = v * v
    inner = jnp.tanh(k * v * (1.0 + 0.044715 * square))
    half = 0.5 * (1.0 + inner)
    slope = half + 0.5 * v * (1.0 - inner * inner) * (k * (1.0 + 3 * 0.044715 * square))
    return v * half, slope


def mm(a, b, dims):
    return lax.dot_general(a, b, (dims, ((), ())), preferred_element_type=f32)


NN = ((1,), (0,))
NT = ((1,), (1,))
TN = ((0,), (0,))


def column_sum(v):
    return jnp.sum(v, axis=0, keepdims=True)


def bits(n):
    out = []
    while n > 1:
        n //= 2
        out.append(n)
    return out


class Net:
    def __init__(self, chips, Z, sems):
        self.chips, self.Z, self.C = chips, Z, 2 * chips
        self.c = lax.axis_index("ctx")
        self.z = lax.axis_index("fsdp")
        self.sems, self.used = sems, 0
        q = self.z ^ (self.c % Z)
        self.home = q * (self.C // Z) + self.c // Z
        self.at_home = self.home == self.c

    def block(self, q, c):
        return self.Z * (c // self.Z) + (q ^ (c % self.Z))

    def take(self, count):
        self.used += count
        return self.used - count

    def barrier(self):
        sem = pltpu.get_barrier_semaphore()
        peers = [(self.c ^ d, self.z) for d in range(1, self.C)]
        peers += [(self.c, self.z ^ d) for d in range(1, self.Z)]
        for peer in peers:
            pl.semaphore_signal(sem, inc=1, device_id=peer, device_id_type=MESH)

        pl.semaphore_wait(sem, len(peers))

    def to(self, device, src, dst, out, into):
        return pltpu.make_async_remote_copy(
            src, dst, self.sems.at[0, out], self.sems.at[1, into],
            device_id=device, device_id_type=MESH,
        )

    def to_ctx(self, d, src, dst, i):
        return self.to((self.c ^ d, self.z), src, dst, i, i)

    def to_z(self, d, src, dst, i):
        return self.to((self.c, self.z ^ d), src, dst, i, i)


class ZGather:
    def __init__(self, net, dst):
        self.net, self.dst = net, dst
        self.base = net.take(net.Z)
        self.copies, self.got = {}, {0}

    def send(self, e, d):
        part = self.dst.at[self.net.z ^ e]
        copy = self.net.to_z(d, part, part, self.base + (e ^ d))
        copy.start()
        self.copies[e ^ d] = copy

    def begin(self):
        for d in bits(self.net.Z):
            self.send(0, d)

    def receive(self, e):
        if e not in self.got:
            self.copies[e].wait_recv()
            self.got.add(e)

    def relay(self):
        held = [0]
        for d in bits(self.net.Z):
            for e in held[1:]:
                self.receive(e)
                self.send(e, d)
            held = held + [e ^ d for e in held]

    def wait(self):
        for e in range(self.net.Z):
            self.receive(e)

    def finish(self):
        for copy in self.copies.values():
            copy.wait_send()


class ZReduce:
    def __init__(self, net, shard, recv, sums):
        self.net, self.shard, self.recv, self.sums = net, shard, recv, sums
        self.base = net.take(net.Z)
        self.terms = {e: [shard(net.z ^ e)] for e in range(net.Z)}
        self.copies, self.slot, self.full = [], 0, 0
        self.stages = bits(net.Z)[::-1]
        self.pending = {}

    def load(self, e):
        if e in self.pending:
            for copy in self.pending.pop(e):
                copy.wait_recv()
        total = None
        for ref in self.terms[e]:
            v = ref[...].astype(f32)
            total = v if total is None else total + v
        return total

    def stage(self, d):
        go = [e for e in sorted(self.terms) if e & d]
        for e in go:
            ref = self.terms[e][0]
            if len(self.terms[e]) > 1:
                total = self.load(e)
                ref = self.sums.at[self.full]
                self.full += 1
                ref[...] = total.astype(bf16)
            del self.terms[e]
            keep = e ^ d
            into = self.recv.at[self.slot]
            copy = self.net.to_z(d, ref, into, self.base + self.slot)
            copy.start()
            self.slot += 1
            self.copies.append(copy)
            self.pending.setdefault(keep, []).append(copy)
            self.terms[keep].append(into)

    def begin(self):
        self.stage(self.stages[0])

    def relay(self):
        for d in self.stages[1:]:
            self.stage(d)

    def total(self):
        return self.load(0)

    def finish(self):
        for copy in self.copies:
            copy.wait_send()


class Gather:
    def __init__(self, net, src, place, rows):
        self.net, self.src, self.place, self.rows = net, src, place, rows
        self.base = net.take(13 if net.chips == 4 else net.C)
        self.sent = []

    def copy(self, d, src, dst, i):
        copy = self.net.to_ctx(d, src, dst, self.base + i)
        copy.start()
        self.sent.append(copy)
        return copy

    def own(self, d, rows, i):
        return self.copy(d, self.src(rows), self.place(self.net.c, rows), i)

    def relay(self, d, rows, target, i):
        part = self.place(self.net.c ^ d, rows)
        return self.copy(target, part, part, i)

    def begin(self):
        every = pl.ds(0, self.rows)
        if self.net.chips == 4:
            half = self.rows // 2
            self.lo, self.hi = pl.ds(0, half), pl.ds(half, half)
            self.x_lo = self.own(2, self.lo, 0)
            self.y_hi = self.own(4, self.hi, 1)
            self.x_hi = self.own(2, self.hi, 2)
            self.y_lo = self.own(4, self.lo, 3)
            self.beside = self.own(1, every, 4)
        else:
            self.far = {d: self.own(2 * d, every, 2 * d) for d in range(self.net.chips - 1, 0, -1)}
            self.beside = self.own(1, every, 1)

    def middle(self):
        if self.net.chips == 4:
            self.x_lo.wait_recv()
            self.r_lo = self.relay(2, self.lo, 4, 5)
            self.s0 = self.relay(2, self.lo, 1, 6)
            self.y_hi.wait_recv()
            self.r_hi = self.relay(4, self.hi, 2, 7)
            self.s1 = self.relay(4, self.hi, 1, 8)

    def finish(self, ready=None):
        ready = ready or (lambda d: None)
        self.beside.wait_recv()
        ready(1)
        if self.net.chips == 4:
            self.x_hi.wait_recv()
            s2 = self.relay(2, self.hi, 1, 9)
            ready(2)
            self.y_lo.wait_recv()
            s3 = self.relay(4, self.lo, 1, 10)
            ready(4)
            self.r_lo.wait_recv()
            s4 = self.relay(6, self.lo, 1, 11)
            self.r_hi.wait_recv()
            s5 = self.relay(6, self.hi, 1, 12)
            ready(6)
            self.s0.wait_recv()
            s2.wait_recv()
            ready(3)
            self.s1.wait_recv()
            s3.wait_recv()
            ready(5)
            s4.wait_recv()
            s5.wait_recv()
            ready(7)
        else:
            on, every = {}, pl.ds(0, self.rows)
            for d, copy in self.far.items():
                copy.wait_recv()
                on[d] = self.relay(2 * d, every, 1, 2 * d + 1)
                ready(2 * d)
            for d, copy in on.items():
                copy.wait_recv()
                ready(2 * d + 1)
        for copy in self.sent:
            copy.wait_send()


class Reduce:
    def __init__(self, net, sib_send, sib_recv, far_send, far_recv, keep):
        self.net = net
        self.base = net.take(2 * net.chips)
        self.sib_send, self.sib_recv = sib_send, sib_recv
        self.far_send, self.far_recv, self.keep = far_send, far_recv, keep
        self.sib, self.far = {}, {}

    def pass_on(self, d):
        self.sib[d].wait_recv()
        total = self.keep[d] + self.sib_recv[d].astype(f32)
        self.far_send[d] = total.astype(bf16)
        self.far[d] = self.net.to_ctx(
            2 * d, self.far_send.at[d], self.far_recv.at[d], self.base + self.net.chips + d
        )
        self.far[d].start()

    def begin(self, partial):
        net = self.net
        core, chip = net.c % 2, net.c // 2
        last = None
        for d in range(net.chips - 1, -1, -1):
            terms = partial(chip ^ d)
            rows = terms.shape[0] // 2
            low, high = terms[:rows], terms[rows:]
            self.sib_send[d] = jnp.where(core == 0, high, low).astype(bf16)
            self.sib[d] = net.to_ctx(1, self.sib_send.at[d], self.sib_recv.at[d], self.base + d)
            self.sib[d].start()
            self.keep[d] = jnp.where(core == 0, low, high)
            if last is not None:
                self.pass_on(last)
            last = d

    def finish(self):
        self.sib[0].wait_recv()
        total = self.keep[0] + self.sib_recv[0].astype(f32)
        for d in range(self.net.chips - 1, 0, -1):
            self.far[d].wait_recv()
            total = total + self.far_recv[d].astype(f32)
        for copy in list(self.sib.values()) + list(self.far.values()):
            copy.wait_send()
        return total


class Swap:
    def __init__(self, net, parts, dst):
        self.net, self.parts, self.dst = net, parts, dst
        self.base = net.take(net.C)

    def start(self):
        net = self.net
        self.copies = [
            net.to_ctx(d, self.parts.at[net.c ^ d], self.dst.at[net.c], self.base + d)
            for d in range(net.C - 1, 0, -1)
        ]
        for copy in self.copies:
            copy.start()
        self.dst[net.c] = self.parts[net.c]

    def wait(self):
        for copy in self.copies:
            copy.wait()


class Spread:
    def __init__(self, net, dst, plane):
        self.net, self.dst, self.plane = net, dst, plane
        self.base = net.take(net.C if plane else net.Z)

    def start(self):
        net = self.net
        part = self.dst.at[net.c if self.plane else net.z]
        send = net.to_ctx if self.plane else net.to_z
        count = net.C if self.plane else net.Z
        self.copies = [send(d, part, part, self.base + d) for d in range(count - 1, 0, -1)]
        for copy in self.copies:
            copy.start()

    def wait(self):
        for copy in self.copies:
            copy.wait()


class Vectors:
    names = ("gain1", "shift1", "qv", "out", "gain2", "shift2", "up", "down")

    def __init__(self, ref, Z, sizes):
        self.ref, self.Z, self.at = ref, Z, {}
        start = 0
        for name, size in zip(self.names, sizes):
            self.at[name] = (start, size)
            start += size

    def get(self, name):
        start, size = self.at[name]
        return jnp.concatenate(
            [self.ref[z, :, start : start + size] for z in range(self.Z)], axis=1
        )


def chosen(pieces, index):
    out = jnp.zeros_like(pieces[0])
    for i, piece in enumerate(pieces):
        out = jnp.where(index == i, piece, out)
    return out


def layer_kernel(names, chips, Z, sizes, aligned, *refs):
    ref = SimpleNamespace(**dict(zip(names, refs)))
    net = Net(chips, Z, ref.sems)
    local = ref.local
    c, z, C = net.c, net.z, net.C
    x_in, cot_in = ref.x_in, ref.cot_in
    R, D = x_in.shape
    S = R * C
    hw = ref.mix.shape[2]
    heads = hw // HEAD_DIM
    fw = ref.hid.shape[1]
    fzc = fw // Z
    r = D // (C * Z)
    step = 2 * R
    xs, n1, n2, cot = (ref.xs, ref.n1, ref.n2, ref.cot)
    bg = xs
    qkv, mix, lse = ref.qkv, ref.mix, ref.lse

    started = []

    def bring(src, dst, i):
        copy = pltpu.make_async_copy(src, dst, local.at[i])
        copy.start()
        return copy

    load_vec = [bring(ref.vec_in, ref.vec.at[z], 0)]
    load_x = bring(x_in, xs.at[c], 1)
    if aligned:
        load_q = [
            bring(
                ref.wqkv_in.at[:, pl.ds(pl.multiple_of(p * D + c * hw, hw), hw)],
                ref.wqkv.at[z, :, p * hw : (p + 1) * hw], 2 + p,
            )
            for p in range(3)
        ]
        FZ = fzc * C
        load_u = [
            bring(
                ref.wup_in.at[:, pl.ds(pl.multiple_of(p * FZ + net.block(p, c) * fzc, fzc), fzc)],
                ref.wup.at[z, :, p * fzc : (p + 1) * fzc], 8 + p,
            )
            for p in range(Z)
        ]
    else:
        load_q = [bring(ref.wqkv_in, ref.wqkv.at[z], 2)]
        load_u = [bring(ref.wup_in, ref.wup.at[z], 8)]
    load_o = bring(ref.wout_in.at[pl.ds(pl.multiple_of(c * r, r), r)], ref.wout_parts.at[z], 5)
    load_d = bring(ref.wdown_in.at[pl.ds(pl.multiple_of(net.block(z, c) * fzc, fzc), fzc)], ref.wdown.at[z], 6)
    load_c = bring(cot_in, cot.at[c], 7)

    zv, zq = ZGather(net, ref.vec), ZGather(net, ref.wqkv)
    zo, zu = ZGather(net, ref.wout_parts), ZGather(net, ref.wup)
    zd = ZGather(net, ref.wdown)
    net.barrier()
    load_vec[0].wait()
    zv.begin()

    def tokens(src, dst):
        return Gather(net, lambda rows: src.at[rows], lambda i, rows: dst.at[i, rows], R)

    gx = tokens(x_in, xs)
    gx.begin()
    load_o.wait()
    zo.begin()
    for copy in load_q:
        copy.wait()
    zq.begin()

    pos = lax.broadcasted_iota(jnp.int32, (S, 1), 0)
    first = jnp.zeros((S, 1), jnp.int32)
    end = jnp.int32(0)
    for i in range(ref.docs.shape[1]):
        end = end + ref.docs[0, i]
        first = jnp.where(pos >= end, end, first)
    ref.first[...] = first

    zv.relay()
    zv.wait()
    vectors = Vectors(ref.vec, Z, sizes)
    gain1, shift1 = vectors.get("gain1"), vectors.get("shift1")
    load_x.wait()

    def norm_one(d):
        block = c ^ d
        xhat, _ = row_stats(xs[block].astype(f32))
        n1[block] = (xhat * gain1 + shift1).astype(bf16)

    norm_one(0)
    gx.middle()
    zo.relay()
    zq.relay()
    gx.finish(norm_one)
    parts_o, wo = ref.wout_parts, ref.wo
    wg = Gather(net, lambda rows: parts_o.at[:, rows], lambda i, rows: wo.at[:, i, rows], r)
    zo.wait()
    wg.begin()
    wo[:, c] = parts_o[...]
    for copy in load_u:
        copy.wait()

    qv = vectors.get("qv")
    bias = jnp.concatenate(
        [
            chosen([qv[:, i * hw : (i + 1) * hw] for i in range(C)], c),
            jnp.zeros((1, hw), f32),
            chosen([qv[:, D + i * hw : D + (i + 1) * hw] for i in range(C)], c),
        ],
        axis=1,
    )
    zq.wait()
    zu.begin()
    wg.middle()
    w_qkv = ref.wqkv[...].reshape(D, 3 * hw)

    def blocks(array, i):
        return array[pl.ds(2 * i, 2)].reshape(step, D)

    def tile(i):
        return pl.ds(pl.multiple_of(i * step, step), step)

    def project(i, carry):
        qkv[tile(i), :] = (mm(blocks(n1, i), w_qkv, NN) + bias).astype(bf16)
        return carry

    lax.fori_loop(0, S // step, project, 0)
    load_c.wait()
    gc = tokens(cot_in, cot)
    gc.begin()
    tiles = S // step

    def masked(i):
        n = (i + 1) * step
        row = lax.broadcasted_iota(jnp.int32, (step, n), 0) + i * step
        col = lax.broadcasted_iota(jnp.int32, (step, n), 1)
        return (col <= row) & (col >= ref.first[i * step : n, :])

    def head(part, h, rows):
        at = part * hw + h * HEAD_DIM
        return qkv[rows, at : at + HEAD_DIM]

    def beside(parts):
        return jnp.concatenate(parts, axis=1) if len(parts) > 1 else parts[0]

    def put(array, i, value):
        array[2 * i], array[2 * i + 1] = value[:R], value[R:]

    for i in range(tiles):
        if i == tiles - 1:
            wg.finish()
            load_d.wait()
            zd.begin()
        n = (i + 1) * step
        rows, keys = slice(i * step, n), slice(0, n)
        allowed = masked(i)
        parts = []
        for h in range(heads):
            s = mm(head(0, h, rows), head(1, h, keys), NT) * score_scale
            s = jnp.where(allowed, s, masked_score)
            top = jnp.max(s, axis=1, keepdims=True)
            e = jnp.exp(s - top)
            total = jnp.sum(e, axis=1, keepdims=True)
            parts.append((mm(e.astype(bf16), head(2, h, keys), NN) / total).astype(bf16))
            lse[h, rows, :] = top + jnp.log(total)
        put(mix, i, beside(parts))
    swap_mix = Swap(net, mix, ref.mixf)
    swap_mix.start()
    gc.middle()
    zu.relay()
    swap_mix.wait()
    w_out = wo[...].reshape(D, D)
    mixed = jnp.concatenate([ref.mixf[i] for i in range(C)], axis=1)
    x_own = xs[c]
    ref.x_own[...] = x_own
    resid = x_own.astype(f32) + mm(mixed, w_out, NN) + vectors.get("out")
    xhat2, scale2 = row_stats(resid)
    gain2 = vectors.get("gain2")
    n2[c] = (xhat2 * gain2 + vectors.get("shift2")).astype(bf16)
    ref.resid[...] = resid
    gc.finish()
    gn = tokens(n2.at[c], n2)
    gn.begin()
    gn.middle()
    zd.relay()
    zu.wait()
    w_up = ref.wup[...].reshape(D, fw)
    up = vectors.get("up")
    b_up = jnp.concatenate(
        [
            chosen(
                [up[:, (q * C + i) * fzc : (q * C + i + 1) * fzc] for i in range(C)],
                net.block(q, c),
            )
            for q in range(Z)
        ],
        axis=1,
    )
    gn.finish()
    hid, pg, slopes = ref.hid, ref.pg, ref.slopes

    def feed(i, carry):
        rows = tile(i)
        value, slope = gelu_both(mm(blocks(n2, i), w_up, NN) + b_up)
        hid[rows, :] = value.astype(bf16)
        slopes[rows, :] = slope
        return carry

    lax.fori_loop(0, tiles, feed, 0)

    lanes = 128

    def whole(array):
        return array[...].reshape(S, D)

    def chunk(i):
        return pl.ds(pl.multiple_of(i * lanes, lanes), lanes)

    dbuf, ubuf, obuf, qbuf = (ref.dbuf, ref.ubuf, ref.obuf, ref.qbuf)

    def down_part(i, carry):
        dbuf[chunk(i), :] = mm(hid[:, chunk(i)], whole(cot), TN).astype(bf16)
        return carry

    lax.fori_loop(0, fw // lanes, down_part, 0)
    zd.wait()
    rd = ZReduce(
        net,
        lambda zs: dbuf.at[pl.ds(pl.multiple_of((zs ^ (c % Z)) * fzc, fzc), fzc)],
        ref.drecv,
        ref.dsum,
    )
    rd.begin()
    w_down = ref.wdown[...].reshape(fw, D)

    up_sums = []

    def feed_back(chip):
        rows = tile(chip)
        grad = (mm(blocks(cot, chip), w_down, NT) * slopes[rows, :]).astype(bf16)
        pg[rows, :] = grad
        up_sums.append(column_sum(grad.astype(f32)))
        return mm(grad, w_up, NT)

    sib_recv, far_recv = ref.sib_recv, ref.far_recv
    red = Reduce(net, ref.sib_send, sib_recv.at[0], ref.far_send, far_recv.at[0], ref.keep)
    red.begin(feed_back)
    up_sums = sum(up_sums)
    per = lanes // (Z * r)

    def up_part(i, carry):
        grad = mm(n2[:, :, chunk(i)].reshape(S, lanes), pg[...], TN).astype(bf16)
        ubuf[pl.ds(i * per, per)] = grad.reshape(per, Z, r, fw)
        return carry

    lax.fori_loop(0, D // lanes, up_part, 0)
    ru = ZReduce(net, lambda zs: ubuf.at[:, zs], ref.urecv, ref.usum)
    ru.begin()

    n2_grad = red.finish()
    cot_own = cot[c].astype(f32)
    xhat2, scale2 = row_stats(ref.resid[...])
    resid_grad = cot_own + norm_back(n2_grad, xhat2, scale2, gain2)
    branch = resid_grad.astype(bf16)
    bg[c] = branch
    ref.rgrad[...] = resid_grad
    back = mm(branch, w_out, NT).astype(bf16)
    mg = ref.mg
    for i in range(C):
        ref.mixf[i] = back[:, i * hw : (i + 1) * hw]
    swap_mg = Swap(net, ref.mixf, mg)
    swap_mg.start()
    gb = tokens(bg.at[c], bg)
    gb.begin()
    sums = {
        "out": column_sum(branch.astype(f32)),
        "gain2": column_sum(n2_grad * xhat2),
        "shift2": column_sum(n2_grad),
        "down": column_sum(cot_own),
    }
    swap_mg.wait()
    rd.relay()
    qg, dkv = ref.qg, ref.dkv
    dkv[...] = jnp.zeros((S, 2 * hw), f32)
    swap_up = Swap(net, ref.uparts, ref.ufrom)
    for i in range(tiles):
        n = (i + 1) * step
        rows, keys = slice(i * step, n), slice(0, n)
        if i == 1:
            gb.middle()
        if i == tiles - 1:
            ru.relay()
        allowed = masked(i)
        g_rows = mg[2 * i : 2 * i + 2].reshape(step, hw)
        m_rows = mix[2 * i : 2 * i + 2].reshape(step, hw)
        dqs, dks, dvs = [], [], []
        for h in range(heads):
            at = h * HEAD_DIM
            q, k, v = head(0, h, rows), head(1, h, keys), head(2, h, keys)
            g, m = g_rows[:, at : at + HEAD_DIM], m_rows[:, at : at + HEAD_DIM]
            s = mm(q, k, NT) * score_scale - lse[h, rows, :]
            p = jnp.where(allowed, jnp.exp(s), 0.0)
            delta = jnp.sum(g.astype(f32) * m.astype(f32), axis=1, keepdims=True)
            ds = (p * (mm(g, v, NT) - delta)).astype(bf16)
            dqs.append(score_scale * mm(ds, k, NN))
            dks.append(score_scale * mm(ds, q, TN))
            dvs.append(mm(p.astype(bf16), g, TN))
        qg[rows, 0:hw] = beside(dqs).astype(bf16)
        dkv[keys, :] += beside(dks + dvs)
    qg[:, hw : 3 * hw] = dkv[...].astype(bf16)

    def qkv_part(i, carry):
        grad = mm(n1[:, :, chunk(i)].reshape(S, lanes), qg[...], TN).astype(bf16)
        qbuf[pl.ds(i * per, per)] = grad.reshape(per, Z, r, 3 * hw)
        return carry

    red = Reduce(net, ref.sib_send, sib_recv.at[1], ref.far_send, far_recv.at[1], ref.keep)
    red.begin(lambda chip: mm(qg[tile(chip), :], w_qkv, NT))
    lax.fori_loop(0, D // lanes, qkv_part, 0)
    rq = ZReduce(net, lambda zs: qbuf.at[:, zs], ref.qrecv, ref.qsum)
    rq.begin()
    gb.finish()
    obuf[...] = mm(mix[...].reshape(S, hw), whole(bg), TN).astype(bf16)
    ro = ZReduce(
        net, lambda zs: obuf.at[pl.ds(pl.multiple_of(zs * r, r), r)], ref.orecv, ref.osum
    )
    ro.begin()
    ref.dparts[...] = rd.total().astype(bf16)
    home = net.take(1)
    there = net.to((net.home, z), ref.dparts, ref.dfrom, home, home)
    here = pltpu.make_async_copy(ref.dparts, ref.dfrom, local.at[0])

    @pl.when(net.at_home)
    def _():
        here.start()

    @pl.when(jnp.logical_not(net.at_home))
    def _():
        there.start()

    qkv_sums = column_sum(qg[...].astype(f32))
    colz, colp = ref.colz, ref.colp
    colz[z] = jnp.concatenate([qkv_sums[:, 0:hw], qkv_sums[:, 2 * hw : 3 * hw], up_sums], axis=1)
    line = Spread(net, colz, False)
    line.start()

    ref.uparts[...] = ru.total().astype(bf16)
    swap_up.start()
    n1_grad = red.finish()
    red_out = Reduce(net, ref.sib_send, sib_recv.at[0], ref.far_send, far_recv.at[0], ref.keep)
    red_out.begin(lambda chip: mm(hid[tile(chip), :], w_down, NN))
    xhat1, scale1 = row_stats(ref.x_own[...].astype(f32))
    ref.input_grad[...] = (ref.rgrad[...] + norm_back(n1_grad, xhat1, scale1, gain1)).astype(bf16)
    stack = jnp.concatenate(
        [
            column_sum(n1_grad * xhat1), column_sum(n1_grad), sums["out"], sums["gain2"],
            sums["shift2"], sums["down"], jnp.zeros((2, D), f32),
        ],
        axis=0,
    )
    w = D // C
    for i in range(C):
        ref.tok_to[i] = stack[:, i * w : (i + 1) * w]
    swap_tok = Swap(net, ref.tok_to, ref.tok_from)
    swap_tok.start()
    rq.relay()
    ro.relay()

    line.wait()
    total = colz[0]
    for i in range(1, Z):
        total = total + colz[i]
    colp[c] = total
    plane = Spread(net, colp, True)
    plane.start()
    swap_tok.wait()
    tokz = ref.tokz
    total = ref.tok_from[0]
    for i in range(1, C):
        total = total + ref.tok_from[i]
    tokz[z] = total
    tok_line = Spread(net, tokz, False)
    tok_line.start()

    @pl.when(net.at_home)
    def _():
        here.wait()

    @pl.when(jnp.logical_not(net.at_home))
    def _():
        there.wait()

    ref.d_down[...] = ref.dfrom[...].astype(f32)
    swap_up.wait()
    for i in range(C):
        for q in range(Z):
            at = (q * C + net.block(q, i)) * fzc
            ref.d_up[:, at : at + fzc] = ref.ufrom[i, :, q * fzc : (q + 1) * fzc].astype(f32)
    ref.qparts[...] = rq.total().astype(bf16)
    swap_q = Swap(net, ref.qparts, ref.qfrom)
    swap_q.start()
    ref.d_out[...] = ro.total()
    tok_line.wait()
    total = tokz[0]
    for i in range(1, Z):
        total = total + tokz[i]
    ref.tok[...] = chosen([total[:, i * r : (i + 1) * r] for i in range(Z)], z)
    total = red_out.finish()
    ref.layer_out[...] = (ref.resid[...] + total + vectors.get("down")).astype(bf16)
    plane.wait()
    mine = c * Z + z
    part = D * 2 // (C * Z)

    def piece(at, size):
        rest, row = at % hw, (at % D) // hw
        start = hw * (at // D) + rest
        return colp[row, :, start : start + size]

    ref.qv[...] = chosen([piece(i * part, part) for i in range(C * Z)], mine)
    ref.up[...] = chosen(
        [
            colp[net.block(q, i), :, 2 * hw + q * fzc : 2 * hw + (q + 1) * fzc]
            for q in range(Z)
            for i in range(C)
        ],
        mine,
    )
    swap_q.wait()
    for i in range(C):
        for p in range(3):
            ref.d_qkv[:, p * D + i * hw : p * D + (i + 1) * hw] = ref.qfrom[
                i, :, p * hw : (p + 1) * hw
            ].astype(f32)
    assert net.used <= ref.sems.shape[1]
    for part in (zv, zq, zo, zu, zd, rd, ru, ro, rq):
        part.finish()


def hand_over(count, *refs):
    big, (tok, qv, up) = refs[:count], refs[count : count + 3]
    rest, sems = refs[count + 3 :], refs[-1]
    outs, held = rest[: count + 8], rest[count + 8 : -1]
    into = [pltpu.make_async_copy(big[i], held[i], sems.at[0, i]) for i in range(count)]
    out = [pltpu.make_async_copy(held[i], outs[i], sems.at[1, i]) for i in range(count)]
    for copy in into:
        copy.start()
    for i in range(6):
        outs[count + i][...] = tok[i : i + 1, :]
    outs[count + 6][...] = qv[...]
    outs[count + 7][...] = up[...]
    for i in range(count):
        into[i].wait()
        out[i].start()
    for copy in out:
        copy.wait()


def shards(
    tokens_in,
    doc_lengths,
    norm1_gain,
    norm1_bias,
    qkv_weight,
    qv_bias,
    out_weight,
    out_bias,
    norm2_gain,
    norm2_bias,
    up_weight,
    up_bias,
    down_weight,
    down_bias,
    out_cotangent,
):
    C, Z = lax.axis_size("ctx"), lax.axis_size("fsdp")
    c, z = lax.axis_index("ctx"), lax.axis_index("fsdp")
    R, D = tokens_in.shape[1:]
    chips, S, hw = C // 2, R * C, D // C
    ff = up_weight.shape[1]
    fw, fzc, r = ff // C, ff // (C * Z), D // (C * Z)
    heads = hw // HEAD_DIM
    all_vectors = (
        norm1_gain, norm1_bias, qv_bias, out_bias, norm2_gain, norm2_bias, up_bias, down_bias
    )
    sizes = tuple(v.shape[0] for v in all_vectors)
    V, W = sum(sizes), 2 * hw + fw
    vec_in, at = jnp.zeros((V,), f32), 0
    for v in all_vectors:
        vec_in = vec_in + jnp.pad(v.astype(f32), (at, V - at - v.shape[0]))
        at += v.shape[0]
    vec_in = vec_in[None]
    aligned = hw % 128 == 0 and fzc % 128 == 0
    wqkv_in, wup_in = qkv_weight, up_weight
    if not aligned:
        wqkv_in = lax.dynamic_index_in_dim(
            qkv_weight.reshape(D // Z, 3, C, hw), c, axis=2, keepdims=False
        ).reshape(D // Z, 3 * hw)
        split = up_weight.reshape(D // Z, Z, C, fzc)
        wup_in = jnp.concatenate(
            [
                lax.dynamic_index_in_dim(
                    split[:, q], Z * (c // Z) + (q ^ (c % Z)), axis=1, keepdims=False
                )
                for q in range(Z)
            ],
            axis=1,
        )

    vmem, hbm = pltpu.VMEM, pl.BlockSpec(memory_space=pl.ANY)
    ins = dict(
        x_in=(tokens_in[0], hbm),
        cot_in=(out_cotangent[0], hbm),
        docs=(doc_lengths, pl.BlockSpec(memory_space=pltpu.SMEM)),
        vec_in=(vec_in, hbm),
        wqkv_in=(wqkv_in, hbm),
        wout_in=(out_weight, hbm),
        wup_in=(wup_in, hbm),
        wdown_in=(down_weight, hbm),
    )
    outs = dict(
        layer_out=((R, D), bf16),
        input_grad=((R, D), bf16),
        d_qkv=((r, 3 * D), f32),
        d_out=((r, D), f32),
        d_up=((r, ff), f32),
        d_down=((fzc, D), f32),
        tok=((8, r), f32),
        qv=((1, 2 * r), f32),
        up=((1, fzc), f32),
    )
    token, own = (C, R, D), (R, D)
    scratch = dict(
        xs=(token, bf16),
        n1=(token, bf16),
        n2=(token, bf16),
        cot=(token, bf16),
        qkv=((S, 3 * hw), bf16),
        qg=((S, 3 * hw), bf16),
        mix=((C, R, hw), bf16),
        mixf=((C, R, hw), bf16),
        mg=((C, R, hw), bf16),
        slopes=((S, fw), f32),
        wo=((Z, C, r, D), bf16),
        lse=((heads, S, 1), f32),
        dkv=((S, 2 * hw), f32),
        hid=((S, fw), bf16),
        pg=((S, fw), bf16),
        x_own=(own, bf16),
        resid=(own, f32),
        rgrad=(own, f32),
        vec=((Z, 1, V), f32),
        wqkv=((Z, D // Z, 3 * hw), bf16),
        wout_parts=((Z, r, D), bf16),
        wup=((Z, D // Z, fw), bf16),
        wdown=((Z, fzc, D), bf16),
        first=((S, 1), jnp.int32),
        sib_send=((chips, R, D), bf16),
        far_send=((chips, R, D), bf16),
        keep=((chips, R, D), f32),
        sib_recv=((2, chips, R, D), bf16),
        far_recv=((2, chips, R, D), bf16),
        dbuf=((fw, D), bf16),
        ubuf=((C, Z, r, fw), bf16),
        obuf=((hw, D), bf16),
        qbuf=((C, Z, r, 3 * hw), bf16),
        colz=((Z, 1, W), f32),
        tok_to=((C, 8, D // C), f32),
        tok_from=((C, 8, D // C), f32),
        colp=((C, 1, W), f32),
        tokz=((Z, 8, D // C), f32),
    )
    shard = dict(d=(fzc, D), u=(C, r, fw), o=(r, D), q=(C, r, 3 * hw))
    for k, shape in shard.items():
        scratch[k + "recv"] = ((Z - 1, *shape), bf16)
        scratch[k + "sum"] = ((Z // 2, *shape), bf16)
        if k != "o":
            scratch[k + "parts"] = (shape, bf16)
            scratch[k + "from"] = (shape, bf16)
    gathers = 5 * max(13, C)
    count = gathers + 12 * Z + 6 * chips + 6 * C + 2
    names = (*ins, *outs, *scratch, "sems", "local")
    got = pl.pallas_call(
        functools.partial(layer_kernel, names, chips, Z, sizes, aligned),
        out_shape=[jax.ShapeDtypeStruct(*v) for v in outs.values()],
        in_specs=[v[1] for v in ins.values()],
        out_specs=[pl.BlockSpec(memory_space=vmem)] * len(outs),
        scratch_shapes=[vmem(*v) for v in scratch.values()]
        + [pltpu.SemaphoreType.DMA((2, count)), pltpu.SemaphoreType.DMA((8 + Z,))],
        compiler_params=pltpu.CompilerParams(
            collective_id=1, has_side_effects=True, vmem_limit_bytes=63 << 20
        ),
        name="layer",
    )(*[v[0] for v in ins.values()])
    big = 6
    results = list(outs.values())[:big] + [((1, r), f32)] * 6 + [outs[k] for k in list(outs)[-2:]]
    done = pl.pallas_call(
        functools.partial(hand_over, big),
        out_shape=[jax.ShapeDtypeStruct(*v) for v in results],
        in_specs=[hbm] * big + [pl.BlockSpec(memory_space=vmem)] * 3,
        out_specs=[hbm] * big + [pl.BlockSpec(memory_space=vmem)] * 8,
        scratch_shapes=[vmem(*v) for v in results[:big]] + [pltpu.SemaphoreType.DMA((2, big))],
        name="hand_over",
    )(*got)
    layer_out, input_grad, d_qkv, d_out, d_up, d_down = done[:big]
    gain1, shift1, out, gain2, shift2, down, qv, up = (v.reshape(-1) for v in done[big:])
    return (
        layer_out[None], input_grad[None], gain1, shift1, d_qkv, qv, d_out, out,
        gain2, shift2, d_up, up, d_down, down,
    )


def solution(mesh):
    token = P("fsdp", "ctx", None)
    flat, table = P("fsdp"), P("fsdp", None)
    home, home2 = P(("ctx", "fsdp")), P(("ctx", "fsdp"), None)
    return jax.shard_map(
        shards,
        mesh=mesh,
        in_specs=(
            token, table, flat, flat, table, flat, table, flat,
            flat, flat, table, flat, table, flat, token,
        ),
        out_specs=(
            token, token, home, home, home2, home, home2, home,
            home, home, home2, home, home2, home,
        ),
        check_vma=False,
    )
```

```python
import functools
from types import SimpleNamespace

import jax
import jax.numpy as jnp
from jax import lax
from jax.experimental import pallas as pl
from jax.experimental.pallas import tpu as pltpu
from jax.sharding import PartitionSpec as P

HEADS = 16
HEAD_DIM = 64
MESH = pl.DeviceIdType.MESH

epsilon = 1e-05
masked_score = -1e30
score_scale = HEAD_DIM ** (-0.5)
f32 = jnp.float32
bf16 = jnp.bfloat16


def row_stats(values):
    mean = jnp.mean(values, axis=-1, keepdims=True)
    centre = values - mean
    spread = jnp.mean(centre * centre, axis=-1, keepdims=True)
    scale = lax.rsqrt(spread + epsilon)
    return centre * scale, scale


def norm_back(grad, xhat, scale, gain):
    gh = grad * gain
    return scale * (
        gh
        - jnp.mean(gh, axis=-1, keepdims=True)
        - xhat * jnp.mean(gh * xhat, axis=-1, keepdims=True)
    )


def gelu_both(v):
    k = 0.7978845608028654
    square = v * v
    inner = jnp.tanh(k * v * (1.0 + 0.044715 * square))
    half = 0.5 * (1.0 + inner)
    slope = half + 0.5 * v * (1.0 - inner * inner) * (k * (1.0 + 3 * 0.044715 * square))
    return v * half, slope


def mm(a, b, dims):
    return lax.dot_general(a, b, (dims, ((), ())), preferred_element_type=f32)


NN = ((1,), (0,))
NT = ((1,), (1,))
TN = ((0,), (0,))


def column_sum(v):
    return jnp.sum(v, axis=0, keepdims=True)


def bits(n):
    out = []
    while n > 1:
        n //= 2
        out.append(n)
    return out


class Net:
    def __init__(self, chips, Z, sems):
        self.chips, self.Z, self.C = chips, Z, 2 * chips
        self.c = lax.axis_index("ctx")
        self.z = lax.axis_index("fsdp")
        self.sems, self.used = sems, 0
        q = self.z ^ (self.c % Z)
        self.home = q * (self.C // Z) + self.c // Z
        self.at_home = self.home == self.c

    def block(self, q, c):
        return self.Z * (c // self.Z) + (q ^ (c % self.Z))

    def take(self, count):
        self.used += count
        return self.used - count

    def barrier(self):
        sem = pltpu.get_barrier_semaphore()
        peers = [(self.c ^ d, self.z) for d in range(1, self.C)]
        peers += [(self.c, self.z ^ d) for d in range(1, self.Z)]
        for peer in peers:
            pl.semaphore_signal(sem, inc=1, device_id=peer, device_id_type=MESH)

        pl.semaphore_wait(sem, len(peers))

    def to(self, device, src, dst, out, into):
        return pltpu.make_async_remote_copy(
            src, dst, self.sems.at[0, out], self.sems.at[1, into],
            device_id=device, device_id_type=MESH,
        )

    def to_ctx(self, d, src, dst, i):
        return self.to((self.c ^ d, self.z), src, dst, i, i)

    def to_z(self, d, src, dst, i):
        return self.to((self.c, self.z ^ d), src, dst, i, i)


class ZGather:
    def __init__(self, net, dst):
        self.net, self.dst = net, dst
        self.base = net.take(net.Z)
        self.copies, self.got = {}, {0}

    def send(self, e, d):
        part = self.dst.at[self.net.z ^ e]
        copy = self.net.to_z(d, part, part, self.base + (e ^ d))
        copy.start()
        self.copies[e ^ d] = copy

    def begin(self):
        for d in bits(self.net.Z):
            self.send(0, d)

    def receive(self, e):
        if e not in self.got:
            self.copies[e].wait_recv()
            self.got.add(e)

    def relay(self):
        held = [0]
        for d in bits(self.net.Z):
            for e in held[1:]:
                self.receive(e)
                self.send(e, d)
            held = held + [e ^ d for e in held]

    def wait(self):
        for e in range(self.net.Z):
            self.receive(e)

    def finish(self):
        for copy in self.copies.values():
            copy.wait_send()


class ZReduce:
    def __init__(self, net, shard, recv, sums):
        self.net, self.shard, self.recv, self.sums = net, shard, recv, sums
        self.base = net.take(net.Z)
        self.terms = {e: [shard(net.z ^ e)] for e in range(net.Z)}
        self.copies, self.slot, self.full = [], 0, 0
        self.stages = bits(net.Z)[::-1]
        self.pending = {}

    def load(self, e):
        if e in self.pending:
            for copy in self.pending.pop(e):
                copy.wait_recv()
        total = None
        for ref in self.terms[e]:
            v = ref[...].astype(f32)
            total = v if total is None else total + v
        return total

    def stage(self, d):
        go = [e for e in sorted(self.terms) if e & d]
        for e in go:
            ref = self.terms[e][0]
            if len(self.terms[e]) > 1:
                total = self.load(e)
                ref = self.sums.at[self.full]
                self.full += 1
                ref[...] = total.astype(bf16)
            del self.terms[e]
            keep = e ^ d
            into = self.recv.at[self.slot]
            copy = self.net.to_z(d, ref, into, self.base + self.slot)
            copy.start()
            self.slot += 1
            self.copies.append(copy)
            self.pending.setdefault(keep, []).append(copy)
            self.terms[keep].append(into)

    def begin(self):
        self.stage(self.stages[0])

    def relay(self):
        for d in self.stages[1:]:
            self.stage(d)

    def total(self):
        return self.load(0)

    def finish(self):
        for copy in self.copies:
            copy.wait_send()


class Gather:
    def __init__(self, net, src, place, rows):
        self.net, self.src, self.place, self.rows = net, src, place, rows
        self.base = net.take(13 if net.chips == 4 else net.C)
        self.sent = []

    def copy(self, d, src, dst, i):
        copy = self.net.to_ctx(d, src, dst, self.base + i)
        copy.start()
        self.sent.append(copy)
        return copy

    def own(self, d, rows, i):
        return self.copy(d, self.src(rows), self.place(self.net.c, rows), i)

    def relay(self, d, rows, target, i):
        part = self.place(self.net.c ^ d, rows)
        return self.copy(target, part, part, i)

    def begin(self):
        every = pl.ds(0, self.rows)
        if self.net.chips == 4:
            half = self.rows // 2
            self.lo, self.hi = pl.ds(0, half), pl.ds(half, half)
            self.x_lo = self.own(2, self.lo, 0)
            self.y_hi = self.own(4, self.hi, 1)
            self.x_hi = self.own(2, self.hi, 2)
            self.y_lo = self.own(4, self.lo, 3)
            self.beside = self.own(1, every, 4)
        else:
            self.far = {d: self.own(2 * d, every, 2 * d) for d in range(self.net.chips - 1, 0, -1)}
            self.beside = self.own(1, every, 1)

    def middle(self):
        if self.net.chips == 4:
            self.x_lo.wait_recv()
            self.r_lo = self.relay(2, self.lo, 4, 5)
            self.s0 = self.relay(2, self.lo, 1, 6)
            self.y_hi.wait_recv()
            self.r_hi = self.relay(4, self.hi, 2, 7)
            self.s1 = self.relay(4, self.hi, 1, 8)

    def finish(self, ready=None):
        ready = ready or (lambda d: None)
        self.beside.wait_recv()
        ready(1)
        if self.net.chips == 4:
            self.x_hi.wait_recv()
            s2 = self.relay(2, self.hi, 1, 9)
            ready(2)
            self.y_lo.wait_recv()
            s3 = self.relay(4, self.lo, 1, 10)
            ready(4)
            self.r_lo.wait_recv()
            s4 = self.relay(6, self.lo, 1, 11)
            self.r_hi.wait_recv()
            s5 = self.relay(6, self.hi, 1, 12)
            ready(6)
            self.s0.wait_recv()
            s2.wait_recv()
            ready(3)
            self.s1.wait_recv()
            s3.wait_recv()
            ready(5)
            s4.wait_recv()
            s5.wait_recv()
            ready(7)
        else:
            on, every = {}, pl.ds(0, self.rows)
            for d, copy in self.far.items():
                copy.wait_recv()
                on[d] = self.relay(2 * d, every, 1, 2 * d + 1)
                ready(2 * d)
            for d, copy in on.items():
                copy.wait_recv()
                ready(2 * d + 1)
        for copy in self.sent:
            copy.wait_send()


class Reduce:
    def __init__(self, net, sib_send, sib_recv, far_send, far_recv, keep):
        self.net = net
        self.base = net.take(2 * net.chips)
        self.sib_send, self.sib_recv = sib_send, sib_recv
        self.far_send, self.far_recv, self.keep = far_send, far_recv, keep
        self.sib, self.far = {}, {}

    def pass_on(self, d):
        self.sib[d].wait_recv()
        total = self.keep[d] + self.sib_recv[d].astype(f32)
        self.far_send[d] = total.astype(bf16)
        self.far[d] = self.net.to_ctx(
            2 * d, self.far_send.at[d], self.far_recv.at[d], self.base + self.net.chips + d
        )
        self.far[d].start()

    def begin(self, partial):
        net = self.net
        core, chip = net.c % 2, net.c // 2
        last = None
        for d in range(net.chips - 1, -1, -1):
            terms = partial(chip ^ d)
            rows = terms.shape[0] // 2
            low, high = terms[:rows], terms[rows:]
            self.sib_send[d] = jnp.where(core == 0, high, low).astype(bf16)
            self.sib[d] = net.to_ctx(1, self.sib_send.at[d], self.sib_recv.at[d], self.base + d)
            self.sib[d].start()
            self.keep[d] = jnp.where(core == 0, low, high)
            if last is not None:
                self.pass_on(last)
            last = d

    def finish(self):
        self.sib[0].wait_recv()
        total = self.keep[0] + self.sib_recv[0].astype(f32)
        for d in range(self.net.chips - 1, 0, -1):
            self.far[d].wait_recv()
            total = total + self.far_recv[d].astype(f32)
        for copy in list(self.sib.values()) + list(self.far.values()):
            copy.wait_send()
        return total


class Swap:
    def __init__(self, net, parts, dst):
        self.net, self.parts, self.dst = net, parts, dst
        self.base = net.take(net.C)

    def start(self):
        net = self.net
        self.copies = [
            net.to_ctx(d, self.parts.at[net.c ^ d], self.dst.at[net.c], self.base + d)
            for d in range(net.C - 1, 0, -1)
        ]
        for copy in self.copies:
            copy.start()
        self.dst[net.c] = self.parts[net.c]

    def wait(self):
        for copy in self.copies:
            copy.wait()


class Spread:
    def __init__(self, net, dst, plane):
        self.net, self.dst, self.plane = net, dst, plane
        self.base = net.take(net.C if plane else net.Z)

    def start(self):
        net = self.net
        part = self.dst.at[net.c if self.plane else net.z]
        send = net.to_ctx if self.plane else net.to_z
        count = net.C if self.plane else net.Z
        self.copies = [send(d, part, part, self.base + d) for d in range(count - 1, 0, -1)]
        for copy in self.copies:
            copy.start()

    def wait(self):
        for copy in self.copies:
            copy.wait()


class Vectors:
    names = ("gain1", "shift1", "qv", "out", "gain2", "shift2", "up", "down")

    def __init__(self, ref, Z, sizes):
        self.ref, self.Z, self.at = ref, Z, {}
        start = 0
        for name, size in zip(self.names, sizes):
            self.at[name] = (start, size)
            start += size

    def get(self, name):
        start, size = self.at[name]
        return jnp.concatenate(
            [self.ref[z, :, start : start + size] for z in range(self.Z)], axis=1
        )


def chosen(pieces, index):
    out = jnp.zeros_like(pieces[0])
    for i, piece in enumerate(pieces):
        out = jnp.where(index == i, piece, out)
    return out


def layer_kernel(names, chips, Z, sizes, aligned, *refs):
    ref = SimpleNamespace(**dict(zip(names, refs)))
    net = Net(chips, Z, ref.sems)
    local = ref.local
    c, z, C = net.c, net.z, net.C
    x_in, cot_in = ref.x_in, ref.cot_in
    R, D = x_in.shape
    S = R * C
    hw = ref.mix.shape[2]
    heads = hw // HEAD_DIM
    fw = ref.hid.shape[1]
    fzc = fw // Z
    r = D // (C * Z)
    step = 2 * R
    xs, n1, n2, cot = (ref.xs, ref.n1, ref.n2, ref.cot)
    bg = xs
    qkv, mix, lse = ref.qkv, ref.mix, ref.lse

    started = []

    def bring(src, dst, i):
        copy = pltpu.make_async_copy(src, dst, local.at[i])
        copy.start()
        return copy

    load_x = bring(x_in, xs.at[c], 1)
    if aligned:
        load_q = [
            bring(
                ref.wqkv_in.at[:, pl.ds(pl.multiple_of(p * D + c * hw, hw), hw)],
                ref.wqkv.at[z, :, p * hw : (p + 1) * hw], 2 + p,
            )
            for p in range(3)
        ]
        FZ = fzc * C
        load_u = [
            bring(
                ref.wup_in.at[:, pl.ds(pl.multiple_of(p * FZ + net.block(p, c) * fzc, fzc), fzc)],
                ref.wup.at[z, :, p * fzc : (p + 1) * fzc], 8 + p,
            )
            for p in range(Z)
        ]
    else:
        load_q = [bring(ref.wqkv_in, ref.wqkv.at[z], 2)]
        load_u = [bring(ref.wup_in, ref.wup.at[z], 8)]
    load_o = bring(ref.wout_in.at[pl.ds(pl.multiple_of(c * r, r), r)], ref.wout_parts.at[z], 5)
    load_d = bring(ref.wdown_in.at[pl.ds(pl.multiple_of(net.block(z, c) * fzc, fzc), fzc)], ref.wdown.at[z], 6)
    load_c = bring(cot_in, cot.at[c], 7)

    zv, zq = ZGather(net, ref.vec), ZGather(net, ref.wqkv)
    zo, zu = ZGather(net, ref.wout_parts), ZGather(net, ref.wup)
    zd = ZGather(net, ref.wdown)
    at = 0
    for own, size in zip(refs[: len(sizes)], sizes):
        ref.vec[z, :, at : at + size] = own[...].astype(f32).reshape(1, size)
        at += size
    net.barrier()
    zv.begin()

    def tokens(src, dst):
        return Gather(net, lambda rows: src.at[rows], lambda i, rows: dst.at[i, rows], R)

    gx = tokens(x_in, xs)
    gx.begin()
    load_o.wait()
    zo.begin()
    for copy in load_q:
        copy.wait()
    zq.begin()

    pos = lax.broadcasted_iota(jnp.int32, (S, 1), 0)
    first = jnp.zeros((S, 1), jnp.int32)
    end = jnp.int32(0)
    for i in range(ref.docs.shape[1]):
        end = end + ref.docs[0, i]
        first = jnp.where(pos >= end, end, first)
    ref.first[...] = first

    zv.relay()
    zv.wait()
    vectors = Vectors(ref.vec, Z, sizes)
    gain1, shift1 = vectors.get("gain1"), vectors.get("shift1")
    load_x.wait()

    def norm_one(d):
        block = c ^ d
        xhat, _ = row_stats(xs[block].astype(f32))
        n1[block] = (xhat * gain1 + shift1).astype(bf16)

    norm_one(0)
    gx.middle()
    zo.relay()
    zq.relay()
    gx.finish(norm_one)
    parts_o, wo = ref.wout_parts, ref.wo
    wg = Gather(net, lambda rows: parts_o.at[:, rows], lambda i, rows: wo.at[:, i, rows], r)
    zo.wait()
    wg.begin()
    wo[:, c] = parts_o[...]
    for copy in load_u:
        copy.wait()

    qv = vectors.get("qv")
    bias = jnp.concatenate(
        [
            chosen([qv[:, i * hw : (i + 1) * hw] for i in range(C)], c),
            jnp.zeros((1, hw), f32),
            chosen([qv[:, D + i * hw : D + (i + 1) * hw] for i in range(C)], c),
        ],
        axis=1,
    )
    zq.wait()
    zu.begin()
    wg.middle()
    w_qkv = ref.wqkv[...].reshape(D, 3 * hw)

    def blocks(array, i):
        return array[pl.ds(2 * i, 2)].reshape(step, D)

    def tile(i):
        return pl.ds(pl.multiple_of(i * step, step), step)

    def project(i, carry):
        qkv[tile(i), :] = (mm(blocks(n1, i), w_qkv, NN) + bias).astype(bf16)
        return carry

    lax.fori_loop(0, S // step, project, 0)
    load_c.wait()
    gc = tokens(cot_in, cot)
    gc.begin()
    tiles = S // step

    def masked(i):
        n = (i + 1) * step
        row = lax.broadcasted_iota(jnp.int32, (step, n), 0) + i * step
        col = lax.broadcasted_iota(jnp.int32, (step, n), 1)
        return (col <= row) & (col >= ref.first[i * step : n, :])

    def head(part, h, rows):
        at = part * hw + h * HEAD_DIM
        return qkv[rows, at : at + HEAD_DIM]

    def beside(parts):
        return jnp.concatenate(parts, axis=1) if len(parts) > 1 else parts[0]

    def put(array, i, value):
        array[2 * i], array[2 * i + 1] = value[:R], value[R:]

    for i in range(tiles):
        if i == tiles - 1:
            wg.finish()
            load_d.wait()
            zd.begin()
        n = (i + 1) * step
        rows, keys = slice(i * step, n), slice(0, n)
        allowed = masked(i)
        parts = []
        for h in range(heads):
            s = mm(head(0, h, rows), head(1, h, keys), NT) * score_scale
            s = jnp.where(allowed, s, masked_score)
            top = jnp.max(s, axis=1, keepdims=True)
            e = jnp.exp(s - top)
            total = jnp.sum(e, axis=1, keepdims=True)
            parts.append((mm(e.astype(bf16), head(2, h, keys), NN) / total).astype(bf16))
            lse[h, rows, :] = top + jnp.log(total)
        put(mix, i, beside(parts))
    swap_mix = Swap(net, mix, ref.mixf)
    swap_mix.start()
    gc.middle()
    zu.relay()
    swap_mix.wait()
    w_out = wo[...].reshape(D, D)
    mixed = jnp.concatenate([ref.mixf[i] for i in range(C)], axis=1)
    x_own = xs[c]
    ref.x_own[...] = x_own
    resid = x_own.astype(f32) + mm(mixed, w_out, NN) + vectors.get("out")
    xhat2, scale2 = row_stats(resid)
    gain2 = vectors.get("gain2")
    n2[c] = (xhat2 * gain2 + vectors.get("shift2")).astype(bf16)
    ref.resid[...] = resid
    gc.finish()
    gn = tokens(n2.at[c], n2)
    gn.begin()
    gn.middle()
    zd.relay()
    zu.wait()
    w_up = ref.wup[...].reshape(D, fw)
    up = vectors.get("up")
    b_up = jnp.concatenate(
        [
            chosen(
                [up[:, (q * C + i) * fzc : (q * C + i + 1) * fzc] for i in range(C)],
                net.block(q, c),
            )
            for q in range(Z)
        ],
        axis=1,
    )
    gn.finish()
    hid, pg, slopes = ref.hid, ref.pg, ref.slopes

    def feed(i, carry):
        rows = tile(i)
        value, slope = gelu_both(mm(blocks(n2, i), w_up, NN) + b_up)
        hid[rows, :] = value.astype(bf16)
        slopes[rows, :] = slope
        return carry

    lax.fori_loop(0, tiles, feed, 0)

    lanes = 128

    def whole(array):
        return array[...].reshape(S, D)

    def chunk(i):
        return pl.ds(pl.multiple_of(i * lanes, lanes), lanes)

    dbuf, ubuf, obuf, qbuf = (ref.dbuf, ref.ubuf, ref.obuf, ref.qbuf)

    def down_part(i, carry):
        dbuf[chunk(i), :] = mm(hid[:, chunk(i)], whole(cot), TN).astype(bf16)
        return carry

    lax.fori_loop(0, fw // lanes, down_part, 0)
    zd.wait()
    rd = ZReduce(
        net,
        lambda zs: dbuf.at[pl.ds(pl.multiple_of((zs ^ (c % Z)) * fzc, fzc), fzc)],
        ref.drecv,
        ref.dsum,
    )
    rd.begin()
    w_down = ref.wdown[...].reshape(fw, D)

    up_sums = []

    def feed_back(chip):
        rows = tile(chip)
        grad = (mm(blocks(cot, chip), w_down, NT) * slopes[rows, :]).astype(bf16)
        pg[rows, :] = grad
        up_sums.append(column_sum(grad.astype(f32)))
        return mm(grad, w_up, NT)

    sib_recv, far_recv = ref.sib_recv, ref.far_recv
    red = Reduce(net, ref.sib_send, sib_recv.at[0], ref.far_send, far_recv.at[0], ref.keep)
    red.begin(feed_back)
    up_sums = sum(up_sums)
    per = lanes // (Z * r)

    def up_part(i, carry):
        grad = mm(n2[:, :, chunk(i)].reshape(S, lanes), pg[...], TN).astype(bf16)
        ubuf[pl.ds(i * per, per)] = grad.reshape(per, Z, r, fw)
        return carry

    lax.fori_loop(0, D // lanes, up_part, 0)
    ru = ZReduce(net, lambda zs: ubuf.at[:, zs], ref.urecv, ref.usum)
    ru.begin()

    n2_grad = red.finish()
    cot_own = cot[c].astype(f32)
    xhat2, scale2 = row_stats(ref.resid[...])
    resid_grad = cot_own + norm_back(n2_grad, xhat2, scale2, gain2)
    branch = resid_grad.astype(bf16)
    bg[c] = branch
    ref.rgrad[...] = resid_grad
    back = mm(branch, w_out, NT).astype(bf16)
    mg = ref.mg
    for i in range(C):
        ref.mixf[i] = back[:, i * hw : (i + 1) * hw]
    swap_mg = Swap(net, ref.mixf, mg)
    swap_mg.start()
    gb = tokens(bg.at[c], bg)
    gb.begin()
    sums = {
        "out": column_sum(branch.astype(f32)),
        "gain2": column_sum(n2_grad * xhat2),
        "shift2": column_sum(n2_grad),
        "down": column_sum(cot_own),
    }
    swap_mg.wait()
    rd.relay()
    qg, dkv = ref.qg, ref.dkv
    dkv[...] = jnp.zeros((S, 2 * hw), f32)
    swap_up = Swap(net, ref.uparts, ref.ufrom)
    for i in range(tiles):
        n = (i + 1) * step
        rows, keys = slice(i * step, n), slice(0, n)
        if i == 1:
            gb.middle()
        if i == tiles - 1:
            ru.relay()
        allowed = masked(i)
        g_rows = mg[2 * i : 2 * i + 2].reshape(step, hw)
        m_rows = mix[2 * i : 2 * i + 2].reshape(step, hw)
        dqs, dks, dvs = [], [], []
        for h in range(heads):
            at = h * HEAD_DIM
            q, k, v = head(0, h, rows), head(1, h, keys), head(2, h, keys)
            g, m = g_rows[:, at : at + HEAD_DIM], m_rows[:, at : at + HEAD_DIM]
            s = mm(q, k, NT) * score_scale - lse[h, rows, :]
            p = jnp.where(allowed, jnp.exp(s), 0.0)
            delta = jnp.sum(g.astype(f32) * m.astype(f32), axis=1, keepdims=True)
            ds = (p * (mm(g, v, NT) - delta)).astype(bf16)
            dqs.append(score_scale * mm(ds, k, NN))
            dks.append(score_scale * mm(ds, q, TN))
            dvs.append(mm(p.astype(bf16), g, TN))
        qg[rows, 0:hw] = beside(dqs).astype(bf16)
        dkv[keys, :] += beside(dks + dvs)
    qg[:, hw : 3 * hw] = dkv[...].astype(bf16)

    def qkv_part(i, carry):
        grad = mm(n1[:, :, chunk(i)].reshape(S, lanes), qg[...], TN).astype(bf16)
        qbuf[pl.ds(i * per, per)] = grad.reshape(per, Z, r, 3 * hw)
        return carry

    red = Reduce(net, ref.sib_send, sib_recv.at[1], ref.far_send, far_recv.at[1], ref.keep)
    red.begin(lambda chip: mm(qg[tile(chip), :], w_qkv, NT))
    lax.fori_loop(0, D // lanes, qkv_part, 0)
    rq = ZReduce(net, lambda zs: qbuf.at[:, zs], ref.qrecv, ref.qsum)
    rq.begin()
    gb.finish()
    obuf[...] = mm(mix[...].reshape(S, hw), whole(bg), TN).astype(bf16)
    ro = ZReduce(
        net, lambda zs: obuf.at[pl.ds(pl.multiple_of(zs * r, r), r)], ref.orecv, ref.osum
    )
    ro.begin()
    ref.dparts[...] = rd.total().astype(bf16)
    home = net.take(1)
    there = net.to((net.home, z), ref.dparts, ref.dfrom, home, home)
    here = pltpu.make_async_copy(ref.dparts, ref.dfrom, local.at[0])

    @pl.when(net.at_home)
    def _():
        here.start()

    @pl.when(jnp.logical_not(net.at_home))
    def _():
        there.start()

    qkv_sums = column_sum(qg[...].astype(f32))
    colz, colp = ref.colz, ref.colp
    colz[z] = jnp.concatenate([qkv_sums[:, 0:hw], qkv_sums[:, 2 * hw : 3 * hw], up_sums], axis=1)
    line = Spread(net, colz, False)
    line.start()

    ref.uparts[...] = ru.total().astype(bf16)
    swap_up.start()
    n1_grad = red.finish()
    red_out = Reduce(net, ref.sib_send, sib_recv.at[0], ref.far_send, far_recv.at[0], ref.keep)
    red_out.begin(lambda chip: mm(hid[tile(chip), :], w_down, NN))
    xhat1, scale1 = row_stats(ref.x_own[...].astype(f32))
    ref.input_grad[...] = (ref.rgrad[...] + norm_back(n1_grad, xhat1, scale1, gain1)).astype(bf16)
    stack = jnp.concatenate(
        [
            column_sum(n1_grad * xhat1), column_sum(n1_grad), sums["out"], sums["gain2"],
            sums["shift2"], sums["down"], jnp.zeros((2, D), f32),
        ],
        axis=0,
    )
    w = D // C
    for i in range(C):
        ref.tok_to[i] = stack[:, i * w : (i + 1) * w]
    swap_tok = Swap(net, ref.tok_to, ref.tok_from)
    swap_tok.start()
    rq.relay()
    ro.relay()

    line.wait()
    total = colz[0]
    for i in range(1, Z):
        total = total + colz[i]
    colp[c] = total
    plane = Spread(net, colp, True)
    plane.start()
    swap_tok.wait()
    tokz = ref.tokz
    total = ref.tok_from[0]
    for i in range(1, C):
        total = total + ref.tok_from[i]
    tokz[z] = total
    tok_line = Spread(net, tokz, False)
    tok_line.start()

    @pl.when(net.at_home)
    def _():
        here.wait()

    @pl.when(jnp.logical_not(net.at_home))
    def _():
        there.wait()

    ref.d_down[...] = ref.dfrom[...].astype(f32)
    swap_up.wait()
    for i in range(C):
        for q in range(Z):
            at = (q * C + net.block(q, i)) * fzc
            ref.d_up[:, at : at + fzc] = ref.ufrom[i, :, q * fzc : (q + 1) * fzc].astype(f32)
    ref.qparts[...] = rq.total().astype(bf16)
    swap_q = Swap(net, ref.qparts, ref.qfrom)
    swap_q.start()
    ref.d_out[...] = ro.total()
    tok_line.wait()
    total = tokz[0]
    for i in range(1, Z):
        total = total + tokz[i]
    ref.tok[...] = chosen([total[:, i * r : (i + 1) * r] for i in range(Z)], z)
    total = red_out.finish()
    ref.layer_out[...] = (ref.resid[...] + total + vectors.get("down")).astype(bf16)
    plane.wait()
    mine = c * Z + z
    part = D * 2 // (C * Z)

    def piece(at, size):
        rest, row = at % hw, (at % D) // hw
        start = hw * (at // D) + rest
        return colp[row, :, start : start + size]

    ref.qv[...] = chosen([piece(i * part, part) for i in range(C * Z)], mine)
    ref.up[...] = chosen(
        [
            colp[net.block(q, i), :, 2 * hw + q * fzc : 2 * hw + (q + 1) * fzc]
            for q in range(Z)
            for i in range(C)
        ],
        mine,
    )
    swap_q.wait()
    for i in range(C):
        for p in range(3):
            ref.d_qkv[:, p * D + i * hw : p * D + (i + 1) * hw] = ref.qfrom[
                i, :, p * hw : (p + 1) * hw
            ].astype(f32)
    assert net.used <= ref.sems.shape[1]
    for part in (zv, zq, zo, zu, zd, rd, ru, ro, rq):
        part.finish()


def hand_over(count, *refs):
    big, (tok, qv, up) = refs[:count], refs[count : count + 3]
    rest, sems = refs[count + 3 :], refs[-1]
    outs, held = rest[: count + 8], rest[count + 8 : -1]
    into = [pltpu.make_async_copy(big[i], held[i], sems.at[0, i]) for i in range(count)]
    out = [pltpu.make_async_copy(held[i], outs[i], sems.at[1, i]) for i in range(count)]
    for copy in into:
        copy.start()
    for i in range(6):
        outs[count + i][...] = tok[i : i + 1, :]
    outs[count + 6][...] = qv[...]
    outs[count + 7][...] = up[...]
    for i in range(count):
        into[i].wait()
        out[i].start()
    for copy in out:
        copy.wait()


def shards(
    tokens_in,
    doc_lengths,
    norm1_gain,
    norm1_bias,
    qkv_weight,
    qv_bias,
    out_weight,
    out_bias,
    norm2_gain,
    norm2_bias,
    up_weight,
    up_bias,
    down_weight,
    down_bias,
    out_cotangent,
):
    C, Z = lax.axis_size("ctx"), lax.axis_size("fsdp")
    c, z = lax.axis_index("ctx"), lax.axis_index("fsdp")
    R, D = tokens_in.shape[1:]
    chips, S, hw = C // 2, R * C, D // C
    ff = up_weight.shape[1]
    fw, fzc, r = ff // C, ff // (C * Z), D // (C * Z)
    heads = hw // HEAD_DIM
    all_vectors = (
        norm1_gain, norm1_bias, qv_bias, out_bias, norm2_gain, norm2_bias, up_bias, down_bias
    )
    sizes = tuple(v.shape[0] for v in all_vectors)
    V, W = sum(sizes), 2 * hw + fw
    aligned = hw % 128 == 0 and fzc % 128 == 0
    wqkv_in, wup_in = qkv_weight, up_weight
    if not aligned:
        wqkv_in = lax.dynamic_index_in_dim(
            qkv_weight.reshape(D // Z, 3, C, hw), c, axis=2, keepdims=False
        ).reshape(D // Z, 3 * hw)
        split = up_weight.reshape(D // Z, Z, C, fzc)
        wup_in = jnp.concatenate(
            [
                lax.dynamic_index_in_dim(
                    split[:, q], Z * (c // Z) + (q ^ (c % Z)), axis=1, keepdims=False
                )
                for q in range(Z)
            ],
            axis=1,
        )

    vmem, hbm = pltpu.VMEM, pl.BlockSpec(memory_space=pl.ANY)
    on_chip = pl.BlockSpec(memory_space=vmem)
    ins = {str(i): (v, on_chip) for i, v in enumerate(all_vectors)}
    ins.update(
        x_in=(tokens_in[0], hbm),
        cot_in=(out_cotangent[0], hbm),
        docs=(doc_lengths, pl.BlockSpec(memory_space=pltpu.SMEM)),
        wqkv_in=(wqkv_in, hbm),
        wout_in=(out_weight, hbm),
        wup_in=(wup_in, hbm),
        wdown_in=(down_weight, hbm),
    )
    outs = dict(
        layer_out=((R, D), bf16),
        input_grad=((R, D), bf16),
        d_qkv=((r, 3 * D), f32),
        d_out=((r, D), f32),
        d_up=((r, ff), f32),
        d_down=((fzc, D), f32),
        tok=((8, r), f32),
        qv=((1, 2 * r), f32),
        up=((1, fzc), f32),
    )
    token, own = (C, R, D), (R, D)
    scratch = dict(
        xs=(token, bf16),
        n1=(token, bf16),
        n2=(token, bf16),
        cot=(token, bf16),
        qkv=((S, 3 * hw), bf16),
        qg=((S, 3 * hw), bf16),
        mix=((C, R, hw), bf16),
        mixf=((C, R, hw), bf16),
        mg=((C, R, hw), bf16),
        slopes=((S, fw), f32),
        wo=((Z, C, r, D), bf16),
        lse=((heads, S, 1), f32),
        dkv=((S, 2 * hw), f32),
        hid=((S, fw), bf16),
        pg=((S, fw), bf16),
        x_own=(own, bf16),
        resid=(own, f32),
        rgrad=(own, f32),
        vec=((Z, 1, V), f32),
        wqkv=((Z, D // Z, 3 * hw), bf16),
        wout_parts=((Z, r, D), bf16),
        wup=((Z, D // Z, fw), bf16),
        wdown=((Z, fzc, D), bf16),
        first=((S, 1), jnp.int32),
        sib_send=((chips, R, D), bf16),
        far_send=((chips, R, D), bf16),
        keep=((chips, R, D), f32),
        sib_recv=((2, chips, R, D), bf16),
        far_recv=((2, chips, R, D), bf16),
        dbuf=((fw, D), bf16),
        ubuf=((C, Z, r, fw), bf16),
        obuf=((hw, D), bf16),
        qbuf=((C, Z, r, 3 * hw), bf16),
        colz=((Z, 1, W), f32),
        tok_to=((C, 8, D // C), f32),
        tok_from=((C, 8, D // C), f32),
        colp=((C, 1, W), f32),
        tokz=((Z, 8, D // C), f32),
    )
    shard = dict(d=(fzc, D), u=(C, r, fw), o=(r, D), q=(C, r, 3 * hw))
    for k, shape in shard.items():
        scratch[k + "recv"] = ((Z - 1, *shape), bf16)
        scratch[k + "sum"] = ((Z // 2, *shape), bf16)
        if k != "o":
            scratch[k + "parts"] = (shape, bf16)
            scratch[k + "from"] = (shape, bf16)
    gathers = 5 * max(13, C)
    count = gathers + 12 * Z + 6 * chips + 6 * C + 2
    names = (*ins, *outs, *scratch, "sems", "local")
    got = pl.pallas_call(
        functools.partial(layer_kernel, names, chips, Z, sizes, aligned),
        out_shape=[jax.ShapeDtypeStruct(*v) for v in outs.values()],
        in_specs=[v[1] for v in ins.values()],
        out_specs=[pl.BlockSpec(memory_space=vmem)] * len(outs),
        scratch_shapes=[vmem(*v) for v in scratch.values()]
        + [pltpu.SemaphoreType.DMA((2, count)), pltpu.SemaphoreType.DMA((8 + Z,))],
        compiler_params=pltpu.CompilerParams(
            collective_id=1, has_side_effects=True, vmem_limit_bytes=63 << 20
        ),
        name="layer",
    )(*[v[0] for v in ins.values()])
    big = 6
    results = list(outs.values())[:big] + [((1, r), f32)] * 6 + [outs[k] for k in list(outs)[-2:]]
    done = pl.pallas_call(
        functools.partial(hand_over, big),
        out_shape=[jax.ShapeDtypeStruct(*v) for v in results],
        in_specs=[hbm] * big + [pl.BlockSpec(memory_space=vmem)] * 3,
        out_specs=[hbm] * big + [pl.BlockSpec(memory_space=vmem)] * 8,
        scratch_shapes=[vmem(*v) for v in results[:big]] + [pltpu.SemaphoreType.DMA((2, big))],
        name="hand_over",
    )(*got)
    layer_out, input_grad, d_qkv, d_out, d_up, d_down = done[:big]
    gain1, shift1, out, gain2, shift2, down, qv, up = (v.reshape(-1) for v in done[big:])
    return (
        layer_out[None], input_grad[None], gain1, shift1, d_qkv, qv, d_out, out,
        gain2, shift2, d_up, up, d_down, down,
    )


def solution(mesh):
    token = P("fsdp", "ctx", None)
    flat, table = P("fsdp"), P("fsdp", None)
    home, home2 = P(("ctx", "fsdp")), P(("ctx", "fsdp"), None)
    return jax.shard_map(
        shards,
        mesh=mesh,
        in_specs=(
            token, table, flat, flat, table, flat, table, flat,
            flat, flat, table, flat, table, flat, token,
        ),
        out_specs=(
            token, token, home, home, home2, home, home2, home,
            home, home, home2, home, home2, home,
        ),
        check_vma=False,
    )
```
